128 devices in a mesh: seq: 16 (over z, y), tensor: 8 (over x, core).
Axes of the slice: x: 4, y: 4, z: 4, core: 2. Of those that a mesh axis runs over, the one named last changes fastest.
Arguments:
- tokens: bfloat16 [256, 4, 3072], P('seq'), may hold values from -6 to 6
- lengths: int32 [256], replicated, may hold values from 1 to 16384, as said below
- page_request: int32 [2048], P('seq'), may hold values from 0 to 255, as said below
- page_block: int32 [2048], P('seq'), may hold values from 0 to 128, as said below
- k_cache: bfloat16 [2048, 8, 128, 128], P('seq', 'tensor'), may hold values from -330 to 330
- v_cache: bfloat16 [2048, 8, 128, 128], P('seq', 'tensor'), may hold values from -6 to 6
- attn_gain: bfloat16 [3072], replicated, may hold values from 0.099609375 to 1.8984375
- w_query: bfloat16 [3072, 3072], P(None, 'tensor'), may hold values from -0.109375 to 0.109375
- w_key: bfloat16 [3072, 1024], P(None, 'tensor'), may hold values from -0.109375 to 0.109375
- w_value: bfloat16 [3072, 1024], P(None, 'tensor'), may hold values from -0.109375 to 0.109375
- w_out: bfloat16 [3072, 3072], P('tensor'), may hold values from -0.109375 to 0.109375
- mlp_gain: bfloat16 [3072], replicated, may hold values from 0.099609375 to 1.8984375
- w_gate: bfloat16 [3072, 4096], P(None, 'tensor'), may hold values from -0.109375 to 0.109375
- w_up: bfloat16 [3072, 4096], P(None, 'tensor'), may hold values from -0.109375 to 0.109375
- w_down: bfloat16 [4096, 3072], P('tensor'), may hold values from -0.09375 to 0.09375
Outputs:
- layer_out: bfloat16 [256, 4, 3072], P('seq', None, 'tensor')
The draws below stay inside these ranges and needn't reach their ends.
Inputs may be any that keep to these rules, and one draw needn't show every extreme that they name: `lengths`: A request r whose index is a multiple of 32 has a long cache, within 128 tokens of 16384; the others have at most 511. Request 0 has exactly 16384. `page_request`: each pair of a long request and a page number below 128, or of a short request and a page number below 4, appears in exactly one slot; slots of pages at or beyond a request's length hold no used position. A short request's pages lie in the slots of the seq index that holds its tokens. `page_block`: slots of page number 128 hold no used position.
All inputs are finite; a program needn't handle non-finite values.
Results may differ from the reference program's by a relative error of at most 0.012.
Values may be sent and summed in bfloat16 or wider, within the bound.
No kernel may reach another device: no remote copies, remote signals or barrier semaphores. Data moves between devices by JAX's collectives and lax.ppermute only.
A program may use at most 128 MiB of HBM per device.

```python
import math
import jax
import jax.numpy as jnp
from jax import lax

D = 3072
HQ = 24
KVH = 8
HD = 128
FF = 4096
NEW = 4
PAGE = 128
LONG_MAX = 16384
SHORT_MAX = 511
REQ_DEV = 16
G = 3
REQS = 256
LONGS = 8
LONG_BLK = 128
SHORT_BLK = 4
PAGES_DEV = 128
POOL = 2048


def shuffle_row(row_key):
    return jax.random.permutation(row_key, PAGES_DEV)


def page_layout(key):
    base_key = jax.random.fold_in(key, 11)
    key_long, key_short, key_rotation, key_shuffle = jax.random.split(base_key, 4)
    seq_count = REQS // REQ_DEV
    requests = jnp.arange(REQS, dtype=jnp.int32)
    is_long = requests % (2 * REQ_DEV) == 0
    long_length = LONG_MAX - jax.random.randint(key_long, (REQS,), 0, PAGE, dtype=jnp.int32)
    short_length = jax.random.randint(key_short, (REQS,), 1, SHORT_MAX + 1, dtype=jnp.int32)
    lengths = jnp.where(is_long, long_length, short_length)
    lengths = jnp.where(requests == 0, LONG_MAX, lengths)
    lengths = jnp.where(requests == 1, SHORT_MAX, lengths)
    lengths = jnp.where(requests == 2, 1, lengths).astype(jnp.int32)
    per_long = LONG_BLK // seq_count
    rotation = jax.random.randint(key_rotation, (LONGS,), 0, seq_count, dtype=jnp.int32)
    device_column = jnp.arange(seq_count, dtype=jnp.int32)[:, None]
    long_slot = jnp.arange(LONGS * per_long, dtype=jnp.int32)[None, :]
    long_index = long_slot // per_long
    long_request = jnp.broadcast_to(long_index * 2 * REQ_DEV, (seq_count, LONGS * per_long))
    long_block = long_slot % per_long * seq_count + (device_column - rotation[long_index]) % seq_count
    short_slot = jnp.arange(REQ_DEV * SHORT_BLK, dtype=jnp.int32)[None, :]
    short_request = device_column * REQ_DEV + short_slot // SHORT_BLK
    short_block = jnp.where(short_request % (2 * REQ_DEV) == 0, LONG_BLK, short_slot % SHORT_BLK)
    owners = jnp.concatenate([long_request, short_request], axis=1)
    blocks = jnp.concatenate([long_block, short_block], axis=1)
    shuffle = jax.vmap(shuffle_row)(jax.random.split(key_shuffle, seq_count))
    owners = jnp.take_along_axis(owners, shuffle, axis=1).reshape(POOL).astype(jnp.int32)
    blocks = jnp.take_along_axis(blocks, shuffle, axis=1).reshape(POOL).astype(jnp.int32)
    return (lengths, owners, blocks)


def draw_lengths(key, part):
    return page_layout(key)[0]


def draw_page_request(key, part):
    return page_layout(key)[1]


def draw_page_block(key, part):
    return page_layout(key)[2]


def draw_k_cache(key, part):
    base_key = jax.random.fold_in(key, 23)
    key_base = jax.random.fold_in(base_key, 0)
    shape = (POOL, KVH, PAGE, HD)
    return jnp.clip(2.5 * jax.random.normal(key_base, shape, jnp.float32), -16.0, 16.0).astype(jnp.bfloat16)


def level_of(rng, dims, shards, least, largest):
    gain = 1.0
    for dim, blocks in shards:
        heights = jax.random.uniform(jax.random.fold_in(jax.random.fold_in(rng, 6), dim), (blocks,), jnp.float32, least / len(shards), largest / len(shards))
        gain = gain * jnp.repeat(jnp.exp(heights), dims[dim] // blocks).reshape((-1,) + (1,) * (len(dims) - 1 - dim))
    return gain


def normal_values(own_key, dims, deviation, limit, shards=(), kind=jnp.bfloat16):
    gain = level_of(own_key, dims, shards, -0.22, 0.18) if shards else 1.0
    array = jax.random.normal(own_key, dims, jnp.float32) * deviation * gain
    return jnp.minimum(jnp.maximum(array, -limit), limit).astype(kind)


def setup_inputs(seed: int = 0) -> dict:
    streams_of = jax.random.split(jax.random.key(seed), 16)
    return {
        "tokens": normal_values(streams_of[0], (REQS, NEW, D), 1.0, 6.0, ((0, 16),)),
        "lengths": draw_lengths(jax.random.fold_in(streams_of[15], 71), 0),
        "page_request": draw_page_request(jax.random.fold_in(streams_of[15], 71), 0),
        "page_block": draw_page_block(jax.random.fold_in(streams_of[15], 71), 0),
        "k_cache": draw_k_cache(jax.random.fold_in(streams_of[15], 71), 0),
        "v_cache": normal_values(streams_of[5], (POOL, KVH, PAGE, HD), 1.0, 6.0, ((0, 16), (1, 8))),
        "attn_gain": jnp.clip(1.0 + 0.18 * jax.random.normal(streams_of[6], (D,), jnp.float32), 0.099609375, 1.8984375).astype(jnp.bfloat16),
        "w_query": normal_values(streams_of[7], (D, HQ * HD), D ** -0.5, 0.109375, ((1, 8),)),
        "w_key": normal_values(streams_of[8], (D, KVH * HD), D ** -0.5, 0.109375, ((1, 8),)),
        "w_value": normal_values(streams_of[9], (D, KVH * HD), D ** -0.5, 0.109375, ((1, 8),)),
        "w_out": normal_values(streams_of[10], (HQ * HD, D), (HQ * HD) ** -0.5, 0.109375, ((0, 8),)),
        "mlp_gain": jnp.clip(1.0 + 0.18 * jax.random.normal(streams_of[11], (D,), jnp.float32), 0.099609375, 1.8984375).astype(jnp.bfloat16),
        "w_gate": normal_values(streams_of[12], (D, FF), D ** -0.5, 0.109375, ((1, 8),)),
        "w_up": normal_values(streams_of[13], (D, FF), D ** -0.5, 0.109375, ((1, 8),)),
        "w_down": normal_values(streams_of[14], (FF, D), FF ** -0.5, 0.09375, ((0, 8),)),
    }


EPSILON = 1e-05
NEGATIVE = -1e+30
ROPE_BASE = 500000.0

def rms_norm(values, gains):
    mean_square = lax.optimization_barrier(jnp.mean(values * values, axis=-1, keepdims=True))
    return values * lax.rsqrt(mean_square + EPSILON) * gains.astype(jnp.float32)

def rotary(values, position):
    head_width = values.shape[-1]
    half_width = head_width // 2
    inverse = 1.0 / ROPE_BASE ** (jnp.arange(half_width, dtype=jnp.float32) * 2.0 / head_width)
    angle = position.astype(jnp.float32)[..., None, None] * inverse
    cosine = jnp.cos(angle)
    sine_table = jnp.sin(angle)
    front_half = values[..., :half_width]
    back_half = values[..., half_width:]
    return jnp.concatenate([front_half * cosine - back_half * sine_table, back_half * cosine + front_half * sine_table], axis=-1)

def reference(tokens, lengths, page_request, page_block, k_cache, v_cache, attn_gain, w_query, w_key, w_value, w_out, mlp_gain, w_gate, w_up, w_down):
    row_count = REQS * NEW
    lanes = NEW * G
    score_scale = 1.0 / math.sqrt(HD)
    values_in = tokens.astype(jnp.float32)
    normed_in = rms_norm(values_in, attn_gain).astype(jnp.bfloat16).reshape(row_count, D)
    position = lengths[:, None] + jnp.arange(NEW, dtype=jnp.int32)[None, :]
    queries = jnp.dot(normed_in, w_query, preferred_element_type=jnp.float32).reshape(REQS, NEW, HQ, HD)
    queries = rotary(queries, position).astype(jnp.bfloat16)
    key_new = jnp.dot(normed_in, w_key, preferred_element_type=jnp.float32).reshape(REQS, NEW, KVH, HD)
    key_new = rotary(key_new, position).astype(jnp.bfloat16)
    value_new = jnp.dot(normed_in, w_value, preferred_element_type=jnp.float32).astype(jnp.bfloat16).reshape(REQS, NEW, KVH, HD)
    offsets = jnp.arange(PAGE, dtype=jnp.int32)
    owner_length = lengths[page_request]
    is_valid = page_block[:, None] * PAGE + offsets[None, :] < owner_length[:, None]
    causal = (jnp.arange(lanes, dtype=jnp.int32) // G)[:, None] >= jnp.arange(NEW, dtype=jnp.int32)[None, :]

    def one_head(operands):
        head_query, head_keys, head_values, fresh_key, fresh_value = operands
        flat_query = head_query.reshape(REQS, lanes, HD)
        chosen = flat_query[page_request].astype(jnp.float32)
        scores = jnp.einsum('pqd,pkd->pqk', chosen, head_keys.astype(jnp.float32)) * score_scale
        scores = jnp.where(is_valid[:, None, :], scores, NEGATIVE)
        page_max = lax.optimization_barrier(jnp.max(scores, axis=-1))
        cache_max = jnp.full((REQS, lanes), NEGATIVE, jnp.float32).at[page_request].max(page_max)
        fresh_scores = jnp.einsum('rqd,rsd->rqs', flat_query.astype(jnp.float32), fresh_key.astype(jnp.float32)) * score_scale
        fresh_scores = jnp.where(causal[None], fresh_scores, NEGATIVE)
        row_max = jnp.maximum(cache_max, lax.optimization_barrier(jnp.max(fresh_scores, axis=-1)))
        weights = jnp.where(is_valid[:, None, :], jnp.exp(scores - row_max[page_request][:, :, None]), 0.0).astype(jnp.bfloat16)
        fresh_weights = jnp.where(causal[None], jnp.exp(fresh_scores - row_max[:, :, None]), 0.0).astype(jnp.bfloat16)
        weight_total = jnp.zeros((REQS, lanes), jnp.float32).at[page_request].add(lax.optimization_barrier(jnp.sum(weights.astype(jnp.float32), axis=-1)))
        weight_total = weight_total + lax.optimization_barrier(jnp.sum(fresh_weights.astype(jnp.float32), axis=-1))
        page_sum = jnp.einsum('pqk,pkd->pqd', weights.astype(jnp.float32), head_values.astype(jnp.float32))
        summed = jnp.zeros((REQS, lanes, HD), jnp.float32).at[page_request].add(page_sum)
        summed = summed + jnp.einsum('rqs,rsd->rqd', fresh_weights.astype(jnp.float32), fresh_value.astype(jnp.float32))
        return (summed / weight_total[:, :, None]).astype(jnp.bfloat16)
    head_queries = jnp.moveaxis(queries.reshape(REQS, NEW, KVH, G, HD), 2, 0)
    head_keys = jnp.moveaxis(k_cache, 1, 0)
    head_values = jnp.moveaxis(v_cache, 1, 0)
    fresh_keys = jnp.moveaxis(key_new, 2, 0)
    fresh_values = jnp.moveaxis(value_new, 2, 0)
    attended = lax.map(one_head, (head_queries, head_keys, head_values, fresh_keys, fresh_values))
    attended = attended.reshape(KVH, REQS, NEW, G, HD).transpose(1, 2, 0, 3, 4).reshape(row_count, HQ * HD)
    residual = (values_in.reshape(row_count, D) + jnp.dot(attended, w_out, preferred_element_type=jnp.float32)).astype(jnp.bfloat16)
    normed = rms_norm(residual.astype(jnp.float32), mlp_gain).astype(jnp.bfloat16)
    gate_out = jnp.dot(normed, w_gate, preferred_element_type=jnp.float32)
    up_out = jnp.dot(normed, w_up, preferred_element_type=jnp.float32)
    activated = (jax.nn.silu(gate_out) * up_out).astype(jnp.bfloat16)
    down_out = jnp.dot(activated, w_down, preferred_element_type=jnp.float32)
    layer_out = (residual.astype(jnp.float32) + down_out).astype(jnp.bfloat16)
    return layer_out.reshape(REQS, NEW, D)
```

```python
import math

import jax
import jax.numpy as jnp
import numpy as np
from jax import lax
from jax.experimental import pallas as pl
from jax.experimental.pallas import tpu as pltpu
from jax.sharding import PartitionSpec as P

EPSILON = 1e-05
NEGATIVE = -1e30
ROPE_BASE = 500000.0
F32 = jnp.float32
BF16 = jnp.bfloat16

SEQ = 16
TEN = 8
D = 3072
HD = 128
PAGE = 128
REQ_DEV = 16
NEW = 4
G = 3
ROWS = REQ_DEV * NEW
QCOLS = G * HD
COLS = D // TEN
FF_DEV = 512
SLOTS = 128
LONG_STEP = 32
LONGS = 8
SHORT_BLK = 4
SCALE = 1.0 / math.sqrt(HD)
UNROLL = 8


VMEM = pl.BlockSpec(memory_space=pltpu.VMEM)
SMEM = pl.BlockSpec(memory_space=pltpu.SMEM)
MIB = 1 << 20


def call(kernel, out_shape, in_specs, scratch, limit, name):
    return pl.pallas_call(
        kernel,
        out_shape=out_shape,
        in_specs=in_specs,
        out_specs=jax.tree.map(lambda _: VMEM, out_shape),
        scratch_shapes=scratch,
        compiler_params=pltpu.CompilerParams(vmem_limit_bytes=limit * MIB),
        name=name,
    )


def sds(shape, dtype):
    return jax.ShapeDtypeStruct(shape, dtype)


def nt_dot(a, b):
    return lax.dot_general(a, b, (((1,), (1,)), ((), ())), preferred_element_type=F32)


def nn_dot(a, b):
    return jnp.dot(a, b, preferred_element_type=F32)


def iota(shape, dim):
    return lax.broadcasted_iota(jnp.int32, shape, dim)


def qkv_kernel(ids, lengths, tok, gain, inv, wq, wk, wv, q_pack, k_new, v_new, q_long, x_s, pos_s, t_s):
    home = ids[0] * REQ_DEV
    for r in range(REQ_DEV):
        x_s[r * NEW : (r + 1) * NEW, :] = tok[r].astype(F32)
        pos_s[r * NEW : (r + 1) * NEW, :] = lengths[home + r] + iota((NEW, HD), 0)
    x = x_s[...]
    mean_square = jnp.mean(x * x, axis=-1, keepdims=True)
    normed = (x * lax.rsqrt(mean_square + EPSILON) * gain[...].astype(F32)).astype(BF16)
    angle = pos_s[...].astype(F32) * inv[...]
    cosine = jnp.cos(angle)
    sine = jnp.sin(angle)
    sine = jnp.where(iota((ROWS, HD), 1) < HD // 2, -sine, sine)

    def rope(v):
        return v * cosine + pltpu.roll(v, HD // 2, 1) * sine

    q = nn_dot(normed, wq[...])
    for g in range(G):
        roped = rope(q[:, g * HD : (g + 1) * HD])
        for pair in range(REQ_DEV // 2):
            q_pack[pair * 32 + g * 8 : pair * 32 + g * 8 + 8, :] = roped[pair * 8 : pair * 8 + 8, :]
        t_s[g * NEW : (g + 1) * NEW, :] = roped[0:NEW, :]
    t_s[G * NEW : 16, :] = jnp.zeros((16 - G * NEW, HD), F32)
    for pair in range(REQ_DEV // 2):
        q_pack[pair * 32 + 24 : pair * 32 + 32, :] = jnp.zeros((8, HD), F32)
    packed = t_s[...].astype(BF16)
    for i in range(SEQ):
        q_long[i] = packed
    k_new[...] = rope(nn_dot(normed, wk[...])).astype(BF16)
    v_new[...] = nn_dot(normed, wv[...]).astype(BF16)


def to_row(column, eye):
    return jnp.sum(jnp.where(eye, column, 0.0), axis=0, keepdims=True)


def short_kernel(
    ids, lengths, page_request, page_block, q_pack, k_new, v_new, k_c, v_c, att, part0, table, s_s, att_s, o_s, m_s, l_s
):
    home = ids[0] * REQ_DEV
    for i in range(REQ_DEV * SHORT_BLK):
        table[i] = 0

    def enter(p, carry):
        r = page_request[p] - home
        b = page_block[p]
        mine = (r >= 0) & (r < REQ_DEV) & (b < SHORT_BLK)
        table[jnp.where(mine, r * SHORT_BLK + b, REQ_DEV * SHORT_BLK)] = p
        return carry

    lax.fori_loop(0, SLOTS, enter, 0, unroll=8)

    row = iota((32, ROWS), 0)
    col = iota((32, ROWS), 1)
    lane = iota((32, PAGE), 1)
    half = iota((32, PAGE), 0) % 8 // NEW

    def pair_step(pair, carry):
        base = pl.multiple_of(pair * 32, 32)
        q = q_pack[pl.ds(base, 32), :].astype(BF16)
        fresh = nt_dot(q, k_new[...]) * SCALE
        row_req = pair * 2 + row % 8 // NEW
        fresh_ok = (row_req == col // NEW) & (col % NEW <= row % NEW)
        fresh = jnp.where(fresh_ok, fresh, NEGATIVE)
        top = jnp.full((32, PAGE), NEGATIVE, F32)
        oks = []
        slots = []
        for a in range(2):
            r = pair * 2 + a
            length = lengths[home + r]
            used = jnp.where((home + r) % LONG_STEP == 0, 0, length)
            for b in range(SHORT_BLK):
                slot = table[r * SHORT_BLK + b]
                slots.append(slot)
                s = nt_dot(q, k_c[slot]) * SCALE
                ok = (half == a) & (lane < used - b * PAGE)
                oks.append(ok)
                s = jnp.where(ok, s, NEGATIVE)
                s_s[a * SHORT_BLK + b] = s
                top = jnp.maximum(top, s)
        m = jnp.maximum(jnp.max(top, axis=1, keepdims=True), jnp.max(fresh, axis=1, keepdims=True))
        w = jnp.where(fresh_ok, jnp.exp(fresh - m), 0.0).astype(BF16)
        total = jnp.sum(w.astype(F32), axis=1, keepdims=True)
        acc = nn_dot(w, v_new[...])
        wsum = jnp.zeros((32, PAGE), F32)
        for i in range(2 * SHORT_BLK):
            w = jnp.where(oks[i], jnp.exp(s_s[i] - m), 0.0).astype(BF16)
            wsum = wsum + w.astype(F32)
            acc = acc + nn_dot(w, v_c[slots[i]])
        total = total + jnp.sum(wsum, axis=1, keepdims=True)
        total = jnp.where(iota((32, 1), 0) < 24, total, 1.0)
        out = acc / total
        at = pl.multiple_of(pair * 8, 8)
        for g in range(G):
            att_s[pl.ds(at, 8), g * HD : (g + 1) * HD] = out[g * 8 : (g + 1) * 8, :]

        @pl.when(pair == 0)
        def _():
            for g in range(G):
                o_s[g * NEW : (g + 1) * NEW, :] = acc[g * 8 : g * 8 + NEW, :]
                m_s[g * NEW : (g + 1) * NEW, :] = jnp.broadcast_to(m[g * 8 : g * 8 + NEW, :], (NEW, HD))
                l_s[g * NEW : (g + 1) * NEW, :] = jnp.broadcast_to(total[g * 8 : g * 8 + NEW, :], (NEW, HD))

        return carry

    lax.fori_loop(0, REQ_DEV // 2, pair_step, 0)
    att[...] = att_s[...]
    eye = (iota((16, HD), 0) == iota((16, HD), 1)) & (iota((16, HD), 0) < G * NEW)
    part0[...] = o_s[...]
    part0[12:13, :] = to_row(m_s[...], eye)
    part0[13:14, :] = to_row(l_s[...], eye)
    part0[14:16, :] = jnp.zeros((2, HD), F32)


def long_kernel(lengths, page_request, page_block, q_all, k_c, v_c, part, slot_t, key_t, lim_t, s_s, m_s, l_s, o_s):
    def enter(p, n):
        r = page_request[p]
        b = page_block[p]
        limit = lengths[r] - b * PAGE
        slot_t[n] = p
        key_t[n] = r // LONG_STEP
        lim_t[n] = limit
        return n + jnp.where((r % LONG_STEP == 0) & (limit > 0), 1, 0)

    n = lax.fori_loop(0, SLOTS, enter, 0, unroll=8)
    for i in range(UNROLL):
        slot_t[n + i] = 0
        key_t[n + i] = 0
        lim_t[n + i] = 0
    trips = (n + UNROLL - 1) // UNROLL
    m_s[...] = jnp.full((LONGS, 16, HD), NEGATIVE, F32)
    l_s[...] = jnp.zeros((LONGS, 16, HD), F32)
    o_s[...] = jnp.zeros((LONGS, 16, HD), F32)
    lane = iota((16, PAGE), 1)

    def score(j, carry):
        got = []
        for i in range(UNROLL):
            e = j * UNROLL + i
            s = nt_dot(q_all[2 * key_t[e]], k_c[slot_t[e]]) * SCALE
            s = jnp.where(lane < lim_t[e], s, NEGATIVE)
            s_s[e] = s
            got.append((key_t[e], s))
        for key, s in got:
            m_s[key] = jnp.maximum(m_s[key], s)
        return carry

    lax.fori_loop(0, trips, score, 0)
    for k in range(LONGS):
        m_s[k] = jnp.broadcast_to(jnp.max(m_s[k], axis=1, keepdims=True), (16, HD))

    def weigh(j, carry):
        got = []
        for i in range(UNROLL):
            e = j * UNROLL + i
            key = key_t[e]
            w = jnp.where(lane < lim_t[e], jnp.exp(s_s[e] - m_s[key]), 0.0).astype(BF16)
            got.append((key, w.astype(F32), nn_dot(w, v_c[slot_t[e]])))
        for key, w, o in got:
            l_s[key] = l_s[key] + w
            o_s[key] = o_s[key] + o
        return carry

    lax.fori_loop(0, trips, weigh, 0)
    eye = (iota((16, HD), 0) == iota((16, HD), 1)) & (iota((16, HD), 0) < G * NEW)
    for k in range(LONGS):
        part[2 * k] = o_s[k]
        part[2 * k, 12:13, :] = to_row(m_s[k], eye)
        total = jnp.broadcast_to(jnp.sum(l_s[k], axis=1, keepdims=True), (16, HD))
        part[2 * k, 13:14, :] = to_row(total, eye)
        part[2 * k, 14:16, :] = jnp.zeros((2, HD), F32)
        part[2 * k + 1] = jnp.zeros((16, HD), F32)


def split_product(ids, a, w, keep, send):
    core = ids[2]
    for x in range(TEN // 2):
        at = pl.multiple_of((2 * x + 1 - core) * COLS, COLS)
        send[x] = nn_dot(a, w[:, pl.ds(at, COLS)]).astype(BF16)
    for x in range(TEN // 2):
        at = pl.multiple_of((2 * x + core) * COLS, COLS)
        keep[x] = nn_dot(a, w[:, pl.ds(at, COLS)]).astype(keep.dtype)


def out_kernel(ids, att, part0, parts, w_out, keep, send, att_s, m_s, l_s):
    att_s[...] = att[...]

    @pl.when(ids[0] % 2 == 0)
    def _():
        m_s[0:SEQ, :] = parts[:, 12, :]
        l_s[0:SEQ, :] = parts[:, 13, :]
        m0 = part0[12:13, :]
        m = m_s[...]
        top = jnp.maximum(jnp.max(m, axis=0, keepdims=True), m0)
        grow = jnp.exp(m - top)
        grow0 = jnp.exp(m0 - top)
        total = jnp.sum(grow * l_s[...], axis=0, keepdims=True) + grow0 * part0[13:14, :]
        live = iota((1, HD), 1) < G * NEW
        inverse = jnp.where(live, 1.0 / jnp.where(live, total, 1.0), 0.0)
        eye = iota((16, HD), 0) == iota((16, HD), 1)

        def scaled(o, coef):
            column = jnp.sum(jnp.where(eye, coef, 0.0), axis=1, keepdims=True)
            return o * column

        out = scaled(part0[...], grow0 * inverse)
        coefs = grow * inverse
        for s in range(SEQ):
            out = out + scaled(parts[s], coefs[s : s + 1, :])
        for g in range(G):
            att_s[0:NEW, g * HD : (g + 1) * HD] = out[g * NEW : (g + 1) * NEW, :]

    split_product(ids, att_s[...].astype(BF16), w_out, keep, send)


def pair_kernel(ids, keep, got, own, s1, s2, s3):
    x = ids[1]
    own[...] = keep[x].astype(F32) + got[x].astype(F32)
    for d, out in ((1, s1), (2, s2), (3, s3)):
        to = (x + d) % 4
        out[...] = (keep[to].astype(F32) + got[to].astype(F32)).astype(BF16)


def residual_kernel(ids, tok, own, r1, r2, r3, res, x_s):
    at = pl.multiple_of((2 * ids[1] + ids[2]) * COLS, COLS)
    for r in range(REQ_DEV):
        x_s[r * NEW : (r + 1) * NEW, :] = tok[r, :, pl.ds(at, COLS)].astype(F32)
    total = own[...] + r1[...].astype(F32) + r2[...].astype(F32) + r3[...].astype(F32)
    res[...] = (x_s[...] + total).astype(BF16)


def mlp_kernel(ids, mine, other, gain, w_gate, w_up, w_down, keep, send):
    x = ids[1]
    core = ids[2]
    square = jnp.zeros((ROWS, 1), F32)
    for d in range(4):
        for blocks in (mine, other):
            v = blocks[d].astype(F32)
            square = square + jnp.sum(v * v, axis=1, keepdims=True)
    inverse = lax.rsqrt(square * (1.0 / D) + EPSILON)
    gate = jnp.zeros((ROWS, FF_DEV), F32)
    up = jnp.zeros((ROWS, FF_DEV), F32)
    for d in range(4):
        for c, blocks in ((core, mine), (1 - core, other)):
            b = (x + 4 - d) % 4 * 2 + c
            normed = (blocks[d].astype(F32) * inverse * gain[b].astype(F32)).astype(BF16)
            at = pl.multiple_of(b * COLS, COLS)
            gate = gate + nn_dot(normed, w_gate[pl.ds(at, COLS), :])
            up = up + nn_dot(normed, w_up[pl.ds(at, COLS), :])
    activated = (gate / (1.0 + jnp.exp(-gate)) * up).astype(BF16)
    split_product(ids, activated, w_down, keep, send)


def final_kernel(res, own, r1, r2, r3, out):
    total = own[...] + r1[...].astype(F32) + r2[...].astype(F32) + r3[...].astype(F32)
    total = (res[...].astype(F32) + total).astype(BF16)
    for r in range(REQ_DEV):
        out[r] = total[r * NEW : (r + 1) * NEW, :]


def swap_core(v):
    return lax.ppermute(v, "tensor", [(i, i ^ 1) for i in range(TEN)])


def along_x(v, d):
    return lax.ppermute(v, "tensor", [(i, (i + 2 * d) % TEN) for i in range(TEN)])


def scatter_sum(ids, keep, send):
    got = swap_core(send)
    block = sds((ROWS, COLS), BF16)
    own, s1, s2, s3 = call(
        pair_kernel,
        (sds((ROWS, COLS), F32), block, block, block),
        [SMEM, VMEM, VMEM],
        [],
        8,
        "pair_add",
    )(ids, keep, got)
    return own, along_x(s1, 1), along_x(s2, 2), along_x(s3, 3)


def per_device(
    tokens,
    lengths,
    page_request,
    page_block,
    k_cache,
    v_cache,
    attn_gain,
    w_query,
    w_key,
    w_value,
    w_out,
    mlp_gain,
    w_gate,
    w_up,
    w_down,
):
    tensor = lax.axis_index("tensor")
    ids = jnp.stack([lax.axis_index("seq"), tensor // 2, tensor % 2]).astype(jnp.int32)
    half = np.arange(HD) % (HD // 2)
    inv = jnp.asarray((1.0 / ROPE_BASE ** (half * 2.0 / HD)).astype(np.float32).reshape(1, HD))
    k_c = k_cache.reshape(SLOTS, PAGE, HD)
    v_c = v_cache.reshape(SLOTS, PAGE, HD)

    q_pack, k_new, v_new, q_long = call(
        qkv_kernel,
        (
            sds((REQ_DEV // 2 * 32, HD), F32),
            sds((ROWS, HD), BF16),
            sds((ROWS, HD), BF16),
            sds((SEQ, 16, HD), BF16),
        ),
        [SMEM, SMEM] + [VMEM] * 6,
        [pltpu.VMEM((ROWS, D), F32), pltpu.VMEM((ROWS, HD), jnp.int32), pltpu.VMEM((16, HD), F32)],
        24,
        "qkv",
    )(ids, lengths, tokens, attn_gain.reshape(1, D), inv, w_query, w_key, w_value)

    q_all = lax.all_to_all(q_long, "seq", 0, 0, tiled=True)

    att, part0 = call(
        short_kernel,
        (sds((ROWS, QCOLS), F32), sds((16, HD), F32)),
        [SMEM] * 4 + [VMEM] * 5,
        [
            pltpu.SMEM((REQ_DEV * SHORT_BLK + 1,), jnp.int32),
            pltpu.VMEM((2 * SHORT_BLK, 32, PAGE), F32),
            pltpu.VMEM((ROWS, QCOLS), F32),
            pltpu.VMEM((16, HD), F32),
            pltpu.VMEM((16, HD), F32),
            pltpu.VMEM((16, HD), F32),
        ],
        24,
        "short",
    )(ids, lengths, page_request, page_block, q_pack, k_new, v_new, k_c, v_c)

    part = call(
        long_kernel,
        sds((SEQ, 16, HD), F32),
        [SMEM] * 3 + [VMEM] * 3,
        [pltpu.SMEM((SLOTS + UNROLL,), jnp.int32)] * 3
        + [pltpu.VMEM((SLOTS + UNROLL, 16, PAGE), F32)]
        + [pltpu.VMEM((LONGS, 16, HD), F32)] * 3,
        24,
        "long",
    )(lengths, page_request, page_block, q_all, k_c, v_c)

    parts = lax.all_to_all(part, "seq", 0, 0, tiled=True)

    halves = (sds((TEN // 2, ROWS, COLS), BF16), sds((TEN // 2, ROWS, COLS), BF16))
    keep, send = call(
        out_kernel,
        halves,
        [SMEM] + [VMEM] * 4,
        [pltpu.VMEM((ROWS, QCOLS), F32), pltpu.VMEM((SEQ, HD), F32), pltpu.VMEM((SEQ, HD), F32)],
        16,
        "out_proj",
    )(ids, att, part0, parts, w_out)
    own, r1, r2, r3 = scatter_sum(ids, keep, send)

    res = call(
        residual_kernel,
        sds((ROWS, COLS), BF16),
        [SMEM] + [VMEM] * 5,
        [pltpu.VMEM((ROWS, COLS), F32)],
        8,
        "residual",
    )(ids, tokens, own, r1, r2, r3)

    mine = jnp.stack([res] + [along_x(res, d) for d in (1, 2, 3)])
    other = swap_core(mine)

    keep, send = call(
        mlp_kernel,
        halves,
        [SMEM] + [VMEM] * 6,
        [],
        32,
        "mlp",
    )(ids, mine, other, mlp_gain.reshape(TEN, 1, COLS), w_gate, w_up, w_down)
    own, r1, r2, r3 = scatter_sum(ids, keep, send)

    return call(
        final_kernel,
        sds((REQ_DEV, NEW, COLS), BF16),
        [VMEM] * 5,
        [],
        8,
        "final",
    )(res, own, r1, r2, r3)


def solution(mesh):
    placed = (
        P("seq", None, None),
        P(),
        P("seq"),
        P("seq"),
        P("seq", "tensor", None, None),
        P("seq", "tensor", None, None),
        P(),
        P(None, "tensor"),
        P(None, "tensor"),
        P(None, "tensor"),
        P("tensor", None),
        P(),
        P(None, "tensor"),
        P(None, "tensor"),
        P("tensor", None),
    )
    return jax.shard_map(
        per_device, mesh=mesh, in_specs=placed, out_specs=P("seq", None, "tensor"), check_vma=False
    )
```

```python
import math

import jax
import jax.numpy as jnp
import numpy as np
from jax import lax
from jax.experimental import pallas as pl
from jax.experimental.pallas import tpu as pltpu
from jax.sharding import PartitionSpec as P

EPSILON = 1e-05
NEGATIVE = -1e30
ROPE_BASE = 500000.0
F32 = jnp.float32
BF16 = jnp.bfloat16

SEQ = 16
TEN = 8
D = 3072
HD = 128
PAGE = 128
REQ_DEV = 16
NEW = 4
G = 3
ROWS = REQ_DEV * NEW
QCOLS = G * HD
COLS = D // TEN
FF_DEV = 512
SLOTS = 128
LONG_STEP = 32
LONGS = 8
SHORT_BLK = 4
SCALE = 1.0 / math.sqrt(HD)
UNROLL = 8


VMEM = pl.BlockSpec(memory_space=pltpu.VMEM)
SMEM = pl.BlockSpec(memory_space=pltpu.SMEM)
HBM = pl.BlockSpec(memory_space=pltpu.HBM)
MIB = 1 << 20


def call(kernel, out_shape, in_specs, scratch, limit, name):
    return pl.pallas_call(
        kernel,
        out_shape=out_shape,
        in_specs=in_specs,
        out_specs=jax.tree.map(lambda _: VMEM, out_shape),
        scratch_shapes=scratch,
        compiler_params=pltpu.CompilerParams(vmem_limit_bytes=limit * MIB),
        name=name,
    )


def sds(shape, dtype):
    return jax.ShapeDtypeStruct(shape, dtype)


def nt_dot(a, b):
    return lax.dot_general(a, b, (((1,), (1,)), ((), ())), preferred_element_type=F32)


def nn_dot(a, b):
    return jnp.dot(a, b, preferred_element_type=F32)


def iota(shape, dim):
    return lax.broadcasted_iota(jnp.int32, shape, dim)


def start_all(pairs, sems):
    copies = [pltpu.make_async_copy(src, dst, sems.at[i]) for i, (src, dst) in enumerate(pairs)]
    for copy in copies:
        copy.start()
    return copies


def qkv_kernel(
    lengths_h, tok_h, gain_h, inv_h, wq_h, wk_h, wv_h,
    q_pack, k_new, v_new, q_long,
    lengths, tok, gain, inv, wq, wk, wv, x_s, pos_s, t_s, sems,
):
    third = D // 3
    copies = start_all(
        [(tok_h, tok), (gain_h, gain), (lengths_h, lengths), (inv_h, inv)]
        + [(wq_h.at[pl.ds(i * third, third)], wq.at[pl.ds(i * third, third)]) for i in range(3)]
        + [(wk_h, wk), (wv_h, wv)],
        sems,
    )
    home = lax.axis_index("seq") * REQ_DEV
    copies[0].wait()
    for r in range(REQ_DEV):
        x_s[r * NEW : (r + 1) * NEW, :] = tok[r].astype(F32)
    x = x_s[...]
    mean_square = jnp.mean(x * x, axis=-1, keepdims=True)
    copies[1].wait()
    normed = (x * lax.rsqrt(mean_square + EPSILON) * gain[...].astype(F32)).astype(BF16)
    copies[2].wait()
    for r in range(REQ_DEV):
        pos_s[r * NEW : (r + 1) * NEW, :] = lengths[home + r] + iota((NEW, HD), 0)
    copies[3].wait()
    angle = pos_s[...].astype(F32) * inv[...]
    cosine = jnp.cos(angle)
    sine = jnp.sin(angle)
    sine = jnp.where(iota((ROWS, HD), 1) < HD // 2, -sine, sine)

    def rope(v):
        return v * cosine + pltpu.roll(v, HD // 2, 1) * sine

    q = jnp.zeros((ROWS, QCOLS), F32)
    for i in range(3):
        copies[4 + i].wait()
        q = q + nn_dot(normed[:, i * third : (i + 1) * third], wq[i * third : (i + 1) * third, :])
    for g in range(G):
        roped = rope(q[:, g * HD : (g + 1) * HD])
        for pair in range(REQ_DEV // 2):
            q_pack[pair * 32 + g * 8 : pair * 32 + g * 8 + 8, :] = roped[pair * 8 : pair * 8 + 8, :]
        t_s[g * NEW : (g + 1) * NEW, :] = roped[0:NEW, :]
    t_s[G * NEW : 16, :] = jnp.zeros((16 - G * NEW, HD), F32)
    for pair in range(REQ_DEV // 2):
        q_pack[pair * 32 + 24 : pair * 32 + 32, :] = jnp.zeros((8, HD), F32)
    packed = t_s[...].astype(BF16)
    for i in range(SEQ):
        q_long[i] = packed
    copies[7].wait()
    k_new[...] = rope(nn_dot(normed, wk[...])).astype(BF16)
    copies[8].wait()
    v_new[...] = nn_dot(normed, wv[...]).astype(BF16)


def to_row(column, eye):
    return jnp.sum(jnp.where(eye, column, 0.0), axis=0, keepdims=True)


def short_kernel(
    lengths_h, request_h, block_h, q_pack, k_new, v_new, k_h, v_h,
    att, part0,
    lengths, page_request, page_block, k_c, v_c, table, s_s, att_s, o_s, m_s, l_s, sems,
):
    copies = start_all(
        [(lengths_h, lengths), (request_h, page_request), (block_h, page_block), (k_h, k_c), (v_h, v_c)],
        sems,
    )
    home = lax.axis_index("seq") * REQ_DEV
    for copy in copies[:3]:
        copy.wait()
    for i in range(REQ_DEV * SHORT_BLK):
        table[i] = 0

    def enter(p, carry):
        r = page_request[p] - home
        b = page_block[p]
        mine = (r >= 0) & (r < REQ_DEV) & (b < SHORT_BLK)
        table[jnp.where(mine, r * SHORT_BLK + b, REQ_DEV * SHORT_BLK)] = p
        return carry

    lax.fori_loop(0, SLOTS, enter, 0, unroll=8)
    for copy in copies[3:5]:
        copy.wait()

    row = iota((32, ROWS), 0)
    col = iota((32, ROWS), 1)
    lane = iota((32, PAGE), 1)
    half = iota((32, PAGE), 0) % 8 // NEW

    def pair_step(pair, carry):
        base = pl.multiple_of(pair * 32, 32)
        q = q_pack[pl.ds(base, 32), :].astype(BF16)
        fresh = nt_dot(q, k_new[...]) * SCALE
        row_req = pair * 2 + row % 8 // NEW
        fresh_ok = (row_req == col // NEW) & (col % NEW <= row % NEW)
        fresh = jnp.where(fresh_ok, fresh, NEGATIVE)
        top = jnp.full((32, PAGE), NEGATIVE, F32)
        oks = []
        slots = []
        for a in range(2):
            r = pair * 2 + a
            length = lengths[home + r]
            used = jnp.where((home + r) % LONG_STEP == 0, 0, length)
            for b in range(SHORT_BLK):
                slot = table[r * SHORT_BLK + b]
                slots.append(slot)
                s = nt_dot(q, k_c[slot]) * SCALE
                ok = (half == a) & (lane < used - b * PAGE)
                oks.append(ok)
                s = jnp.where(ok, s, NEGATIVE)
                s_s[a * SHORT_BLK + b] = s
                top = jnp.maximum(top, s)
        m = jnp.maximum(jnp.max(top, axis=1, keepdims=True), jnp.max(fresh, axis=1, keepdims=True))
        w = jnp.where(fresh_ok, jnp.exp(fresh - m), 0.0).astype(BF16)
        total = jnp.sum(w.astype(F32), axis=1, keepdims=True)
        acc = nn_dot(w, v_new[...])
        wsum = jnp.zeros((32, PAGE), F32)
        for i in range(2 * SHORT_BLK):
            w = jnp.where(oks[i], jnp.exp(s_s[i] - m), 0.0).astype(BF16)
            wsum = wsum + w.astype(F32)
            acc = acc + nn_dot(w, v_c[slots[i]])
        total = total + jnp.sum(wsum, axis=1, keepdims=True)
        total = jnp.where(iota((32, 1), 0) < 24, total, 1.0)
        out = acc / total
        at = pl.multiple_of(pair * 8, 8)
        for g in range(G):
            att_s[pl.ds(at, 8), g * HD : (g + 1) * HD] = out[g * 8 : (g + 1) * 8, :]

        @pl.when(pair == 0)
        def _():
            for g in range(G):
                o_s[g * NEW : (g + 1) * NEW, :] = acc[g * 8 : g * 8 + NEW, :]
                m_s[g * NEW : (g + 1) * NEW, :] = jnp.broadcast_to(m[g * 8 : g * 8 + NEW, :], (NEW, HD))
                l_s[g * NEW : (g + 1) * NEW, :] = jnp.broadcast_to(total[g * 8 : g * 8 + NEW, :], (NEW, HD))

        return carry

    lax.fori_loop(0, REQ_DEV // 2, pair_step, 0)
    att[...] = att_s[...]
    eye = (iota((16, HD), 0) == iota((16, HD), 1)) & (iota((16, HD), 0) < G * NEW)
    part0[...] = o_s[...]
    part0[12:13, :] = to_row(m_s[...], eye)
    part0[13:14, :] = to_row(l_s[...], eye)
    part0[14:16, :] = jnp.zeros((2, HD), F32)


def long_kernel(
    lengths_h, request_h, block_h, q_all, k_h, v_h,
    part,
    lengths, page_request, page_block, k_c, v_c, slot_t, key_t, lim_t, s_s, m_s, l_s, o_s, sems,
):
    copies = start_all(
        [(lengths_h, lengths), (request_h, page_request), (block_h, page_block), (k_h, k_c), (v_h, v_c)],
        sems,
    )
    for copy in copies[:3]:
        copy.wait()

    def enter(p, n):
        r = page_request[p]
        b = page_block[p]
        limit = lengths[r] - b * PAGE
        slot_t[n] = p
        key_t[n] = r // LONG_STEP
        lim_t[n] = limit
        return n + jnp.where((r % LONG_STEP == 0) & (limit > 0), 1, 0)

    n = lax.fori_loop(0, SLOTS, enter, 0, unroll=8)
    for i in range(UNROLL):
        slot_t[n + i] = 0
        key_t[n + i] = 0
        lim_t[n + i] = 0
    trips = (n + UNROLL - 1) // UNROLL
    m_s[...] = jnp.full((LONGS, 16, HD), NEGATIVE, F32)
    l_s[...] = jnp.zeros((LONGS, 16, HD), F32)
    o_s[...] = jnp.zeros((LONGS, 16, HD), F32)
    lane = iota((16, PAGE), 1)
    copies[3].wait()

    def score(j, carry):
        got = []
        for i in range(UNROLL):
            e = j * UNROLL + i
            s = nt_dot(q_all[2 * key_t[e]], k_c[slot_t[e]]) * SCALE
            s = jnp.where(lane < lim_t[e], s, NEGATIVE)
            s_s[e] = s
            got.append((key_t[e], s))
        for key, s in got:
            m_s[key] = jnp.maximum(m_s[key], s)
        return carry

    lax.fori_loop(0, trips, score, 0)
    for k in range(LONGS):
        m_s[k] = jnp.broadcast_to(jnp.max(m_s[k], axis=1, keepdims=True), (16, HD))

    copies[4].wait()

    def weigh(j, carry):
        got = []
        for i in range(UNROLL):
            e = j * UNROLL + i
            key = key_t[e]
            w = jnp.where(lane < lim_t[e], jnp.exp(s_s[e] - m_s[key]), 0.0).astype(BF16)
            got.append((key, w.astype(F32), nn_dot(w, v_c[slot_t[e]])))
        for key, w, o in got:
            l_s[key] = l_s[key] + w
            o_s[key] = o_s[key] + o
        return carry

    lax.fori_loop(0, trips, weigh, 0)
    eye = (iota((16, HD), 0) == iota((16, HD), 1)) & (iota((16, HD), 0) < G * NEW)
    for k in range(LONGS):
        part[2 * k] = o_s[k]
        part[2 * k, 12:13, :] = to_row(m_s[k], eye)
        total = jnp.broadcast_to(jnp.sum(l_s[k], axis=1, keepdims=True), (16, HD))
        part[2 * k, 13:14, :] = to_row(total, eye)
        part[2 * k, 14:16, :] = jnp.zeros((2, HD), F32)
        part[2 * k + 1] = jnp.zeros((16, HD), F32)


def place():
    tensor = lax.axis_index("tensor")
    return tensor // 2, tensor % 2


def split_product(a, w, keep, send):
    core = place()[1]
    for x in range(TEN // 2):
        at = pl.multiple_of((2 * x + 1 - core) * COLS, COLS)
        send[x] = nn_dot(a, w[:, pl.ds(at, COLS)]).astype(BF16)
    for x in range(TEN // 2):
        at = pl.multiple_of((2 * x + core) * COLS, COLS)
        keep[x] = nn_dot(a, w[:, pl.ds(at, COLS)]).astype(keep.dtype)


def out_kernel(att, part0, parts, w_out, keep, send, att_s, m_s, l_s):
    att_s[...] = att[...]

    @pl.when(lax.axis_index("seq") % 2 == 0)
    def _():
        m_s[0:SEQ, :] = parts[:, 12, :]
        l_s[0:SEQ, :] = parts[:, 13, :]
        m0 = part0[12:13, :]
        m = m_s[...]
        top = jnp.maximum(jnp.max(m, axis=0, keepdims=True), m0)
        grow = jnp.exp(m - top)
        grow0 = jnp.exp(m0 - top)
        total = jnp.sum(grow * l_s[...], axis=0, keepdims=True) + grow0 * part0[13:14, :]
        live = iota((1, HD), 1) < G * NEW
        inverse = jnp.where(live, 1.0 / jnp.where(live, total, 1.0), 0.0)
        eye = iota((16, HD), 0) == iota((16, HD), 1)

        def scaled(o, coef):
            column = jnp.sum(jnp.where(eye, coef, 0.0), axis=1, keepdims=True)
            return o * column

        out = scaled(part0[...], grow0 * inverse)
        coefs = grow * inverse
        for s in range(SEQ):
            out = out + scaled(parts[s], coefs[s : s + 1, :])
        for g in range(G):
            att_s[0:NEW, g * HD : (g + 1) * HD] = out[g * NEW : (g + 1) * NEW, :]

    split_product(att_s[...].astype(BF16), w_out, keep, send)


def pair_kernel(keep, got, own, s1, s2, s3):
    x = place()[0]
    own[...] = keep[x].astype(F32) + got[x].astype(F32)
    for d, out in ((1, s1), (2, s2), (3, s3)):
        to = (x + d) % 4
        out[...] = (keep[to].astype(F32) + got[to].astype(F32)).astype(BF16)


def residual_kernel(tok, own, r1, r2, r3, res, x_s):
    at = pl.multiple_of(lax.axis_index("tensor") * COLS, COLS)
    for r in range(REQ_DEV):
        x_s[r * NEW : (r + 1) * NEW, :] = tok[r, :, pl.ds(at, COLS)].astype(F32)
    total = own[...] + r1[...].astype(F32) + r2[...].astype(F32) + r3[...].astype(F32)
    res[...] = (x_s[...] + total).astype(BF16)


def mlp_kernel(mine, other, gain, w_gate, w_up, w_down, keep, send):
    x, core = place()
    square = jnp.zeros((ROWS, 1), F32)
    for d in range(4):
        for blocks in (mine, other):
            v = blocks[d].astype(F32)
            square = square + jnp.sum(v * v, axis=1, keepdims=True)
    inverse = lax.rsqrt(square * (1.0 / D) + EPSILON)
    gate = jnp.zeros((ROWS, FF_DEV), F32)
    up = jnp.zeros((ROWS, FF_DEV), F32)
    for d in range(4):
        for c, blocks in ((core, mine), (1 - core, other)):
            b = (x + 4 - d) % 4 * 2 + c
            at = pl.multiple_of(b * COLS, COLS)
            normed = (blocks[d].astype(F32) * inverse * gain[:, pl.ds(at, COLS)].astype(F32)).astype(BF16)
            gate = gate + nn_dot(normed, w_gate[pl.ds(at, COLS), :])
            up = up + nn_dot(normed, w_up[pl.ds(at, COLS), :])
    activated = (gate / (1.0 + jnp.exp(-gate)) * up).astype(BF16)
    split_product(activated, w_down, keep, send)


def final_kernel(res, own, r1, r2, r3, out):
    total = own[...] + r1[...].astype(F32) + r2[...].astype(F32) + r3[...].astype(F32)
    total = (res[...].astype(F32) + total).astype(BF16)
    for r in range(REQ_DEV):
        out[r] = total[r * NEW : (r + 1) * NEW, :]


def swap_core(v):
    return lax.ppermute(v, "tensor", [(i, i ^ 1) for i in range(TEN)])


def along_x(v, d):
    return lax.ppermute(v, "tensor", [(i, (i + 2 * d) % TEN) for i in range(TEN)])


def scatter_sum(keep, send):
    got = swap_core(send)
    block = sds((ROWS, COLS), BF16)
    own, s1, s2, s3 = call(
        pair_kernel,
        (sds((ROWS, COLS), F32), block, block, block),
        [VMEM, VMEM],
        [],
        1,
        "pair_add",
    )(keep, got)
    return own, along_x(s1, 1), along_x(s2, 2), along_x(s3, 3)


def per_device(
    tokens,
    lengths,
    page_request,
    page_block,
    k_cache,
    v_cache,
    attn_gain,
    w_query,
    w_key,
    w_value,
    w_out,
    mlp_gain,
    w_gate,
    w_up,
    w_down,
):
    half = np.arange(HD) % (HD // 2)
    inv = jnp.asarray((1.0 / ROPE_BASE ** (half * 2.0 / HD)).astype(np.float32).reshape(1, HD))
    k_cache = k_cache.reshape(SLOTS, PAGE, HD)
    v_cache = v_cache.reshape(SLOTS, PAGE, HD)
    dma = pltpu.SemaphoreType.DMA

    def in_hbm(*arrays):
        return tuple(pltpu.with_memory_space_constraint(a, pltpu.HBM) for a in arrays)

    q_pack, k_new, v_new, q_long = call(
        qkv_kernel,
        (
            sds((REQ_DEV // 2 * 32, HD), F32),
            sds((ROWS, HD), BF16),
            sds((ROWS, HD), BF16),
            sds((SEQ, 16, HD), BF16),
        ),
        [HBM] * 7,
        [
            pltpu.SMEM(lengths.shape, jnp.int32),
            pltpu.VMEM(tokens.shape, BF16),
            pltpu.VMEM((1, D), BF16),
            pltpu.VMEM((1, HD), F32),
            pltpu.VMEM(w_query.shape, BF16),
            pltpu.VMEM(w_key.shape, BF16),
            pltpu.VMEM(w_value.shape, BF16),
            pltpu.VMEM((ROWS, D), F32),
            pltpu.VMEM((ROWS, HD), jnp.int32),
            pltpu.VMEM((16, HD), F32),
            dma((9,)),
        ],
        12,
        "qkv",
    )(*in_hbm(lengths, tokens, attn_gain.reshape(1, D), inv, w_query, w_key, w_value))

    q_all = lax.all_to_all(q_long, "seq", 0, 0, tiled=True)

    pages = in_hbm(lengths, page_request, page_block)
    caches = in_hbm(k_cache, v_cache)
    held = [
        pltpu.SMEM(lengths.shape, jnp.int32),
        pltpu.SMEM(page_request.shape, jnp.int32),
        pltpu.SMEM(page_block.shape, jnp.int32),
        pltpu.VMEM(k_cache.shape, BF16),
        pltpu.VMEM(v_cache.shape, BF16),
    ]

    att, part0 = call(
        short_kernel,
        (sds((ROWS, QCOLS), F32), sds((16, HD), F32)),
        [HBM] * 3 + [VMEM] * 3 + [HBM] * 2,
        held
        + [
            pltpu.SMEM((REQ_DEV * SHORT_BLK + 1,), jnp.int32),
            pltpu.VMEM((2 * SHORT_BLK, 32, PAGE), F32),
            pltpu.VMEM((ROWS, QCOLS), F32),
            pltpu.VMEM((16, HD), F32),
            pltpu.VMEM((16, HD), F32),
            pltpu.VMEM((16, HD), F32),
            dma((5,)),
        ],
        12,
        "short",
    )(*pages, q_pack, k_new, v_new, *caches)

    q_all, att = lax.optimization_barrier((q_all, att))

    part = call(
        long_kernel,
        sds((SEQ, 16, HD), F32),
        [HBM] * 3 + [VMEM] + [HBM] * 2,
        held
        + [pltpu.SMEM((SLOTS + UNROLL,), jnp.int32)] * 3
        + [pltpu.VMEM((SLOTS + UNROLL, 16, PAGE), F32)]
        + [pltpu.VMEM((LONGS, 16, HD), F32)] * 3
        + [dma((5,))],
        14,
        "long",
    )(*pages, q_all, *caches)

    parts = lax.all_to_all(part, "seq", 0, 0, tiled=True)

    halves = (sds((TEN // 2, ROWS, COLS), BF16), sds((TEN // 2, ROWS, COLS), BF16))
    keep, send = call(
        out_kernel,
        halves,
        [VMEM] * 4,
        [pltpu.VMEM((ROWS, QCOLS), F32), pltpu.VMEM((SEQ, HD), F32), pltpu.VMEM((SEQ, HD), F32)],
        2,
        "out_proj",
    )(att, part0, parts, w_out)
    own, r1, r2, r3 = scatter_sum(keep, send)

    res = call(
        residual_kernel,
        sds((ROWS, COLS), BF16),
        [VMEM] * 5,
        [pltpu.VMEM((ROWS, COLS), F32)],
        1,
        "residual",
    )(tokens, own, r1, r2, r3)

    mine = jnp.stack([res] + [along_x(res, d) for d in (1, 2, 3)])
    other = swap_core(mine)

    keep, send = call(
        mlp_kernel,
        halves,
        [VMEM] * 6,
        [],
        4,
        "mlp",
    )(mine, other, mlp_gain.reshape(1, D), w_gate, w_up, w_down)
    own, r1, r2, r3 = scatter_sum(keep, send)

    return call(
        final_kernel,
        sds((REQ_DEV, NEW, COLS), BF16),
        [VMEM] * 5,
        [],
        1,
        "final",
    )(res, own, r1, r2, r3)


def solution(mesh):
    placed = (
        P("seq", None, None),
        P(),
        P("seq"),
        P("seq"),
        P("seq", "tensor", None, None),
        P("seq", "tensor", None, None),
        P(),
        P(None, "tensor"),
        P(None, "tensor"),
        P(None, "tensor"),
        P("tensor", None),
        P(),
        P(None, "tensor"),
        P(None, "tensor"),
        P("tensor", None),
    )
    return jax.shard_map(
        per_device, mesh=mesh, in_specs=placed, out_specs=P("seq", None, "tensor"), check_vma=False
    )
```

```python
import math

import jax
import jax.numpy as jnp
import numpy as np
from jax import lax
from jax.experimental import pallas as pl
from jax.experimental.pallas import tpu as pltpu
from jax.sharding import PartitionSpec as P

EPSILON = 1e-05
NEGATIVE = -1e30
ROPE_BASE = 500000.0
F32 = jnp.float32
BF16 = jnp.bfloat16

SEQ = 16
TEN = 8
D = 3072
HD = 128
PAGE = 128
REQ_DEV = 16
NEW = 4
G = 3
ROWS = REQ_DEV * NEW
QCOLS = G * HD
COLS = D // TEN
FF_DEV = 512
SLOTS = 128
LONG_STEP = 32
LONGS = 8
SHORT_BLK = 4
SCALE = 1.0 / math.sqrt(HD)
UNROLL = 16
COST_QKV = 48


VMEM = pl.BlockSpec(memory_space=pltpu.VMEM)
SMEM = pl.BlockSpec(memory_space=pltpu.SMEM)
HBM = pl.BlockSpec(memory_space=pltpu.HBM)
MIB = 1 << 20


def call(kernel, out_shape, in_specs, scratch, limit, name, out_specs=None, cost=4):
    return pl.pallas_call(
        cost_estimate=pl.CostEstimate(flops=0, transcendentals=0, bytes_accessed=cost * MIB),
        kernel=kernel,
        out_shape=out_shape,
        in_specs=in_specs,
        out_specs=out_specs or jax.tree.map(lambda _: VMEM, out_shape),
        scratch_shapes=scratch,
        compiler_params=pltpu.CompilerParams(vmem_limit_bytes=limit * MIB),
        name=name,
    )


def sds(shape, dtype):
    return jax.ShapeDtypeStruct(shape, dtype)


def nt_dot(a, b):
    return lax.dot_general(a, b, (((1,), (1,)), ((), ())), preferred_element_type=F32)


def nn_dot(a, b):
    return jnp.dot(a, b, preferred_element_type=F32)


def iota(shape, dim):
    return lax.broadcasted_iota(jnp.int32, shape, dim)


def start_all(pairs, sems):
    copies = [pltpu.make_async_copy(src, dst, sems.at[i]) for i, (src, dst) in enumerate(pairs)]
    for copy in copies:
        copy.start()
    return copies


def qkv_kernel(
    lengths_h, request_h, block_h, tok_h, gain_h, inv_h, wq_h, wk_h, wv_h,
    q_pack, k_new, v_new, q_long, table,
    lengths, request, block, tok, gain, inv, wq, wk, wv, x_s, pos_s, t_s, table_s, sems, table_sem,
):
    third = D // 3
    copies = start_all(
        [(tok_h, tok), (gain_h, gain), (lengths_h, lengths), (inv_h, inv)]
        + [(wq_h.at[pl.ds(i * third, third)], wq.at[pl.ds(i * third, third)]) for i in range(3)]
        + [(wk_h, wk), (wv_h, wv), (request_h, request.at[0]), (block_h, block.at[0])],
        sems,
    )
    home = lax.axis_index("seq") * REQ_DEV
    copies[9].wait()
    copies[10].wait()
    copies[2].wait()
    req = jnp.broadcast_to(request[...], (8, SLOTS))
    blk = jnp.broadcast_to(block[...], (8, SLOTS))
    lane = iota((8, SLOTS), 1)
    long_len = jnp.zeros((8, SLOTS), jnp.int32)
    for k in range(LONGS):
        long_len = jnp.where(req == k * LONG_STEP, lengths[k * LONG_STEP], long_len)
    limit = long_len - blk * PAGE
    used = jnp.where(limit > 0, 1, 0)
    count = used
    for step in (1, 2, 4, 8, 16, 32, 64):
        count = count + jnp.where(lane >= step, pltpu.roll(count, step, 1), 0)
    packed = lane + req // LONG_STEP * 128 + jnp.minimum(limit, PAGE) * 1024
    mine = (req >= home) & (req < home + REQ_DEV) & (blk < SHORT_BLK)
    index = jnp.where(mine, (req - home) * SHORT_BLK + blk, -1)
    slot = iota((SLOTS, SLOTS), 0)
    spot = iota((SLOTS, SLOTS), 1)

    def column(row):
        wide = jnp.broadcast_to(row[0:1, :].astype(F32), (SLOTS, SLOTS))
        return jnp.sum(jnp.where(slot == spot, wide, 0.0), axis=1, keepdims=True)

    def scatter(at, value):
        return jnp.sum(jnp.where(at == spot.astype(F32), value, 0.0), axis=0, keepdims=True).astype(jnp.int32)

    table_s[0:1, :] = scatter(column(index), slot.astype(F32))
    table_s[1:2, :] = scatter(column(jnp.where(used > 0, count - 1, -1)), column(packed))
    facts = jnp.where(lane == 0, jnp.sum(used[0:1, :].astype(F32), axis=1, keepdims=True).astype(jnp.int32), 0)
    for r in range(REQ_DEV):
        known = jnp.where((home + r) % LONG_STEP == 0, 0, lengths[home + r])
        facts = jnp.where(lane == 16 + r, known, facts)
    table_s[2:3, :] = facts[0:1, :]
    table_s[3:8, :] = jnp.zeros((5, SLOTS), jnp.int32)
    give = pltpu.make_async_copy(table_s, table, table_sem)
    give.start()
    copies[0].wait()
    for r in range(REQ_DEV):
        x_s[r * NEW : (r + 1) * NEW, :] = tok[r].astype(F32)
    x = x_s[...]
    mean_square = jnp.mean(x * x, axis=-1, keepdims=True)
    copies[1].wait()
    normed = (x * lax.rsqrt(mean_square + EPSILON) * gain[...].astype(F32).reshape(1, D)).astype(BF16)
    for r in range(REQ_DEV):
        pos_s[r * NEW : (r + 1) * NEW, :] = lengths[home + r] + iota((NEW, HD), 0)
    copies[3].wait()
    angle = pos_s[...].astype(F32) * inv[...]
    cosine = jnp.cos(angle)
    sine = jnp.sin(angle)
    sine = jnp.where(iota((ROWS, HD), 1) < HD // 2, -sine, sine)

    def rope(v):
        return v * cosine + pltpu.roll(v, HD // 2, 1) * sine

    q = jnp.zeros((ROWS, QCOLS), F32)
    for i in range(3):
        copies[4 + i].wait()
        q = q + nn_dot(normed[:, i * third : (i + 1) * third], wq[i * third : (i + 1) * third, :])
    for g in range(G):
        roped = rope(q[:, g * HD : (g + 1) * HD])
        for pair in range(REQ_DEV // 2):
            q_pack[pair * 32 + g * 8 : pair * 32 + g * 8 + 8, :] = roped[pair * 8 : pair * 8 + 8, :]
        t_s[g * NEW : (g + 1) * NEW, :] = roped[0:NEW, :]
    t_s[G * NEW : 16, :] = jnp.zeros((16 - G * NEW, HD), F32)
    for pair in range(REQ_DEV // 2):
        q_pack[pair * 32 + 24 : pair * 32 + 32, :] = jnp.zeros((8, HD), F32)
    packed = t_s[...].astype(BF16)
    for i in range(SEQ):
        q_long[i] = packed
    copies[7].wait()
    k_new[...] = rope(nn_dot(normed, wk[...])).astype(BF16)
    copies[8].wait()
    v_new[...] = nn_dot(normed, wv[...]).astype(BF16)
    give.wait()


def to_row(column, eye):
    return jnp.sum(jnp.where(eye, column, 0.0), axis=0, keepdims=True)


def short_kernel(table, q_pack, k_new, v_new, k_c, v_c, att, part0, s_s, att_s, o_s, m_s, l_s):
    row = iota((32, ROWS), 0)
    col = iota((32, ROWS), 1)
    lane = iota((32, PAGE), 1)
    half = iota((32, PAGE), 0) % 8 // NEW

    def pair_step(pair, carry):
        base = pl.multiple_of(pair * 32, 32)
        q = q_pack[pl.ds(base, 32), :].astype(BF16)
        fresh = nt_dot(q, k_new[...]) * SCALE
        row_req = pair * 2 + row % 8 // NEW
        fresh_ok = (row_req == col // NEW) & (col % NEW <= row % NEW)
        fresh = jnp.where(fresh_ok, fresh, NEGATIVE)
        top = jnp.full((32, PAGE), NEGATIVE, F32)
        oks = []
        slots = []
        for a in range(2):
            r = pair * 2 + a
            used = table[2, 16 + r]
            for b in range(SHORT_BLK):
                slot = table[0, r * SHORT_BLK + b]
                slots.append(slot)
                s = nt_dot(q, k_c[slot]) * SCALE
                ok = (half == a) & (lane < used - b * PAGE)
                oks.append(ok)
                s = jnp.where(ok, s, NEGATIVE)
                s_s[a * SHORT_BLK + b] = s
                top = jnp.maximum(top, s)
        m = jnp.maximum(jnp.max(top, axis=1, keepdims=True), jnp.max(fresh, axis=1, keepdims=True))
        w = jnp.where(fresh_ok, jnp.exp(fresh - m), 0.0).astype(BF16)
        total = jnp.sum(w.astype(F32), axis=1, keepdims=True)
        acc = nn_dot(w, v_new[...])
        wsum = jnp.zeros((32, PAGE), F32)
        for i in range(2 * SHORT_BLK):
            w = jnp.where(oks[i], jnp.exp(s_s[i] - m), 0.0).astype(BF16)
            wsum = wsum + w.astype(F32)
            acc = acc + nn_dot(w, v_c[slots[i]])
        total = total + jnp.sum(wsum, axis=1, keepdims=True)
        total = jnp.where(iota((32, 1), 0) < 24, total, 1.0)
        out = acc / total
        at = pl.multiple_of(pair * 8, 8)
        for g in range(G):
            att_s[pl.ds(at, 8), g * HD : (g + 1) * HD] = out[g * 8 : (g + 1) * 8, :]

        @pl.when(pair == 0)
        def _():
            for g in range(G):
                o_s[g * NEW : (g + 1) * NEW, :] = acc[g * 8 : g * 8 + NEW, :]
                m_s[g * NEW : (g + 1) * NEW, :] = jnp.broadcast_to(m[g * 8 : g * 8 + NEW, :], (NEW, HD))
                l_s[g * NEW : (g + 1) * NEW, :] = jnp.broadcast_to(total[g * 8 : g * 8 + NEW, :], (NEW, HD))

        return carry

    lax.fori_loop(0, REQ_DEV // 2, pair_step, 0, unroll=2)
    att[...] = att_s[...]
    eye = (iota((16, HD), 0) == iota((16, HD), 1)) & (iota((16, HD), 0) < G * NEW)
    part0[...] = o_s[...]
    part0[12:13, :] = to_row(m_s[...], eye)
    part0[13:14, :] = to_row(l_s[...], eye)
    part0[14:16, :] = jnp.zeros((2, HD), F32)


def long_kernel(table, q_all, k_c, v_c, part, s_s, m_s, l_s, o_s):
    n = table[2, 0]
    trips = (n + UNROLL - 1) // UNROLL
    m_s[...] = jnp.full((LONGS, 16, HD), NEGATIVE, F32)
    l_s[...] = jnp.zeros((LONGS, 16, HD), F32)
    o_s[...] = jnp.zeros((LONGS, 16, HD), F32)
    lane = iota((16, PAGE), 1)

    def entry(e):
        word = table[1, e]
        return word % 128, word // 128 % 8, word // 1024

    def score(j, carry):
        got = []
        for i in range(UNROLL):
            e = j * UNROLL + i
            slot, key, limit = entry(e)
            s = nt_dot(q_all[2 * key], k_c[slot]) * SCALE
            s = jnp.where(lane < limit, s, NEGATIVE)
            s_s[e] = s
            got.append((key, s))
        for key, s in got:
            m_s[key] = jnp.maximum(m_s[key], s)
        return carry

    lax.fori_loop(0, trips, score, 0)
    for k in range(LONGS):
        m_s[k] = jnp.broadcast_to(jnp.max(m_s[k], axis=1, keepdims=True), (16, HD))

    def weigh(j, carry):
        got = []
        for i in range(UNROLL):
            e = j * UNROLL + i
            slot, key, limit = entry(e)
            w = jnp.where(lane < limit, jnp.exp(s_s[e] - m_s[key]), 0.0).astype(BF16)
            got.append((key, w.astype(F32), nn_dot(w, v_c[slot])))
        for key, w, o in got:
            l_s[key] = l_s[key] + w
            o_s[key] = o_s[key] + o
        return carry

    lax.fori_loop(0, trips, weigh, 0)
    for k in range(LONGS):
        total = jnp.broadcast_to(jnp.sum(l_s[k], axis=1, keepdims=True), (16, HD))
        part[2 * k, 0:12, :] = o_s[k, 0:12, :].astype(BF16)
        part[2 * k, 12:14, :] = jnp.concatenate([spread(m_s[k]), spread(total)], axis=0).astype(BF16)
        part[2 * k, 14:16, :] = jnp.zeros((2, HD), BF16)
        part[2 * k + 1] = jnp.zeros((16, HD), BF16)


def spread(column):
    row = iota((16, HD), 0)
    lane = iota((16, HD), 1)
    out = jnp.zeros((16, HD), F32)
    rest = column
    for i in range(3):
        piece = lax.reduce_precision(rest, 8, 7)
        rest = rest - piece
        out = jnp.where((lane == row + 16 * i) & (row < G * NEW), piece, out)
    return jnp.sum(out, axis=0, keepdims=True)


def gathered(row):
    return row + pltpu.roll(row, HD - 16, 1) + pltpu.roll(row, HD - 32, 1)


def place():
    tensor = lax.axis_index("tensor")
    return tensor // 2, tensor % 2


def split_product(a, w, keep, send):
    core = place()[1]
    for x in range(TEN // 2):
        at = pl.multiple_of((2 * x + 1 - core) * COLS, COLS)
        send[x] = nn_dot(a, w[:, pl.ds(at, COLS)]).astype(BF16)
    for x in range(TEN // 2):
        at = pl.multiple_of((2 * x + core) * COLS, COLS)
        keep[x] = nn_dot(a, w[:, pl.ds(at, COLS)]).astype(keep.dtype)


def out_kernel(att, part0, parts, w_out, keep, send, att_s, m_s, l_s):
    att_s[...] = att[...]

    @pl.when(lax.axis_index("seq") % 2 == 0)
    def _():
        for s in range(SEQ):
            stats = parts[s].astype(F32)
            m_s[s : s + 1, :] = stats[12:13, :]
            l_s[s : s + 1, :] = stats[13:14, :]
        m0 = part0[12:13, :]
        m = gathered(m_s[...])
        top = jnp.maximum(jnp.max(m, axis=0, keepdims=True), m0)
        grow = jnp.exp(m - top)
        grow0 = jnp.exp(m0 - top)
        total = jnp.sum(grow * gathered(l_s[...]), axis=0, keepdims=True) + grow0 * part0[13:14, :]
        live = iota((1, HD), 1) < G * NEW
        inverse = jnp.where(live, 1.0 / jnp.where(live, total, 1.0), 0.0)
        eye = iota((16, HD), 0) == iota((16, HD), 1)

        def scaled(o, coef):
            column = jnp.sum(jnp.where(eye, coef, 0.0), axis=1, keepdims=True)
            return o * column

        out = scaled(part0[...], grow0 * inverse)
        coefs = grow * inverse
        for s in range(SEQ):
            out = out + scaled(parts[s].astype(F32), coefs[s : s + 1, :])
        for g in range(G):
            att_s[0:NEW, g * HD : (g + 1) * HD] = out[g * NEW : (g + 1) * NEW, :]

    split_product(att_s[...].astype(BF16), w_out, keep, send)


def pair_kernel(keep, got, own, s1, s2, s3):
    x = place()[0]
    own[...] = keep[x].astype(F32) + got[x].astype(F32)
    for d, out in ((1, s1), (2, s2), (3, s3)):
        to = (x + d) % 4
        out[...] = (keep[to].astype(F32) + got[to].astype(F32)).astype(BF16)


def residual_kernel(tok, own, r1, r2, r3, res, x_s):
    at = pl.multiple_of(lax.axis_index("tensor") * COLS, COLS)
    for r in range(REQ_DEV):
        x_s[r * NEW : (r + 1) * NEW, :] = tok[r, :, pl.ds(at, COLS)].astype(F32)
    total = own[...] + r1[...].astype(F32) + r2[...].astype(F32) + r3[...].astype(F32)
    res[...] = (x_s[...] + total).astype(BF16)


def mlp_kernel(mine, other, gain, w_gate, w_up, w_down, keep, send):
    x, core = place()
    square = jnp.zeros((ROWS, 1), F32)
    for d in range(4):
        for blocks in (mine, other):
            v = blocks[d].astype(F32)
            square = square + jnp.sum(v * v, axis=1, keepdims=True)
    inverse = lax.rsqrt(square * (1.0 / D) + EPSILON)
    gate = jnp.zeros((ROWS, FF_DEV), F32)
    up = jnp.zeros((ROWS, FF_DEV), F32)
    for d in range(4):
        for c, blocks in ((core, mine), (1 - core, other)):
            b = (x + 4 - d) % 4 * 2 + c
            at = pl.multiple_of(b * COLS, COLS)
            normed = (blocks[d].astype(F32) * inverse * gain[:, pl.ds(at, COLS)].astype(F32)).astype(BF16)
            gate = gate + nn_dot(normed, w_gate[pl.ds(at, COLS), :])
            up = up + nn_dot(normed, w_up[pl.ds(at, COLS), :])
    activated = (gate / (1.0 + jnp.exp(-gate)) * up).astype(BF16)
    split_product(activated, w_down, keep, send)


def final_kernel(res, own, r1, r2, r3, out):
    total = own[...] + r1[...].astype(F32) + r2[...].astype(F32) + r3[...].astype(F32)
    total = (res[...].astype(F32) + total).astype(BF16)
    for r in range(REQ_DEV):
        out[r] = total[r * NEW : (r + 1) * NEW, :]


def swap_core(v):
    return lax.ppermute(v, "tensor", [(i, i ^ 1) for i in range(TEN)])


def along_x(v, d):
    return lax.ppermute(v, "tensor", [(i, (i + 2 * d) % TEN) for i in range(TEN)])


def scatter_sum(keep, send):
    got = swap_core(send)
    block = sds((ROWS, COLS), BF16)
    own, s1, s2, s3 = call(
        pair_kernel,
        (sds((ROWS, COLS), F32), block, block, block),
        [VMEM, VMEM],
        [],
        1,
        "pair_add",
    )(keep, got)
    return own, along_x(s1, 1), along_x(s2, 2), along_x(s3, 3)


def per_device(
    tokens,
    lengths,
    page_request,
    page_block,
    k_cache,
    v_cache,
    attn_gain,
    w_query,
    w_key,
    w_value,
    w_out,
    mlp_gain,
    w_gate,
    w_up,
    w_down,
):
    half = np.arange(HD) % (HD // 2)
    inv = jnp.asarray((1.0 / ROPE_BASE ** (half * 2.0 / HD)).astype(np.float32).reshape(1, HD))
    k_cache = k_cache.reshape(SLOTS, PAGE, HD)
    v_cache = v_cache.reshape(SLOTS, PAGE, HD)
    dma = pltpu.SemaphoreType.DMA

    def in_hbm(*arrays):
        return tuple(pltpu.with_memory_space_constraint(a, pltpu.HBM) for a in arrays)

    q_pack, k_new, v_new, q_long, table = call(
        qkv_kernel,
        (
            sds((REQ_DEV // 2 * 32, HD), F32),
            sds((ROWS, HD), BF16),
            sds((ROWS, HD), BF16),
            sds((SEQ, 16, HD), BF16),
            pltpu.SMEM((8, SLOTS), jnp.int32),
        ),
        [HBM] * 9,
        [
            pltpu.SMEM(lengths.shape, jnp.int32),
            pltpu.VMEM((1, SLOTS), jnp.int32),
            pltpu.VMEM((1, SLOTS), jnp.int32),
            pltpu.VMEM(tokens.shape, BF16),
            pltpu.VMEM((D,), BF16),
            pltpu.VMEM((1, HD), F32),
            pltpu.VMEM(w_query.shape, BF16),
            pltpu.VMEM(w_key.shape, BF16),
            pltpu.VMEM(w_value.shape, BF16),
            pltpu.VMEM((ROWS, D), F32),
            pltpu.VMEM((ROWS, HD), jnp.int32),
            pltpu.VMEM((16, HD), F32),
            pltpu.VMEM((8, SLOTS), jnp.int32),
            dma((11,)),
            dma(()),
        ],
        8,
        "qkv",
        [VMEM] * 4 + [SMEM],
        COST_QKV,
    )(*in_hbm(lengths, page_request, page_block, tokens, attn_gain, inv, w_query, w_key, w_value))

    q_all = lax.all_to_all(q_long, "seq", 0, 0, tiled=True)
    q_all, q_pack = lax.optimization_barrier((q_all, q_pack))

    att, part0 = call(
        short_kernel,
        (sds((ROWS, QCOLS), F32), sds((16, HD), F32)),
        [SMEM] + [VMEM] * 5,
        [
            pltpu.VMEM((2 * SHORT_BLK, 32, PAGE), F32),
            pltpu.VMEM((ROWS, QCOLS), F32),
            pltpu.VMEM((16, HD), F32),
            pltpu.VMEM((16, HD), F32),
            pltpu.VMEM((16, HD), F32),
        ],
        2,
        "short",
    )(table, q_pack, k_new, v_new, k_cache, v_cache)

    q_all, att = lax.optimization_barrier((q_all, att))

    part = call(
        long_kernel,
        sds((SEQ, 16, HD), BF16),
        [SMEM] + [VMEM] * 3,
        [pltpu.VMEM((SLOTS, 16, PAGE), F32)] + [pltpu.VMEM((LONGS, 16, HD), F32)] * 3,
        2,
        "long",
    )(table, q_all, k_cache, v_cache)

    parts = lax.all_to_all(part, "seq", 0, 0, tiled=True)

    halves = (sds((TEN // 2, ROWS, COLS), BF16), sds((TEN // 2, ROWS, COLS), BF16))
    keep, send = call(
        out_kernel,
        halves,
        [VMEM] * 4,
        [pltpu.VMEM((ROWS, QCOLS), F32), pltpu.VMEM((SEQ, HD), F32), pltpu.VMEM((SEQ, HD), F32)],
        2,
        "out_proj",
    )(att, part0, parts, w_out)
    own, r1, r2, r3 = scatter_sum(keep, send)

    res = call(
        residual_kernel,
        sds((ROWS, COLS), BF16),
        [VMEM] * 5,
        [pltpu.VMEM((ROWS, COLS), F32)],
        1,
        "residual",
    )(tokens, own, r1, r2, r3)

    mine = jnp.stack([res] + [along_x(res, d) for d in (1, 2, 3)])
    other = swap_core(mine)

    keep, send = call(
        mlp_kernel,
        halves,
        [VMEM] * 6,
        [],
        4,
        "mlp",
    )(mine, other, mlp_gain.reshape(1, D), w_gate, w_up, w_down)
    own, r1, r2, r3 = scatter_sum(keep, send)

    return call(
        final_kernel,
        sds((REQ_DEV, NEW, COLS), BF16),
        [VMEM] * 5,
        [],
        1,
        "final",
    )(res, own, r1, r2, r3)


def solution(mesh):
    placed = (
        P("seq", None, None),
        P(),
        P("seq"),
        P("seq"),
        P("seq", "tensor", None, None),
        P("seq", "tensor", None, None),
        P(),
        P(None, "tensor"),
        P(None, "tensor"),
        P(None, "tensor"),
        P("tensor", None),
        P(),
        P(None, "tensor"),
        P(None, "tensor"),
        P("tensor", None),
    )
    return jax.shard_map(
        per_device, mesh=mesh, in_specs=placed, out_specs=P("seq", None, "tensor"), check_vma=False
    )
```

```python
import math

import jax
import jax.numpy as jnp
import numpy as np
from jax import lax
from jax.experimental import pallas as pl
from jax.experimental.pallas import tpu as pltpu
from jax.sharding import PartitionSpec as P

EPSILON = 1e-05
NEGATIVE = -1e30
ROPE_BASE = 500000.0
F32 = jnp.float32
BF16 = jnp.bfloat16

SEQ = 16
TEN = 8
D = 3072
HD = 128
PAGE = 128
REQ_DEV = 16
NEW = 4
G = 3
ROWS = REQ_DEV * NEW
QCOLS = G * HD
COLS = D // TEN
FF_DEV = 512
SLOTS = 128
LONG_STEP = 32
LONGS = 8
SHORT_BLK = 4
SCALE = 1.0 / math.sqrt(HD)
UNROLL = 16


VMEM = pl.BlockSpec(memory_space=pltpu.VMEM)
SMEM = pl.BlockSpec(memory_space=pltpu.SMEM)
HBM = pl.BlockSpec(memory_space=pltpu.HBM)
MIB = 1 << 20


def call(kernel, out_shape, in_specs, scratch, limit, name, out_specs=None):
    return pl.pallas_call(
        kernel,
        out_shape=out_shape,
        in_specs=in_specs,
        out_specs=out_specs or jax.tree.map(lambda _: VMEM, out_shape),
        scratch_shapes=scratch,
        compiler_params=pltpu.CompilerParams(vmem_limit_bytes=limit * MIB),
        name=name,
    )


def sds(shape, dtype):
    return jax.ShapeDtypeStruct(shape, dtype)


def nt_dot(a, b):
    return lax.dot_general(a, b, (((1,), (1,)), ((), ())), preferred_element_type=F32)


def nn_dot(a, b):
    return jnp.dot(a, b, preferred_element_type=F32)


def iota(shape, dim):
    return lax.broadcasted_iota(jnp.int32, shape, dim)


def start_all(pairs, sems):
    copies = [pltpu.make_async_copy(src, dst, sems.at[i]) for i, (src, dst) in enumerate(pairs)]
    for copy in copies:
        copy.start()
    return copies


def qkv_kernel(
    lengths_h, request_h, block_h, tok_h, gain_h, inv_h, wq_h, wk_h, wv_h,
    q_pack, k_new, v_new, q_long, table,
    lengths, request, block, tok, gain, inv, wq, wk, wv, x_s, pos_s, t_s, table_s, sems, table_sem,
):
    third = D // 3
    copies = start_all(
        [(tok_h, tok), (gain_h, gain), (lengths_h, lengths), (inv_h, inv)]
        + [(wq_h.at[pl.ds(i * third, third)], wq.at[pl.ds(i * third, third)]) for i in range(3)]
        + [(wk_h, wk), (wv_h, wv), (request_h, request.at[0]), (block_h, block.at[0])],
        sems,
    )
    home = lax.axis_index("seq") * REQ_DEV
    copies[9].wait()
    copies[10].wait()
    copies[2].wait()
    req = jnp.broadcast_to(request[...], (8, SLOTS))
    blk = jnp.broadcast_to(block[...], (8, SLOTS))
    lane = iota((8, SLOTS), 1)
    long_len = jnp.zeros((8, SLOTS), jnp.int32)
    for k in range(LONGS):
        long_len = jnp.where(req == k * LONG_STEP, lengths[k * LONG_STEP], long_len)
    limit = long_len - blk * PAGE
    used = jnp.where(limit > 0, 1, 0)
    count = used
    for step in (1, 2, 4, 8, 16, 32, 64):
        count = count + jnp.where(lane >= step, pltpu.roll(count, step, 1), 0)
    packed = lane + req // LONG_STEP * 128 + jnp.minimum(limit, PAGE) * 1024
    mine = (req >= home) & (req < home + REQ_DEV) & (blk < SHORT_BLK)
    index = jnp.where(mine, (req - home) * SHORT_BLK + blk, -1)
    slot = iota((SLOTS, SLOTS), 0)
    spot = iota((SLOTS, SLOTS), 1)

    def column(row):
        wide = jnp.broadcast_to(row[0:1, :].astype(F32), (SLOTS, SLOTS))
        return jnp.sum(jnp.where(slot == spot, wide, 0.0), axis=1, keepdims=True)

    def scatter(at, value):
        return jnp.sum(jnp.where(at == spot.astype(F32), value, 0.0), axis=0, keepdims=True).astype(jnp.int32)

    table_s[0:1, :] = scatter(column(index), slot.astype(F32))
    table_s[1:2, :] = scatter(column(jnp.where(used > 0, count - 1, -1)), column(packed))
    facts = jnp.where(lane == 0, jnp.sum(used[0:1, :].astype(F32), axis=1, keepdims=True).astype(jnp.int32), 0)
    for r in range(REQ_DEV):
        known = jnp.where((home + r) % LONG_STEP == 0, 0, lengths[home + r])
        facts = jnp.where(lane == 16 + r, known, facts)
    table_s[2:3, :] = facts[0:1, :]
    table_s[3:8, :] = jnp.zeros((5, SLOTS), jnp.int32)
    give = pltpu.make_async_copy(table_s, table, table_sem)
    give.start()
    copies[0].wait()
    for r in range(REQ_DEV):
        x_s[r * NEW : (r + 1) * NEW, :] = tok[r].astype(F32)
    x = x_s[...]
    mean_square = jnp.mean(x * x, axis=-1, keepdims=True)
    copies[1].wait()
    normed = (x * lax.rsqrt(mean_square + EPSILON) * gain[...].astype(F32).reshape(1, D)).astype(BF16)
    for r in range(REQ_DEV):
        pos_s[r * NEW : (r + 1) * NEW, :] = lengths[home + r] + iota((NEW, HD), 0)
    copies[3].wait()
    angle = pos_s[...].astype(F32) * inv[...]
    cosine = jnp.cos(angle)
    sine = jnp.sin(angle)
    sine = jnp.where(iota((ROWS, HD), 1) < HD // 2, -sine, sine)

    def rope(v):
        return v * cosine + pltpu.roll(v, HD // 2, 1) * sine

    q = jnp.zeros((ROWS, QCOLS), F32)
    for i in range(3):
        copies[4 + i].wait()
        q = q + nn_dot(normed[:, i * third : (i + 1) * third], wq[i * third : (i + 1) * third, :])
    for g in range(G):
        roped = rope(q[:, g * HD : (g + 1) * HD])
        for pair in range(REQ_DEV // 2):
            q_pack[pair * 32 + g * 8 : pair * 32 + g * 8 + 8, :] = roped[pair * 8 : pair * 8 + 8, :]
        t_s[g * NEW : (g + 1) * NEW, :] = roped[0:NEW, :]
    t_s[G * NEW : 16, :] = jnp.zeros((16 - G * NEW, HD), F32)
    for pair in range(REQ_DEV // 2):
        q_pack[pair * 32 + 24 : pair * 32 + 32, :] = jnp.zeros((8, HD), F32)
    packed = t_s[...].astype(BF16)
    for i in range(SEQ):
        q_long[i] = packed
    copies[7].wait()
    k_new[...] = rope(nn_dot(normed, wk[...])).astype(BF16)
    copies[8].wait()
    v_new[...] = nn_dot(normed, wv[...]).astype(BF16)
    give.wait()


def to_row(column, eye):
    return jnp.sum(jnp.where(eye, column, 0.0), axis=0, keepdims=True)


def attend_kernel(
    table, q_pack, k_new, v_new, q_all, k_c, v_h,
    att, part0, part,
    v_c, fresh_s, short_s, top_s, acc_s, sum_s, att_s, o_0, m_0, l_0, long_s, m_s, l_s, o_s, sem,
):
    copy = pltpu.make_async_copy(v_h, v_c, sem)
    copy.start()
    row = iota((32, ROWS), 0)
    col = iota((32, ROWS), 1)
    lane = iota((32, PAGE), 1)
    half = iota((32, PAGE), 0) % 8 // NEW

    def pair_score(pair, carry):
        q = q_pack[pl.ds(pl.multiple_of(pair * 32, 32), 32), :].astype(BF16)
        fresh = nt_dot(q, k_new[...]) * SCALE
        fresh_ok = (pair * 2 + row % 8 // NEW == col // NEW) & (col % NEW <= row % NEW)
        fresh = jnp.where(fresh_ok, fresh, NEGATIVE)
        fresh_s[pair] = fresh
        top = jnp.full((32, PAGE), NEGATIVE, F32)
        for a in range(2):
            r = pair * 2 + a
            used = table[2, 16 + r]
            for b in range(SHORT_BLK):
                s = nt_dot(q, k_c[table[0, r * SHORT_BLK + b]]) * SCALE
                s = jnp.where((half == a) & (lane < used - b * PAGE), s, NEGATIVE)
                short_s[pair, a * SHORT_BLK + b] = s
                top = jnp.maximum(top, s)
        m = jnp.maximum(jnp.max(top, axis=1, keepdims=True), jnp.max(fresh, axis=1, keepdims=True))
        top_s[pair] = jnp.broadcast_to(m, (32, HD))
        return carry

    lax.fori_loop(0, REQ_DEV // 2, pair_score, 0, unroll=2)

    trips = (table[2, 0] + UNROLL - 1) // UNROLL
    m_s[...] = jnp.full((LONGS, 16, HD), NEGATIVE, F32)
    l_s[...] = jnp.zeros((LONGS, 16, HD), F32)
    o_s[...] = jnp.zeros((LONGS, 16, HD), F32)
    key_lane = iota((16, PAGE), 1)

    def entry(e):
        word = table[1, e]
        return word % 128, word // 128 % 8, word // 1024

    def long_score(j, carry):
        got = []
        for i in range(UNROLL):
            e = j * UNROLL + i
            slot, key, limit = entry(e)
            s = nt_dot(q_all[2 * key], k_c[slot]) * SCALE
            s = jnp.where(key_lane < limit, s, NEGATIVE)
            long_s[e] = s
            got.append((key, s))
        for key, s in got:
            m_s[key] = jnp.maximum(m_s[key], s)
        return carry

    lax.fori_loop(0, trips, long_score, 0)
    for k in range(LONGS):
        m_s[k] = jnp.broadcast_to(jnp.maximum(jnp.max(m_s[k], axis=1, keepdims=True), 0.1 * NEGATIVE), (16, HD))
    copy.wait()

    def pair_sum(pair, carry):
        m = top_s[pair]
        w = jnp.exp(fresh_s[pair] - m[:, 0:ROWS]).astype(BF16)
        total = jnp.sum(w.astype(F32), axis=1, keepdims=True)
        acc = nn_dot(w, v_new[...])
        wsum = jnp.zeros((32, PAGE), F32)
        for i in range(2 * SHORT_BLK):
            w = jnp.exp(short_s[pair, i] - m).astype(BF16)
            wsum = wsum + w.astype(F32)
            acc = acc + nn_dot(w, v_c[table[0, pair * 2 * SHORT_BLK + i]])
        total = total + jnp.sum(wsum, axis=1, keepdims=True)
        acc_s[pair] = acc
        sum_s[pair] = jnp.broadcast_to(total, (32, HD))
        out = acc / total
        at = pl.multiple_of(pair * 8, 8)
        for g in range(G):
            att_s[pl.ds(at, 8), g * HD : (g + 1) * HD] = out[g * 8 : (g + 1) * 8, :]
        return carry

    lax.fori_loop(0, REQ_DEV // 2, pair_sum, 0, unroll=2)
    att[...] = att_s[...]
    for g in range(G):
        o_0[g * NEW : (g + 1) * NEW, :] = acc_s[0, g * 8 : g * 8 + NEW, :]
        m_0[g * NEW : (g + 1) * NEW, :] = top_s[0, g * 8 : g * 8 + NEW, :]
        l_0[g * NEW : (g + 1) * NEW, :] = sum_s[0, g * 8 : g * 8 + NEW, :]
    eye = (iota((16, HD), 0) == iota((16, HD), 1)) & (iota((16, HD), 0) < G * NEW)
    part0[...] = o_0[...]
    part0[12:13, :] = to_row(m_0[...], eye)
    part0[13:14, :] = to_row(l_0[...], eye)
    part0[14:16, :] = jnp.zeros((2, HD), F32)

    def long_sum(j, carry):
        got = []
        for i in range(UNROLL):
            e = j * UNROLL + i
            slot, key, _ = entry(e)
            w = jnp.exp(long_s[e] - m_s[key]).astype(BF16)
            got.append((key, w.astype(F32), nn_dot(w, v_c[slot])))
        for key, w, o in got:
            l_s[key] = l_s[key] + w
            o_s[key] = o_s[key] + o
        return carry

    lax.fori_loop(0, trips, long_sum, 0)
    for k in range(LONGS):
        total = jnp.broadcast_to(jnp.sum(l_s[k], axis=1, keepdims=True), (16, HD))
        part[2 * k, 0:12, :] = o_s[k, 0:12, :].astype(BF16)
        part[2 * k, 12:14, :] = jnp.concatenate([spread(m_s[k]), spread(total)], axis=0).astype(BF16)
        part[2 * k, 14:16, :] = jnp.zeros((2, HD), BF16)
        part[2 * k + 1] = jnp.zeros((16, HD), BF16)


def spread(column):
    row = iota((16, HD), 0)
    lane = iota((16, HD), 1)
    out = jnp.zeros((16, HD), F32)
    rest = column
    for i in range(3):
        piece = lax.reduce_precision(rest, 8, 7)
        rest = rest - piece
        out = jnp.where((lane == row + 16 * i) & (row < G * NEW), piece, out)
    return jnp.sum(out, axis=0, keepdims=True)


def gathered(row):
    return row + pltpu.roll(row, HD - 16, 1) + pltpu.roll(row, HD - 32, 1)


def place():
    tensor = lax.axis_index("tensor")
    return tensor // 2, tensor % 2


def split_product(a, w, keep, send):
    core = place()[1]
    for x in range(TEN // 2):
        at = pl.multiple_of((2 * x + 1 - core) * COLS, COLS)
        send[x] = nn_dot(a, w[:, pl.ds(at, COLS)]).astype(BF16)
    for x in range(TEN // 2):
        at = pl.multiple_of((2 * x + core) * COLS, COLS)
        keep[x] = nn_dot(a, w[:, pl.ds(at, COLS)]).astype(keep.dtype)


def out_kernel(att, part0, parts, w_out, keep, send, att_s, m_s, l_s):
    att_s[...] = att[...]

    @pl.when(lax.axis_index("seq") % 2 == 0)
    def _():
        for s in range(SEQ):
            stats = parts[s].astype(F32)
            m_s[s : s + 1, :] = stats[12:13, :]
            l_s[s : s + 1, :] = stats[13:14, :]
        m0 = part0[12:13, :]
        m = gathered(m_s[...])
        top = jnp.maximum(jnp.max(m, axis=0, keepdims=True), m0)
        grow = jnp.exp(m - top)
        grow0 = jnp.exp(m0 - top)
        total = jnp.sum(grow * gathered(l_s[...]), axis=0, keepdims=True) + grow0 * part0[13:14, :]
        live = iota((1, HD), 1) < G * NEW
        inverse = jnp.where(live, 1.0 / jnp.where(live, total, 1.0), 0.0)
        eye = iota((16, HD), 0) == iota((16, HD), 1)

        def scaled(o, coef):
            column = jnp.sum(jnp.where(eye, coef, 0.0), axis=1, keepdims=True)
            return o * column

        out = scaled(part0[...], grow0 * inverse)
        coefs = grow * inverse
        for s in range(SEQ):
            out = out + scaled(parts[s].astype(F32), coefs[s : s + 1, :])
        for g in range(G):
            att_s[0:NEW, g * HD : (g + 1) * HD] = out[g * NEW : (g + 1) * NEW, :]

    split_product(att_s[...].astype(BF16), w_out, keep, send)


def pair_kernel(keep, got, own, s1, s2, s3):
    x = place()[0]
    own[...] = keep[x].astype(F32) + got[x].astype(F32)
    for d, out in ((1, s1), (2, s2), (3, s3)):
        to = (x + d) % 4
        out[...] = (keep[to].astype(F32) + got[to].astype(F32)).astype(BF16)


def residual_kernel(tok, own, r1, r2, r3, res, x_s):
    at = pl.multiple_of(lax.axis_index("tensor") * COLS, COLS)
    for r in range(REQ_DEV):
        x_s[r * NEW : (r + 1) * NEW, :] = tok[r, :, pl.ds(at, COLS)].astype(F32)
    total = own[...] + r1[...].astype(F32) + r2[...].astype(F32) + r3[...].astype(F32)
    res[...] = (x_s[...] + total).astype(BF16)


def mlp_kernel(mine, other, gain, w_gate, w_up, w_down, keep, send):
    x, core = place()
    square = jnp.zeros((ROWS, 1), F32)
    for d in range(4):
        for blocks in (mine, other):
            v = blocks[d].astype(F32)
            square = square + jnp.sum(v * v, axis=1, keepdims=True)
    inverse = lax.rsqrt(square * (1.0 / D) + EPSILON)
    gate = jnp.zeros((ROWS, FF_DEV), F32)
    up = jnp.zeros((ROWS, FF_DEV), F32)
    for d in range(4):
        for c, blocks in ((core, mine), (1 - core, other)):
            b = (x + 4 - d) % 4 * 2 + c
            at = pl.multiple_of(b * COLS, COLS)
            normed = (blocks[d].astype(F32) * inverse * gain[:, pl.ds(at, COLS)].astype(F32)).astype(BF16)
            gate = gate + nn_dot(normed, w_gate[pl.ds(at, COLS), :])
            up = up + nn_dot(normed, w_up[pl.ds(at, COLS), :])
    activated = (gate / (1.0 + jnp.exp(-gate)) * up).astype(BF16)
    split_product(activated, w_down, keep, send)


def final_kernel(res, own, r1, r2, r3, out):
    total = own[...] + r1[...].astype(F32) + r2[...].astype(F32) + r3[...].astype(F32)
    total = (res[...].astype(F32) + total).astype(BF16)
    for r in range(REQ_DEV):
        out[r] = total[r * NEW : (r + 1) * NEW, :]


def swap_core(v):
    return lax.ppermute(v, "tensor", [(i, i ^ 1) for i in range(TEN)])


def along_x(v, d):
    return lax.ppermute(v, "tensor", [(i, (i + 2 * d) % TEN) for i in range(TEN)])


def scatter_sum(keep, send):
    got = swap_core(send)
    block = sds((ROWS, COLS), BF16)
    own, s1, s2, s3 = call(
        pair_kernel,
        (sds((ROWS, COLS), F32), block, block, block),
        [VMEM, VMEM],
        [],
        1,
        "pair_add",
    )(keep, got)
    r2 = along_x(s2, 2)
    return own, along_x(s1, 1), r2, along_x(s3, 3)


def per_device(
    tokens,
    lengths,
    page_request,
    page_block,
    k_cache,
    v_cache,
    attn_gain,
    w_query,
    w_key,
    w_value,
    w_out,
    mlp_gain,
    w_gate,
    w_up,
    w_down,
):
    half = np.arange(HD) % (HD // 2)
    inv = jnp.asarray((1.0 / ROPE_BASE ** (half * 2.0 / HD)).astype(np.float32).reshape(1, HD))
    k_cache = k_cache.reshape(SLOTS, PAGE, HD)
    v_cache = v_cache.reshape(SLOTS, PAGE, HD)
    dma = pltpu.SemaphoreType.DMA

    def in_hbm(*arrays):
        return tuple(pltpu.with_memory_space_constraint(a, pltpu.HBM) for a in arrays)

    q_pack, k_new, v_new, q_long, table = call(
        qkv_kernel,
        (
            sds((REQ_DEV // 2 * 32, HD), F32),
            sds((ROWS, HD), BF16),
            sds((ROWS, HD), BF16),
            sds((SEQ, 16, HD), BF16),
            pltpu.SMEM((8, SLOTS), jnp.int32),
        ),
        [HBM] * 9,
        [
            pltpu.SMEM(lengths.shape, jnp.int32),
            pltpu.VMEM((1, SLOTS), jnp.int32),
            pltpu.VMEM((1, SLOTS), jnp.int32),
            pltpu.VMEM(tokens.shape, BF16),
            pltpu.VMEM((D,), BF16),
            pltpu.VMEM((1, HD), F32),
            pltpu.VMEM(w_query.shape, BF16),
            pltpu.VMEM(w_key.shape, BF16),
            pltpu.VMEM(w_value.shape, BF16),
            pltpu.VMEM((ROWS, D), F32),
            pltpu.VMEM((ROWS, HD), jnp.int32),
            pltpu.VMEM((16, HD), F32),
            pltpu.VMEM((8, SLOTS), jnp.int32),
            dma((11,)),
            dma(()),
        ],
        8,
        "qkv",
        [VMEM] * 4 + [SMEM],
    )(*in_hbm(lengths, page_request, page_block, tokens, attn_gain, inv, w_query, w_key, w_value))

    q_all = lax.all_to_all(q_long, "seq", 0, 0, tiled=True)

    column = pltpu.VMEM((16, HD), F32)
    longs = pltpu.VMEM((LONGS, 16, HD), F32)
    pairs = REQ_DEV // 2
    att, part0, part = call(
        attend_kernel,
        (sds((ROWS, QCOLS), F32), sds((16, HD), F32), sds((SEQ, 16, HD), BF16)),
        [SMEM] + [VMEM] * 5 + [HBM],
        [
            pltpu.VMEM(v_cache.shape, BF16),
            pltpu.VMEM((pairs, 32, ROWS), F32),
            pltpu.VMEM((pairs, 2 * SHORT_BLK, 32, PAGE), F32),
            pltpu.VMEM((pairs, 32, HD), F32),
            pltpu.VMEM((pairs, 32, HD), F32),
            pltpu.VMEM((pairs, 32, HD), F32),
            pltpu.VMEM((ROWS, QCOLS), F32),
            column,
            column,
            column,
            pltpu.VMEM((SLOTS, 16, PAGE), F32),
            longs,
            longs,
            longs,
            dma(()),
        ],
        10,
        "attend",
    )(table, q_pack, k_new, v_new, q_all, k_cache, *in_hbm(v_cache))

    parts = lax.all_to_all(part, "seq", 0, 0, tiled=True)

    halves = (sds((TEN // 2, ROWS, COLS), BF16), sds((TEN // 2, ROWS, COLS), BF16))
    keep, send = call(
        out_kernel,
        halves,
        [VMEM] * 4,
        [pltpu.VMEM((ROWS, QCOLS), F32), pltpu.VMEM((SEQ, HD), F32), pltpu.VMEM((SEQ, HD), F32)],
        2,
        "out_proj",
    )(att, part0, parts, w_out)
    own, r1, r2, r3 = scatter_sum(keep, send)

    res = call(
        residual_kernel,
        sds((ROWS, COLS), BF16),
        [VMEM] * 5,
        [pltpu.VMEM((ROWS, COLS), F32)],
        1,
        "residual",
    )(tokens, own, r1, r2, r3)

    mine = jnp.stack([res] + [along_x(res, d) for d in (1, 2, 3)])
    other = swap_core(mine)

    keep, send = call(
        mlp_kernel,
        halves,
        [VMEM] * 6,
        [],
        4,
        "mlp",
    )(mine, other, mlp_gain.reshape(1, D), w_gate, w_up, w_down)
    own, r1, r2, r3 = scatter_sum(keep, send)

    return call(
        final_kernel,
        sds((REQ_DEV, NEW, COLS), BF16),
        [VMEM] * 5,
        [],
        1,
        "final",
    )(res, own, r1, r2, r3)


def solution(mesh):
    placed = (
        P("seq", None, None),
        P(),
        P("seq"),
        P("seq"),
        P("seq", "tensor", None, None),
        P("seq", "tensor", None, None),
        P(),
        P(None, "tensor"),
        P(None, "tensor"),
        P(None, "tensor"),
        P("tensor", None),
        P(),
        P(None, "tensor"),
        P(None, "tensor"),
        P("tensor", None),
    )
    return jax.shard_map(
        per_device, mesh=mesh, in_specs=placed, out_specs=P("seq", None, "tensor"), check_vma=False
    )
```

```python
import math

import jax
import jax.numpy as jnp
import numpy as np
from jax import lax
from jax.experimental import pallas as pl
from jax.experimental.pallas import tpu as pltpu
from jax.sharding import PartitionSpec as P

EPSILON = 1e-05
NEGATIVE = -1e30
ROPE_BASE = 500000.0
F32 = jnp.float32
BF16 = jnp.bfloat16

SEQ = 16
TEN = 8
D = 3072
HD = 128
PAGE = 128
REQ_DEV = 16
NEW = 4
G = 3
ROWS = REQ_DEV * NEW
QCOLS = G * HD
COLS = D // TEN
FF_DEV = 512
SLOTS = 128
LONG_STEP = 32
LONGS = 8
SHORT_BLK = 4
SCALE = 1.0 / math.sqrt(HD)
CHUNK = 8


VMEM = pl.BlockSpec(memory_space=pltpu.VMEM)
SMEM = pl.BlockSpec(memory_space=pltpu.SMEM)
HBM = pl.BlockSpec(memory_space=pltpu.HBM)
MIB = 1 << 20


def call(kernel, out_shape, in_specs, scratch, limit, name, out_specs=None):
    return pl.pallas_call(
        kernel,
        out_shape=out_shape,
        in_specs=in_specs,
        out_specs=out_specs or jax.tree.map(lambda _: VMEM, out_shape),
        scratch_shapes=scratch,
        compiler_params=pltpu.CompilerParams(vmem_limit_bytes=limit * MIB),
        name=name,
    )


def sds(shape, dtype):
    return jax.ShapeDtypeStruct(shape, dtype)


def nt_dot(a, b):
    return lax.dot_general(a, b, (((1,), (1,)), ((), ())), preferred_element_type=F32)


def nn_dot(a, b):
    return jnp.dot(a, b, preferred_element_type=F32)


def iota(shape, dim):
    return lax.broadcasted_iota(jnp.int32, shape, dim)


def start_all(pairs, sems):
    copies = [pltpu.make_async_copy(src, dst, sems.at[i]) for i, (src, dst) in enumerate(pairs)]
    for copy in copies:
        copy.start(priority=1)
    return copies


def qkv_kernel(
    lengths_h, request_h, block_h, tok_h, gain_h, inv_h, wq_h, wk_h, wv_h,
    q_pack, k_new, v_new, q_long, table,
    lengths, request, block, tok, gain, inv, wq, wk, wv, x_s, pos_s, t_s, table_s, sems, table_sem,
):
    third = D // 3
    copies = start_all(
        [(tok_h, tok), (gain_h, gain), (lengths_h, lengths), (inv_h, inv)]
        + [(wq_h.at[pl.ds(i * third, third)], wq.at[pl.ds(i * third, third)]) for i in range(3)]
        + [(wk_h, wk), (wv_h, wv), (request_h, request.at[0]), (block_h, block.at[0])],
        sems,
    )
    home = lax.axis_index("seq") * REQ_DEV
    copies[9].wait()
    copies[10].wait()
    copies[2].wait()
    req = jnp.broadcast_to(request[...], (8, SLOTS))
    blk = jnp.broadcast_to(block[...], (8, SLOTS))
    lane = iota((8, SLOTS), 1)
    long_len = jnp.zeros((8, SLOTS), jnp.int32)
    for k in range(LONGS):
        long_len = jnp.where(req == k * LONG_STEP, lengths[k * LONG_STEP], long_len)
    limit = long_len - blk * PAGE
    key = jnp.where(limit > 0, req // LONG_STEP, LONGS)
    start = jnp.zeros((8, SLOTS), F32)
    first = jnp.zeros((8, SLOTS), F32)
    for k in range(LONGS):
        held = jnp.sum(jnp.where(key == k, 1.0, 0.0), axis=1, keepdims=True)
        first = jnp.where(key == k, start, first)
        start = start + jnp.floor((held + (CHUNK - 1)) * (1.0 / CHUNK)) * CHUNK
    packed = lane + key * 128 + jnp.minimum(limit, PAGE) * 1024
    mine = (req >= home) & (req < home + REQ_DEV) & (blk < SHORT_BLK)
    index = jnp.where(mine, (req - home) * SHORT_BLK + blk, -1)
    slot = iota((SLOTS, SLOTS), 0)
    spot = iota((SLOTS, SLOTS), 1)

    def column(row):
        wide = jnp.broadcast_to(row[0:1, :].astype(F32), (SLOTS, SLOTS))
        return jnp.sum(jnp.where(slot == spot, wide, 0.0), axis=1, keepdims=True)

    def scatter(at, value):
        return jnp.sum(jnp.where(at == spot.astype(F32), value, 0.0), axis=0, keepdims=True).astype(jnp.int32)

    table_s[0:1, :] = scatter(column(index), slot.astype(F32))
    keys = key[0:1, :].astype(F32)
    ahead = jnp.sum(jnp.where((column(key) == keys) & (slot < spot), 1.0, 0.0), axis=0, keepdims=True)
    at = column(jnp.where(keys < LONGS, first[0:1, :] + ahead, -1.0))
    words = column(packed)
    table_s[1:2, :] = scatter(at, words)
    table_s[2:3, :] = scatter(at - SLOTS, words)
    facts = jnp.where(lane == 0, (start * (1.0 / CHUNK)).astype(jnp.int32), 0)
    for r in range(REQ_DEV):
        known = jnp.where((home + r) % LONG_STEP == 0, 0, lengths[home + r])
        facts = jnp.where(lane == 16 + r, known, facts)
    table_s[3:4, :] = facts[0:1, :]
    table_s[4:8, :] = jnp.zeros((4, SLOTS), jnp.int32)
    give = pltpu.make_async_copy(table_s, table, table_sem)
    give.start()
    copies[0].wait()
    for r in range(REQ_DEV):
        x_s[r * NEW : (r + 1) * NEW, :] = tok[r].astype(F32)
    x = x_s[...]
    mean_square = jnp.mean(x * x, axis=-1, keepdims=True)
    copies[1].wait()
    normed = (x * lax.rsqrt(mean_square + EPSILON) * gain[...].astype(F32).reshape(1, D)).astype(BF16)
    for r in range(REQ_DEV):
        pos_s[r * NEW : (r + 1) * NEW, :] = lengths[home + r] + iota((NEW, HD), 0)
    copies[3].wait()
    angle = pos_s[...].astype(F32) * inv[...]
    cosine = jnp.cos(angle)
    sine = jnp.sin(angle)
    sine = jnp.where(iota((ROWS, HD), 1) < HD // 2, -sine, sine)

    def rope(v):
        return v * cosine + pltpu.roll(v, HD // 2, 1) * sine

    q = jnp.zeros((ROWS, QCOLS), F32)
    for i in range(3):
        copies[4 + i].wait()
        q = q + nn_dot(normed[:, i * third : (i + 1) * third], wq[i * third : (i + 1) * third, :])
    for g in range(G):
        roped = rope(q[:, g * HD : (g + 1) * HD])
        for pair in range(REQ_DEV // 2):
            q_pack[pair * 32 + g * 8 : pair * 32 + g * 8 + 8, :] = roped[pair * 8 : pair * 8 + 8, :]
        t_s[g * NEW : (g + 1) * NEW, :] = roped[0:NEW, :]
    t_s[G * NEW : 16, :] = jnp.zeros((16 - G * NEW, HD), F32)
    for pair in range(REQ_DEV // 2):
        q_pack[pair * 32 + 24 : pair * 32 + 32, :] = jnp.zeros((8, HD), F32)
    packed = t_s[...].astype(BF16)
    for i in range(SEQ):
        q_long[i] = packed
    copies[7].wait()
    k_new[...] = rope(nn_dot(normed, wk[...])).astype(BF16)
    copies[8].wait()
    v_new[...] = nn_dot(normed, wv[...]).astype(BF16)
    give.wait()


def to_row(column, eye):
    return jnp.sum(jnp.where(eye, column, 0.0), axis=0, keepdims=True)


def attend_kernel(
    table, q_pack, k_new, v_new, q_all, k_c, v_h,
    att, part0, part,
    v_c, fresh_s, short_s, top_s, acc_s, sum_s, att_s, o_0, m_0, l_0, long_s, m_s, l_s, o_s, sem,
):
    copy = pltpu.make_async_copy(v_h, v_c, sem)
    copy.start(priority=1)
    row = iota((32, ROWS), 0)
    col = iota((32, ROWS), 1)
    lane = iota((32, PAGE), 1)
    half = iota((32, PAGE), 0) % 8 // NEW

    def pair_score(pair, carry):
        q = q_pack[pl.ds(pl.multiple_of(pair * 32, 32), 32), :].astype(BF16)
        fresh = nt_dot(q, k_new[...]) * SCALE
        fresh_ok = (pair * 2 + row % 8 // NEW == col // NEW) & (col % NEW <= row % NEW)
        fresh = jnp.where(fresh_ok, fresh, NEGATIVE)
        fresh_s[pair] = fresh
        pages = [k_c[table[0, pair * CHUNK + i]] for i in range(CHUNK)]
        s = nt_dot(q, jnp.concatenate(pages, axis=0)) * SCALE
        own = jnp.where(half == 0, table[3, 16 + pair * 2], table[3, 17 + pair * 2])
        tops = []
        for i in range(CHUNK):
            inside = (half == i // SHORT_BLK) & (lane < own - i % SHORT_BLK * PAGE)
            part_s = jnp.where(inside, s[:, i * PAGE : (i + 1) * PAGE], NEGATIVE)
            short_s[pair, :, i * PAGE : (i + 1) * PAGE] = part_s
            tops.append(part_s)
        while len(tops) > 1:
            tops = [jnp.maximum(x, y) for x, y in zip(tops[::2], tops[1::2])]
        m = jnp.maximum(jnp.max(tops[0], axis=1, keepdims=True), jnp.max(fresh, axis=1, keepdims=True))
        top_s[pair] = jnp.broadcast_to(m, (32, HD))
        return carry

    lax.fori_loop(0, REQ_DEV // 2, pair_score, 0, unroll=2)

    trips = (table[3, 0] + 1) // 2
    m_s[...] = jnp.full((LONGS, 16, HD), NEGATIVE, F32)
    l_s[...] = jnp.zeros((LONGS, 16, HD), F32)
    o_s[...] = jnp.zeros((LONGS, 16, HD), F32)
    key_lane = iota((16, PAGE), 1)

    def entries(chunk):
        words = [table[1 + chunk // (SLOTS // CHUNK), chunk % (SLOTS // CHUNK) * CHUNK + i] for i in range(CHUNK)]
        return words, (words[0] >> 7) & 7

    def long_score(j, carry):
        got = []
        for chunk in (2 * j, 2 * j + 1):
            words, key = entries(chunk)
            pages = [k_c[word & 127] for word in words]
            s = nt_dot(q_all[2 * key], jnp.concatenate(pages, axis=0)) * SCALE
            tops = []
            for i, word in enumerate(words):
                part_s = jnp.where(key_lane < (word >> 10), s[:, i * PAGE : (i + 1) * PAGE], NEGATIVE)
                long_s[chunk, :, i * PAGE : (i + 1) * PAGE] = part_s
                tops.append(part_s)
            while len(tops) > 1:
                tops = [jnp.maximum(x, y) for x, y in zip(tops[::2], tops[1::2])]
            got.append((key, tops[0]))
        for key, top in got:
            m_s[key] = jnp.maximum(m_s[key], top)
        return carry

    lax.fori_loop(0, trips, long_score, 0)
    for k in range(LONGS):
        m_s[k] = jnp.broadcast_to(jnp.maximum(jnp.max(m_s[k], axis=1, keepdims=True), 0.1 * NEGATIVE), (16, HD))
    copy.wait()

    def pair_sum(pair, carry):
        m = top_s[pair]
        w = jnp.exp(fresh_s[pair] - m[:, 0:ROWS]).astype(BF16)
        total = jnp.sum(w.astype(F32), axis=1, keepdims=True)
        acc = nn_dot(w, v_new[...])
        ws = [jnp.exp(short_s[pair, :, i * PAGE : (i + 1) * PAGE] - m).astype(BF16) for i in range(CHUNK)]
        pages = [v_c[table[0, pair * CHUNK + i]] for i in range(CHUNK)]
        acc = acc + nn_dot(jnp.concatenate(ws, axis=1), jnp.concatenate(pages, axis=0))
        total = total + jnp.sum(sum(w.astype(F32) for w in ws), axis=1, keepdims=True)
        acc_s[pair] = acc
        sum_s[pair] = jnp.broadcast_to(total, (32, HD))
        out = acc / total
        at = pl.multiple_of(pair * 8, 8)
        for g in range(G):
            att_s[pl.ds(at, 8), g * HD : (g + 1) * HD] = out[g * 8 : (g + 1) * 8, :]
        return carry

    lax.fori_loop(0, REQ_DEV // 2, pair_sum, 0, unroll=2)
    att[...] = att_s[...]
    for g in range(G):
        o_0[g * NEW : (g + 1) * NEW, :] = acc_s[0, g * 8 : g * 8 + NEW, :]
        m_0[g * NEW : (g + 1) * NEW, :] = top_s[0, g * 8 : g * 8 + NEW, :]
        l_0[g * NEW : (g + 1) * NEW, :] = sum_s[0, g * 8 : g * 8 + NEW, :]
    eye = (iota((16, HD), 0) == iota((16, HD), 1)) & (iota((16, HD), 0) < G * NEW)
    part0[...] = o_0[...]
    part0[12:13, :] = to_row(m_0[...], eye)
    part0[13:14, :] = to_row(l_0[...], eye)
    part0[14:16, :] = jnp.zeros((2, HD), F32)

    def long_sum(j, carry):
        got = []
        for chunk in (2 * j, 2 * j + 1):
            words, key = entries(chunk)
            m = m_s[key]
            ws = [jnp.exp(long_s[chunk, :, i * PAGE : (i + 1) * PAGE] - m).astype(BF16) for i in range(CHUNK)]
            pages = [v_c[word & 127] for word in words]
            o = nn_dot(jnp.concatenate(ws, axis=1), jnp.concatenate(pages, axis=0))
            got.append((key, sum(w.astype(F32) for w in ws), o))
        for key, w, o in got:
            l_s[key] = l_s[key] + w
            o_s[key] = o_s[key] + o
        return carry

    lax.fori_loop(0, trips, long_sum, 0)
    for k in range(LONGS):
        total = jnp.broadcast_to(jnp.sum(l_s[k], axis=1, keepdims=True), (16, HD))
        part[2 * k, 0:12, :] = o_s[k, 0:12, :].astype(BF16)
        part[2 * k, 12:14, :] = jnp.concatenate([spread(m_s[k]), spread(total)], axis=0).astype(BF16)
        part[2 * k, 14:16, :] = jnp.zeros((2, HD), BF16)
        part[2 * k + 1] = jnp.zeros((16, HD), BF16)


def spread(column):
    row = iota((16, HD), 0)
    lane = iota((16, HD), 1)
    out = jnp.zeros((16, HD), F32)
    rest = column
    for i in range(3):
        piece = lax.reduce_precision(rest, 8, 7)
        rest = rest - piece
        out = jnp.where((lane == row + 16 * i) & (row < G * NEW), piece, out)
    return jnp.sum(out, axis=0, keepdims=True)


def gathered(row):
    return row + pltpu.roll(row, HD - 16, 1) + pltpu.roll(row, HD - 32, 1)


def place():
    tensor = lax.axis_index("tensor")
    return tensor // 2, tensor % 2


def split_product(a, w, keep, send):
    core = place()[1]
    for x in range(TEN // 2):
        at = pl.multiple_of((2 * x + 1 - core) * COLS, COLS)
        send[x] = nn_dot(a, w[:, pl.ds(at, COLS)]).astype(BF16)
    for x in range(TEN // 2):
        at = pl.multiple_of((2 * x + core) * COLS, COLS)
        keep[x] = nn_dot(a, w[:, pl.ds(at, COLS)]).astype(keep.dtype)


def out_kernel(att, part0, parts, w_out, keep, send, att_s, m_s, l_s):
    att_s[...] = att[...]

    @pl.when(lax.axis_index("seq") % 2 == 0)
    def _():
        for s in range(SEQ):
            stats = parts[s].astype(F32)
            m_s[s : s + 1, :] = stats[12:13, :]
            l_s[s : s + 1, :] = stats[13:14, :]
        m0 = part0[12:13, :]
        m = gathered(m_s[...])
        top = jnp.maximum(jnp.max(m, axis=0, keepdims=True), m0)
        grow = jnp.exp(m - top)
        grow0 = jnp.exp(m0 - top)
        total = jnp.sum(grow * gathered(l_s[...]), axis=0, keepdims=True) + grow0 * part0[13:14, :]
        live = iota((1, HD), 1) < G * NEW
        inverse = jnp.where(live, 1.0 / jnp.where(live, total, 1.0), 0.0)
        eye = iota((16, HD), 0) == iota((16, HD), 1)

        def scaled(o, coef):
            column = jnp.sum(jnp.where(eye, coef, 0.0), axis=1, keepdims=True)
            return o * column

        out = scaled(part0[...], grow0 * inverse)
        coefs = grow * inverse
        for s in range(SEQ):
            out = out + scaled(parts[s].astype(F32), coefs[s : s + 1, :])
        for g in range(G):
            att_s[0:NEW, g * HD : (g + 1) * HD] = out[g * NEW : (g + 1) * NEW, :]

    split_product(att_s[...].astype(BF16), w_out, keep, send)


def pair_kernel(keep, got, own, s1, s2, s3):
    x = place()[0]
    own[...] = keep[x].astype(F32) + got[x].astype(F32)
    for d, out in ((1, s1), (2, s2), (3, s3)):
        to = (x + d) % 4
        out[...] = (keep[to].astype(F32) + got[to].astype(F32)).astype(BF16)


def residual_kernel(tok, own, r1, r2, r3, res, x_s):
    at = pl.multiple_of(lax.axis_index("tensor") * COLS, COLS)
    for r in range(REQ_DEV):
        x_s[r * NEW : (r + 1) * NEW, :] = tok[r, :, pl.ds(at, COLS)].astype(F32)
    total = own[...] + r1[...].astype(F32) + r2[...].astype(F32) + r3[...].astype(F32)
    res[...] = (x_s[...] + total).astype(BF16)


def mlp_kernel(mine, other, gain, w_gate, w_up, w_down, keep, send):
    x, core = place()
    square = jnp.zeros((ROWS, 1), F32)
    for d in range(4):
        for blocks in (mine, other):
            v = blocks[d].astype(F32)
            square = square + jnp.sum(v * v, axis=1, keepdims=True)
    inverse = lax.rsqrt(square * (1.0 / D) + EPSILON)
    gate = jnp.zeros((ROWS, FF_DEV), F32)
    up = jnp.zeros((ROWS, FF_DEV), F32)
    for d in range(4):
        for c, blocks in ((core, mine), (1 - core, other)):
            b = (x + 4 - d) % 4 * 2 + c
            at = pl.multiple_of(b * COLS, COLS)
            normed = (blocks[d].astype(F32) * inverse * gain[:, pl.ds(at, COLS)].astype(F32)).astype(BF16)
            gate = gate + nn_dot(normed, w_gate[pl.ds(at, COLS), :])
            up = up + nn_dot(normed, w_up[pl.ds(at, COLS), :])
    activated = (gate / (1.0 + jnp.exp(-gate)) * up).astype(BF16)
    split_product(activated, w_down, keep, send)


def final_kernel(res, own, r1, r2, r3, out):
    total = own[...] + r1[...].astype(F32) + r2[...].astype(F32) + r3[...].astype(F32)
    total = (res[...].astype(F32) + total).astype(BF16)
    for r in range(REQ_DEV):
        out[r] = total[r * NEW : (r + 1) * NEW, :]


def swap_core(v):
    return lax.ppermute(v, "tensor", [(i, i ^ 1) for i in range(TEN)])


def along_x(v, d):
    return lax.ppermute(v, "tensor", [(i, (i + 2 * d) % TEN) for i in range(TEN)])


def scatter_sum(keep, send):
    got = swap_core(send)
    block = sds((ROWS, COLS), BF16)
    own, s1, s2, s3 = call(
        pair_kernel,
        (sds((ROWS, COLS), F32), block, block, block),
        [VMEM, VMEM],
        [],
        1,
        "pair_add",
    )(keep, got)
    r2 = along_x(s2, 2)
    return own, along_x(s1, 1), r2, along_x(s3, 3)


def per_device(
    tokens,
    lengths,
    page_request,
    page_block,
    k_cache,
    v_cache,
    attn_gain,
    w_query,
    w_key,
    w_value,
    w_out,
    mlp_gain,
    w_gate,
    w_up,
    w_down,
):
    half = np.arange(HD) % (HD // 2)
    inv = jnp.asarray((1.0 / ROPE_BASE ** (half * 2.0 / HD)).astype(np.float32).reshape(1, HD))
    k_cache = k_cache.reshape(SLOTS, PAGE, HD)
    v_cache = v_cache.reshape(SLOTS, PAGE, HD)
    dma = pltpu.SemaphoreType.DMA

    def in_hbm(*arrays):
        return tuple(pltpu.with_memory_space_constraint(a, pltpu.HBM) for a in arrays)

    q_pack, k_new, v_new, q_long, table = call(
        qkv_kernel,
        (
            sds((REQ_DEV // 2 * 32, HD), F32),
            sds((ROWS, HD), BF16),
            sds((ROWS, HD), BF16),
            sds((SEQ, 16, HD), BF16),
            pltpu.SMEM((8, SLOTS), jnp.int32),
        ),
        [HBM] * 9,
        [
            pltpu.SMEM(lengths.shape, jnp.int32),
            pltpu.VMEM((1, SLOTS), jnp.int32),
            pltpu.VMEM((1, SLOTS), jnp.int32),
            pltpu.VMEM(tokens.shape, BF16),
            pltpu.VMEM((D,), BF16),
            pltpu.VMEM((1, HD), F32),
            pltpu.VMEM(w_query.shape, BF16),
            pltpu.VMEM(w_key.shape, BF16),
            pltpu.VMEM(w_value.shape, BF16),
            pltpu.VMEM((ROWS, D), F32),
            pltpu.VMEM((ROWS, HD), jnp.int32),
            pltpu.VMEM((16, HD), F32),
            pltpu.VMEM((8, SLOTS), jnp.int32),
            dma((11,)),
            dma(()),
        ],
        8,
        "qkv",
        [VMEM] * 4 + [SMEM],
    )(*in_hbm(lengths, page_request, page_block, tokens, attn_gain, inv, w_query, w_key, w_value))

    q_all = lax.all_to_all(q_long, "seq", 0, 0, tiled=True)

    column = pltpu.VMEM((16, HD), F32)
    longs = pltpu.VMEM((LONGS, 16, HD), F32)
    pairs = REQ_DEV // 2
    att, part0, part = call(
        attend_kernel,
        (sds((ROWS, QCOLS), F32), sds((16, HD), F32), sds((SEQ, 16, HD), BF16)),
        [SMEM] + [VMEM] * 5 + [HBM],
        [
            pltpu.VMEM(v_cache.shape, BF16),
            pltpu.VMEM((pairs, 32, ROWS), F32),
            pltpu.VMEM((pairs, 32, CHUNK * PAGE), F32),
            pltpu.VMEM((pairs, 32, HD), F32),
            pltpu.VMEM((pairs, 32, HD), F32),
            pltpu.VMEM((pairs, 32, HD), F32),
            pltpu.VMEM((ROWS, QCOLS), F32),
            column,
            column,
            column,
            pltpu.VMEM((2 * SLOTS // CHUNK, 16, CHUNK * PAGE), F32),
            longs,
            longs,
            longs,
            dma(()),
        ],
        10,
        "attend",
    )(table, q_pack, k_new, v_new, q_all, k_cache, *in_hbm(v_cache))

    parts = lax.all_to_all(part, "seq", 0, 0, tiled=True)

    halves = (sds((TEN // 2, ROWS, COLS), BF16), sds((TEN // 2, ROWS, COLS), BF16))
    keep, send = call(
        out_kernel,
        halves,
        [VMEM] * 4,
        [pltpu.VMEM((ROWS, QCOLS), F32), pltpu.VMEM((SEQ, HD), F32), pltpu.VMEM((SEQ, HD), F32)],
        2,
        "out_proj",
    )(att, part0, parts, w_out)
    own, r1, r2, r3 = scatter_sum(keep, send)

    res = call(
        residual_kernel,
        sds((ROWS, COLS), BF16),
        [VMEM] * 5,
        [pltpu.VMEM((ROWS, COLS), F32)],
        1,
        "residual",
    )(tokens, own, r1, r2, r3)

    mine = jnp.stack([res] + [along_x(res, d) for d in (1, 2, 3)])
    other = swap_core(mine)

    keep, send = call(
        mlp_kernel,
        halves,
        [VMEM] * 6,
        [],
        4,
        "mlp",
    )(mine, other, mlp_gain.reshape(1, D), w_gate, w_up, w_down)
    own, r1, r2, r3 = scatter_sum(keep, send)

    return call(
        final_kernel,
        sds((REQ_DEV, NEW, COLS), BF16),
        [VMEM] * 5,
        [],
        1,
        "final",
    )(res, own, r1, r2, r3)


def solution(mesh):
    placed = (
        P("seq", None, None),
        P(),
        P("seq"),
        P("seq"),
        P("seq", "tensor", None, None),
        P("seq", "tensor", None, None),
        P(),
        P(None, "tensor"),
        P(None, "tensor"),
        P(None, "tensor"),
        P("tensor", None),
        P(),
        P(None, "tensor"),
        P(None, "tensor"),
        P("tensor", None),
    )
    return jax.shard_map(
        per_device, mesh=mesh, in_specs=placed, out_specs=P("seq", None, "tensor"), check_vma=False
    )
```

```python
import math

import jax
import jax.numpy as jnp
import numpy as np
from jax import lax
from jax.experimental import pallas as pl
from jax.experimental.pallas import tpu as pltpu
from jax.sharding import PartitionSpec as P


EPSILON = 1e-05
NEGATIVE = -1e30
ROPE_BASE = 500000.0
F32 = jnp.float32
BF16 = jnp.bfloat16

SEQ = 16
TEN = 8
D = 3072
HD = 128
PAGE = 128
REQ_DEV = 16
NEW = 4
G = 3
ROWS = REQ_DEV * NEW
QCOLS = G * HD
COLS = D // TEN
FF_DEV = 512
SLOTS = 128
LONG_STEP = 32
LONGS = 8
SHORT_BLK = 4
SCALE = 1.0 / math.sqrt(HD)
CHUNK = 8


VMEM = pl.BlockSpec(memory_space=pltpu.VMEM)
SMEM = pl.BlockSpec(memory_space=pltpu.SMEM)
HBM = pl.BlockSpec(memory_space=pltpu.HBM)
MIB = 1 << 20


def call(kernel, out_shape, in_specs, scratch, limit, out_specs=None):
    return pl.pallas_call(
        kernel,
        out_shape=out_shape,
        in_specs=in_specs,
        out_specs=out_specs or jax.tree.map(lambda _: VMEM, out_shape),
        scratch_shapes=scratch,
        compiler_params=pltpu.CompilerParams(vmem_limit_bytes=limit * MIB),
    )


def sds(shape, dtype):
    return jax.ShapeDtypeStruct(shape, dtype)


def nt_dot(a, b):
    return lax.dot_general(a, b, (((1,), (1,)), ((), ())), preferred_element_type=F32)


def nn_dot(a, b):
    return jnp.dot(a, b, preferred_element_type=F32)


def iota(shape, dim):
    return lax.broadcasted_iota(jnp.int32, shape, dim)


def start_all(pairs, sems):
    copies = [pltpu.make_async_copy(src, dst, sems.at[i]) for i, (src, dst) in enumerate(pairs)]
    for copy in copies:
        copy.start(priority=1)
    return copies


def qkv_kernel(
    lengths_h, request_h, block_h, tok_h, gain_h, inv_h, wq_h, wk_h, wv_h,
    q_pack, k_new, v_new, q_long, table,
    lengths, request, block, tok, gain, inv, wq, wk, wv, x_s, pos_s, t_s, table_s, sems, table_sem,
):
    third = D // 3
    copies = start_all(
        [(tok_h, tok), (gain_h, gain), (lengths_h, lengths), (inv_h, inv)]
        + [(wq_h.at[pl.ds(i * third, third)], wq.at[pl.ds(i * third, third)]) for i in range(3)]
        + [(wk_h, wk), (wv_h, wv), (request_h, request.at[0]), (block_h, block.at[0])],
        sems,
    )
    home = lax.axis_index("seq") * REQ_DEV
    copies[9].wait()
    copies[10].wait()
    copies[2].wait()
    req = jnp.broadcast_to(request[...], (8, SLOTS))
    blk = jnp.broadcast_to(block[...], (8, SLOTS))
    lane = iota((8, SLOTS), 1)
    long_len = jnp.zeros((8, SLOTS), jnp.int32)
    for k in range(LONGS):
        long_len = jnp.where(req == k * LONG_STEP, lengths[k * LONG_STEP], long_len)
    limit = long_len - blk * PAGE
    key = jnp.where(limit > 0, req // LONG_STEP, LONGS)
    start = jnp.zeros((8, SLOTS), F32)
    first = jnp.zeros((8, SLOTS), F32)
    for k in range(LONGS):
        held = jnp.sum(jnp.where(key == k, 1.0, 0.0), axis=1, keepdims=True)
        first = jnp.where(key == k, start, first)
        start = start + jnp.floor((held + (CHUNK - 1)) * (1.0 / CHUNK)) * CHUNK
    packed = lane + key * 128 + jnp.minimum(limit, PAGE) * 1024
    mine = (req >= home) & (req < home + REQ_DEV) & (blk < SHORT_BLK)
    index = jnp.where(mine, (req - home) * SHORT_BLK + blk, -1)
    slot = iota((SLOTS, SLOTS), 0)
    spot = iota((SLOTS, SLOTS), 1)

    def column(row):
        wide = jnp.broadcast_to(row[0:1, :].astype(F32), (SLOTS, SLOTS))
        return jnp.sum(jnp.where(slot == spot, wide, 0.0), axis=1, keepdims=True)

    def scatter(at, value):
        return jnp.sum(jnp.where(at == spot.astype(F32), value, 0.0), axis=0, keepdims=True).astype(jnp.int32)

    table_s[0:1, :] = scatter(column(index), slot.astype(F32))
    keys = key[0:1, :].astype(F32)
    ahead = jnp.sum(jnp.where((column(key) == keys) & (slot < spot), 1.0, 0.0), axis=0, keepdims=True)
    at = column(jnp.where(keys < LONGS, first[0:1, :] + ahead, -1.0))
    words = column(packed)
    table_s[1:2, :] = scatter(at, words)
    table_s[2:3, :] = scatter(at - SLOTS, words)
    facts = jnp.where(lane == 0, (start * (1.0 / CHUNK)).astype(jnp.int32), 0)
    for r in range(REQ_DEV):
        known = jnp.where((home + r) % LONG_STEP == 0, 0, lengths[home + r])
        facts = jnp.where(lane == 16 + r, known, facts)
    table_s[3:4, :] = facts[0:1, :]
    table_s[4:8, :] = jnp.zeros((4, SLOTS), jnp.int32)
    give = pltpu.make_async_copy(table_s, table, table_sem)
    give.start()
    copies[0].wait()
    for r in range(REQ_DEV):
        x_s[r * NEW : (r + 1) * NEW, :] = tok[r].astype(F32)
    x = x_s[...]
    mean_square = jnp.mean(x * x, axis=-1, keepdims=True)
    copies[1].wait()
    normed = (x * lax.rsqrt(mean_square + EPSILON) * gain[...].astype(F32).reshape(1, D)).astype(BF16)
    for r in range(REQ_DEV):
        pos_s[r * NEW : (r + 1) * NEW, :] = lengths[home + r] + iota((NEW, HD), 0)
    copies[3].wait()
    angle = pos_s[...].astype(F32) * inv[...]
    cosine = jnp.cos(angle)
    sine = jnp.sin(angle)
    sine = jnp.where(iota((ROWS, HD), 1) < HD // 2, -sine, sine)

    def rope(v):
        return v * cosine + pltpu.roll(v, HD // 2, 1) * sine

    q = jnp.zeros((ROWS, QCOLS), F32)
    for i in range(3):
        copies[4 + i].wait()
        q = q + nn_dot(normed[:, i * third : (i + 1) * third], wq[i * third : (i + 1) * third, :])
    for g in range(G):
        roped = rope(q[:, g * HD : (g + 1) * HD])
        for pair in range(REQ_DEV // 2):
            q_pack[pair * 32 + g * 8 : pair * 32 + g * 8 + 8, :] = roped[pair * 8 : pair * 8 + 8, :]
        t_s[g * NEW : (g + 1) * NEW, :] = roped[0:NEW, :]
    t_s[G * NEW : 16, :] = jnp.zeros((16 - G * NEW, HD), F32)
    for pair in range(REQ_DEV // 2):
        q_pack[pair * 32 + 24 : pair * 32 + 32, :] = jnp.zeros((8, HD), F32)
    packed = t_s[...].astype(BF16)
    for i in range(SEQ):
        q_long[i] = packed
    copies[7].wait()
    k_new[...] = rope(nn_dot(normed, wk[...])).astype(BF16)
    copies[8].wait()
    v_new[...] = nn_dot(normed, wv[...]).astype(BF16)
    give.wait()


def to_row(column, eye):
    return jnp.sum(jnp.where(eye, column, 0.0), axis=0, keepdims=True)


def attend_kernel(
    table, q_pack, k_new, v_new, q_all, k_c, v_h,
    att, part0, part,
    v_c, fresh_s, short_s, top_s, acc_s, sum_s, att_s, o_0, m_0, l_0, long_s, m_s, l_s, o_s, sem,
):
    copy = pltpu.make_async_copy(v_h, v_c, sem)
    copy.start(priority=1)
    row = iota((32, ROWS), 0)
    col = iota((32, ROWS), 1)
    lane = iota((32, PAGE), 1)
    half = iota((32, PAGE), 0) % 8 // NEW

    def pair_score(pair, carry):
        q = q_pack[pl.ds(pl.multiple_of(pair * 32, 32), 32), :].astype(BF16)
        fresh = nt_dot(q, k_new[...]) * SCALE
        fresh_ok = (pair * 2 + row % 8 // NEW == col // NEW) & (col % NEW <= row % NEW)
        fresh = jnp.where(fresh_ok, fresh, NEGATIVE)
        fresh_s[pair] = fresh
        pages = [k_c[table[0, pair * CHUNK + i]] for i in range(CHUNK)]
        s = nt_dot(q, jnp.concatenate(pages, axis=0)) * SCALE
        own = jnp.where(half == 0, table[3, 16 + pair * 2], table[3, 17 + pair * 2])
        tops = []
        for i in range(CHUNK):
            inside = (half == i // SHORT_BLK) & (lane < own - i % SHORT_BLK * PAGE)
            part_s = jnp.where(inside, s[:, i * PAGE : (i + 1) * PAGE], NEGATIVE)
            short_s[pair, :, i * PAGE : (i + 1) * PAGE] = part_s
            tops.append(part_s)
        while len(tops) > 1:
            tops = [jnp.maximum(x, y) for x, y in zip(tops[::2], tops[1::2])]
        m = jnp.maximum(jnp.max(tops[0], axis=1, keepdims=True), jnp.max(fresh, axis=1, keepdims=True))
        top_s[pair] = jnp.broadcast_to(m, (32, HD))
        return carry

    lax.fori_loop(0, REQ_DEV // 2, pair_score, 0, unroll=2)

    trips = (table[3, 0] + 1) // 2
    m_s[...] = jnp.full((LONGS, 16, HD), NEGATIVE, F32)
    l_s[...] = jnp.zeros((LONGS, 16, HD), F32)
    o_s[...] = jnp.zeros((LONGS, 16, HD), F32)
    key_lane = iota((16, PAGE), 1)

    def entries(chunk):
        words = [table[1 + chunk // (SLOTS // CHUNK), chunk % (SLOTS // CHUNK) * CHUNK + i] for i in range(CHUNK)]
        return words, (words[0] >> 7) & 7

    def long_score(j, carry):
        got = []
        for chunk in (2 * j, 2 * j + 1):
            words, key = entries(chunk)
            pages = [k_c[word & 127] for word in words]
            s = nt_dot(q_all[2 * key], jnp.concatenate(pages, axis=0)) * SCALE
            tops = []
            for i, word in enumerate(words):
                part_s = jnp.where(key_lane < (word >> 10), s[:, i * PAGE : (i + 1) * PAGE], NEGATIVE)
                long_s[chunk, :, i * PAGE : (i + 1) * PAGE] = part_s
                tops.append(part_s)
            while len(tops) > 1:
                tops = [jnp.maximum(x, y) for x, y in zip(tops[::2], tops[1::2])]
            got.append((key, tops[0]))
        for key, top in got:
            m_s[key] = jnp.maximum(m_s[key], top)
        return carry

    lax.fori_loop(0, trips, long_score, 0)
    for k in range(LONGS):
        m_s[k] = jnp.broadcast_to(jnp.maximum(jnp.max(m_s[k], axis=1, keepdims=True), 0.1 * NEGATIVE), (16, HD))
    copy.wait()

    def pair_sum(pair, carry):
        m = top_s[pair]
        w = jnp.exp(fresh_s[pair] - m[:, 0:ROWS]).astype(BF16)
        total = jnp.sum(w.astype(F32), axis=1, keepdims=True)
        acc = nn_dot(w, v_new[...])
        ws = [jnp.exp(short_s[pair, :, i * PAGE : (i + 1) * PAGE] - m).astype(BF16) for i in range(CHUNK)]
        pages = [v_c[table[0, pair * CHUNK + i]] for i in range(CHUNK)]
        acc = acc + nn_dot(jnp.concatenate(ws, axis=1), jnp.concatenate(pages, axis=0))
        total = total + jnp.sum(sum(w.astype(F32) for w in ws), axis=1, keepdims=True)
        acc_s[pair] = acc
        sum_s[pair] = jnp.broadcast_to(total, (32, HD))
        out = acc / total
        at = pl.multiple_of(pair * 8, 8)
        for g in range(G):
            att_s[pl.ds(at, 8), g * HD : (g + 1) * HD] = out[g * 8 : (g + 1) * 8, :]
        return carry

    lax.fori_loop(0, REQ_DEV // 2, pair_sum, 0, unroll=2)
    att[...] = att_s[...]
    for g in range(G):
        o_0[g * NEW : (g + 1) * NEW, :] = acc_s[0, g * 8 : g * 8 + NEW, :]
        m_0[g * NEW : (g + 1) * NEW, :] = top_s[0, g * 8 : g * 8 + NEW, :]
        l_0[g * NEW : (g + 1) * NEW, :] = sum_s[0, g * 8 : g * 8 + NEW, :]
    eye = (iota((16, HD), 0) == iota((16, HD), 1)) & (iota((16, HD), 0) < G * NEW)
    part0[...] = o_0[...]
    part0[12:13, :] = to_row(m_0[...], eye)
    part0[13:14, :] = to_row(l_0[...], eye)
    part0[14:16, :] = jnp.zeros((2, HD), F32)

    def long_sum(j, carry):
        got = []
        for chunk in (2 * j, 2 * j + 1):
            words, key = entries(chunk)
            m = m_s[key]
            ws = [jnp.exp(long_s[chunk, :, i * PAGE : (i + 1) * PAGE] - m).astype(BF16) for i in range(CHUNK)]
            pages = [v_c[word & 127] for word in words]
            o = nn_dot(jnp.concatenate(ws, axis=1), jnp.concatenate(pages, axis=0))
            got.append((key, sum(w.astype(F32) for w in ws), o))
        for key, w, o in got:
            l_s[key] = l_s[key] + w
            o_s[key] = o_s[key] + o
        return carry

    lax.fori_loop(0, trips, long_sum, 0)
    for k in range(LONGS):
        total = jnp.broadcast_to(jnp.sum(l_s[k], axis=1, keepdims=True), (16, HD))
        part[2 * k, 0:12, :] = o_s[k, 0:12, :].astype(BF16)
        part[2 * k, 12:14, :] = jnp.concatenate([spread(m_s[k]), spread(total)], axis=0).astype(BF16)
        part[2 * k, 14:16, :] = jnp.zeros((2, HD), BF16)
        part[2 * k + 1] = jnp.zeros((16, HD), BF16)


def spread(column):
    row = iota((16, HD), 0)
    lane = iota((16, HD), 1)
    out = jnp.zeros((16, HD), F32)
    rest = column
    for i in range(3):
        piece = lax.reduce_precision(rest, 8, 7)
        rest = rest - piece
        out = jnp.where((lane == row + 16 * i) & (row < G * NEW), piece, out)
    return jnp.sum(out, axis=0, keepdims=True)


def gathered(row):
    return row + pltpu.roll(row, HD - 16, 1) + pltpu.roll(row, HD - 32, 1)


def place():
    tensor = lax.axis_index("tensor")
    return tensor // 2, tensor % 2


def split_product(a, w, keep, send):
    core = place()[1]
    for x in range(TEN // 2):
        at = pl.multiple_of((2 * x + 1 - core) * COLS, COLS)
        send[x] = nn_dot(a, w[:, pl.ds(at, COLS)]).astype(BF16)
    for x in range(TEN // 2):
        at = pl.multiple_of((2 * x + core) * COLS, COLS)
        keep[x] = nn_dot(a, w[:, pl.ds(at, COLS)]).astype(keep.dtype)


def out_kernel(att, part0, parts, w_out, keep, send, att_s, m_s, l_s):
    att_s[...] = att[...]

    @pl.when(lax.axis_index("seq") % 2 == 0)
    def _():
        for s in range(SEQ):
            stats = parts[s].astype(F32)
            m_s[s : s + 1, :] = stats[12:13, :]
            l_s[s : s + 1, :] = stats[13:14, :]
        m0 = part0[12:13, :]
        m = gathered(m_s[...])
        top = jnp.maximum(jnp.max(m, axis=0, keepdims=True), m0)
        grow = jnp.exp(m - top)
        grow0 = jnp.exp(m0 - top)
        total = jnp.sum(grow * gathered(l_s[...]), axis=0, keepdims=True) + grow0 * part0[13:14, :]
        live = iota((1, HD), 1) < G * NEW
        inverse = jnp.where(live, 1.0 / jnp.where(live, total, 1.0), 0.0)
        eye = iota((16, HD), 0) == iota((16, HD), 1)

        def scaled(o, coef):
            column = jnp.sum(jnp.where(eye, coef, 0.0), axis=1, keepdims=True)
            return o * column

        out = scaled(part0[...], grow0 * inverse)
        coefs = grow * inverse
        for s in range(SEQ):
            out = out + scaled(parts[s].astype(F32), coefs[s : s + 1, :])
        for g in range(G):
            att_s[0:NEW, g * HD : (g + 1) * HD] = out[g * NEW : (g + 1) * NEW, :]

    split_product(att_s[...].astype(BF16), w_out, keep, send)


def pair_kernel(keep, got, own, s1, s2, s3):
    x = place()[0]
    own[...] = keep[x].astype(F32) + got[x].astype(F32)
    for d, out in ((1, s1), (2, s2), (3, s3)):
        to = (x + d) % 4
        out[...] = (keep[to].astype(F32) + got[to].astype(F32)).astype(BF16)


def core_sum_kernel(keep, got, out):
    out[...] = (keep[...].astype(F32) + got[...].astype(F32)).astype(BF16)


def residual_kernel(tok, own, r1, r2, r3, res, x_s):
    core = place()[1]
    for x in range(TEN // 2):
        at = pl.multiple_of((2 * x + core) * COLS, COLS)
        for r in range(REQ_DEV):
            x_s[r * NEW : (r + 1) * NEW, :] = tok[r, :, pl.ds(at, COLS)].astype(F32)
        total = own[x].astype(F32) + r1[x].astype(F32) + r2[x].astype(F32) + r3[x].astype(F32)
        res[x] = (x_s[...] + total).astype(BF16)


def mlp_kernel(mine, other, gain, w_gate, w_up, w_down, keep, send):
    core = place()[1]
    square = jnp.zeros((ROWS, 1), F32)
    for d in range(4):
        for blocks in (mine, other):
            v = blocks[d].astype(F32)
            square = square + jnp.sum(v * v, axis=1, keepdims=True)
    inverse = lax.rsqrt(square * (1.0 / D) + EPSILON)
    gate = jnp.zeros((ROWS, FF_DEV), F32)
    up = jnp.zeros((ROWS, FF_DEV), F32)
    for d in range(4):
        for c, blocks in ((core, mine), (1 - core, other)):
            b = 2 * d + c
            at = pl.multiple_of(b * COLS, COLS)
            normed = (blocks[d].astype(F32) * inverse * gain[:, pl.ds(at, COLS)].astype(F32)).astype(BF16)
            gate = gate + nn_dot(normed, w_gate[pl.ds(at, COLS), :])
            up = up + nn_dot(normed, w_up[pl.ds(at, COLS), :])
    activated = (gate / (1.0 + jnp.exp(-gate)) * up).astype(BF16)
    split_product(activated, w_down, keep, send)


def final_kernel(res, own, r1, r2, r3, out):
    total = own[...] + r1[...].astype(F32) + r2[...].astype(F32) + r3[...].astype(F32)
    total = (res[place()[0]].astype(F32) + total).astype(BF16)
    for r in range(REQ_DEV):
        out[r] = total[r * NEW : (r + 1) * NEW, :]


def swap_core(v):
    return lax.ppermute(v, "tensor", [(i, i ^ 1) for i in range(TEN)])


def along_x(v, d):
    return lax.ppermute(v, "tensor", [(i, (i + 2 * d) % TEN) for i in range(TEN)])


def scatter_sum(keep, send):
    got = swap_core(send)
    block = sds((ROWS, COLS), BF16)
    own, s1, s2, s3 = call(pair_kernel, (sds((ROWS, COLS), F32), block, block, block), [VMEM, VMEM], [], 1)(keep, got)
    return own, along_x(s1, 1), along_x(s2, 2), along_x(s3, 3)


def per_device(
    tokens,
    lengths,
    page_request,
    page_block,
    k_cache,
    v_cache,
    attn_gain,
    w_query,
    w_key,
    w_value,
    w_out,
    mlp_gain,
    w_gate,
    w_up,
    w_down,
):
    half = np.arange(HD) % (HD // 2)
    inv = jnp.asarray((1.0 / ROPE_BASE ** (half * 2.0 / HD)).astype(np.float32).reshape(1, HD))
    k_cache = k_cache.reshape(SLOTS, PAGE, HD)
    v_cache = v_cache.reshape(SLOTS, PAGE, HD)
    dma = pltpu.SemaphoreType.DMA

    def in_hbm(*arrays):
        return tuple(pltpu.with_memory_space_constraint(a, pltpu.HBM) for a in arrays)

    q_pack, k_new, v_new, q_long, table = call(
        qkv_kernel,
        (
            sds((REQ_DEV // 2 * 32, HD), F32),
            sds((ROWS, HD), BF16),
            sds((ROWS, HD), BF16),
            sds((SEQ, 16, HD), BF16),
            pltpu.SMEM((8, SLOTS), jnp.int32),
        ),
        [HBM] * 9,
        [
            pltpu.SMEM(lengths.shape, jnp.int32),
            pltpu.VMEM((1, SLOTS), jnp.int32),
            pltpu.VMEM((1, SLOTS), jnp.int32),
            pltpu.VMEM(tokens.shape, BF16),
            pltpu.VMEM((D,), BF16),
            pltpu.VMEM((1, HD), F32),
            pltpu.VMEM(w_query.shape, BF16),
            pltpu.VMEM(w_key.shape, BF16),
            pltpu.VMEM(w_value.shape, BF16),
            pltpu.VMEM((ROWS, D), F32),
            pltpu.VMEM((ROWS, HD), jnp.int32),
            pltpu.VMEM((16, HD), F32),
            pltpu.VMEM((8, SLOTS), jnp.int32),
            dma((11,)),
            dma(()),
        ],
        8,
        [VMEM] * 4 + [SMEM],
    )(*in_hbm(lengths, page_request, page_block, tokens, attn_gain, inv, w_query, w_key, w_value))

    q_all = lax.all_to_all(q_long, "seq", 0, 0, tiled=True)

    column = pltpu.VMEM((16, HD), F32)
    longs = pltpu.VMEM((LONGS, 16, HD), F32)
    pairs = REQ_DEV // 2
    att, part0, part = call(
        attend_kernel,
        (sds((ROWS, QCOLS), F32), sds((16, HD), F32), sds((SEQ, 16, HD), BF16)),
        [SMEM] + [VMEM] * 5 + [HBM],
        [
            pltpu.VMEM(v_cache.shape, BF16),
            pltpu.VMEM((pairs, 32, ROWS), F32),
            pltpu.VMEM((pairs, 32, CHUNK * PAGE), F32),
            pltpu.VMEM((pairs, 32, HD), F32),
            pltpu.VMEM((pairs, 32, HD), F32),
            pltpu.VMEM((pairs, 32, HD), F32),
            pltpu.VMEM((ROWS, QCOLS), F32),
            column,
            column,
            column,
            pltpu.VMEM((2 * SLOTS // CHUNK, 16, CHUNK * PAGE), F32),
            longs,
            longs,
            longs,
            dma(()),
        ],
        10,
    )(table, q_pack, k_new, v_new, q_all, k_cache, *in_hbm(v_cache))

    parts = lax.all_to_all(part, "seq", 0, 0, tiled=True)

    halves = (sds((TEN // 2, ROWS, COLS), BF16), sds((TEN // 2, ROWS, COLS), BF16))
    keep, send = call(
        out_kernel,
        halves,
        [VMEM] * 4,
        [pltpu.VMEM((ROWS, QCOLS), F32), pltpu.VMEM((SEQ, HD), F32), pltpu.VMEM((SEQ, HD), F32)],
        2,
    )(att, part0, parts, w_out)
    half = sds((TEN // 2, ROWS, COLS), BF16)
    own = call(core_sum_kernel, half, [VMEM] * 2, [], 1)(keep, swap_core(send))
    mine = call(
        residual_kernel, half, [VMEM] * 5, [pltpu.VMEM((ROWS, COLS), F32)], 1
    )(tokens, own, along_x(own, 1), along_x(own, 2), along_x(own, 3))
    other = swap_core(mine)

    keep, send = call(mlp_kernel, halves, [VMEM] * 6, [], 4)(mine, other, mlp_gain.reshape(1, D), w_gate, w_up, w_down)
    own, r1, r2, r3 = scatter_sum(keep, send)

    return call(final_kernel, sds((REQ_DEV, NEW, COLS), BF16), [VMEM] * 5, [], 1)(mine, own, r1, r2, r3)


def solution(mesh):
    placed = (
        P("seq", None, None),
        P(),
        P("seq"),
        P("seq"),
        P("seq", "tensor", None, None),
        P("seq", "tensor", None, None),
        P(),
        P(None, "tensor"),
        P(None, "tensor"),
        P(None, "tensor"),
        P("tensor", None),
        P(),
        P(None, "tensor"),
        P(None, "tensor"),
        P("tensor", None),
    )

    return jax.shard_map(per_device, mesh=mesh, in_specs=placed, out_specs=P("seq", None, "tensor"), check_vma=False)
```

```python
import math

import jax
import jax.numpy as jnp
import numpy as np
from jax import lax
from jax.experimental import pallas as pl
from jax.experimental.pallas import tpu as pltpu
from jax.sharding import PartitionSpec as P


EPSILON = 1e-05
NEGATIVE = -1e30
ROPE_BASE = 500000.0
F32 = jnp.float32
BF16 = jnp.bfloat16

SEQ = 16
TEN = 8
D = 3072
HD = 128
PAGE = 128
REQ_DEV = 16
NEW = 4
G = 3
ROWS = REQ_DEV * NEW
QCOLS = G * HD
COLS = D // TEN
FF_DEV = 512
SLOTS = 128
LONG_STEP = 32
LONGS = 8
SHORT_BLK = 4
SCALE = 1.0 / math.sqrt(HD)
CHUNK = 8


VMEM = pl.BlockSpec(memory_space=pltpu.VMEM)
SMEM = pl.BlockSpec(memory_space=pltpu.SMEM)
HBM = pl.BlockSpec(memory_space=pltpu.HBM)
MIB = 1 << 20


def call(kernel, out_shape, in_specs, scratch, limit, out_specs=None):
    return pl.pallas_call(
        kernel,
        out_shape=out_shape,
        in_specs=in_specs,
        out_specs=out_specs or jax.tree.map(lambda _: VMEM, out_shape),
        scratch_shapes=scratch,
        compiler_params=pltpu.CompilerParams(vmem_limit_bytes=limit * MIB),
    )


def sds(shape, dtype):
    return jax.ShapeDtypeStruct(shape, dtype)


def nt_dot(a, b):
    return lax.dot_general(a, b, (((1,), (1,)), ((), ())), preferred_element_type=F32)


def nn_dot(a, b):
    return jnp.dot(a, b, preferred_element_type=F32)


def iota(shape, dim):
    return lax.broadcasted_iota(jnp.int32, shape, dim)


def start_all(pairs, sems):
    copies = [pltpu.make_async_copy(src, dst, sems.at[i]) for i, (src, dst) in enumerate(pairs)]
    for copy in copies:
        copy.start(priority=1)
    return copies


def qkv_kernel(
    lengths_h, request_h, block_h, tok_h, gain_h, inv_h, wq_h, wk_h, wv_h,
    q_pack, k_new, v_new, q_long, table,
    lengths, request, block, tok, gain, inv, wq, wk, wv, x_s, pos_s, t_s, table_s, sems, table_sem,
):
    third = D // 3
    copies = start_all(
        [(tok_h, tok), (gain_h, gain), (lengths_h, lengths), (inv_h, inv)]
        + [(wq_h.at[pl.ds(i * third, third)], wq.at[pl.ds(i * third, third)]) for i in range(3)]
        + [(wk_h, wk), (wv_h, wv), (request_h, request.at[0]), (block_h, block.at[0])],
        sems,
    )
    home = lax.axis_index("seq") * REQ_DEV
    copies[9].wait()
    copies[10].wait()
    copies[2].wait()
    req = jnp.broadcast_to(request[...], (8, SLOTS))
    blk = jnp.broadcast_to(block[...], (8, SLOTS))
    lane = iota((8, SLOTS), 1)
    long_len = jnp.zeros((8, SLOTS), jnp.int32)
    for k in range(LONGS):
        long_len = jnp.where(req == k * LONG_STEP, lengths[k * LONG_STEP], long_len)
    limit = long_len - blk * PAGE
    key = jnp.where(limit > 0, req // LONG_STEP, LONGS)
    start = jnp.zeros((8, SLOTS), F32)
    first = jnp.zeros((8, SLOTS), F32)
    for k in range(LONGS):
        held = jnp.sum(jnp.where(key == k, 1.0, 0.0), axis=1, keepdims=True)
        first = jnp.where(key == k, start, first)
        start = start + jnp.floor((held + (CHUNK - 1)) * (1.0 / CHUNK)) * CHUNK
    packed = lane + key * 128 + jnp.minimum(limit, PAGE) * 1024
    mine = (req >= home) & (req < home + REQ_DEV) & (blk < SHORT_BLK)
    index = jnp.where(mine, (req - home) * SHORT_BLK + blk, -1)
    slot = iota((SLOTS, SLOTS), 0)
    spot = iota((SLOTS, SLOTS), 1)

    def column(row):
        wide = jnp.broadcast_to(row[0:1, :].astype(F32), (SLOTS, SLOTS))
        return jnp.sum(jnp.where(slot == spot, wide, 0.0), axis=1, keepdims=True)

    def scatter(at, value):
        return jnp.sum(jnp.where(at == spot.astype(F32), value, 0.0), axis=0, keepdims=True).astype(jnp.int32)

    table_s[0:1, :] = scatter(column(index), slot.astype(F32))
    keys = key[0:1, :].astype(F32)
    ahead = jnp.sum(jnp.where((column(key) == keys) & (slot < spot), 1.0, 0.0), axis=0, keepdims=True)
    at = column(jnp.where(keys < LONGS, first[0:1, :] + ahead, -1.0))
    words = column(packed)
    table_s[1:2, :] = scatter(at, words)
    table_s[2:3, :] = scatter(at - SLOTS, words)
    facts = jnp.where(lane == 0, (start * (1.0 / CHUNK)).astype(jnp.int32), 0)
    for r in range(REQ_DEV):
        known = jnp.where((home + r) % LONG_STEP == 0, 0, lengths[home + r])
        facts = jnp.where(lane == 16 + r, known, facts)
    table_s[3:4, :] = facts[0:1, :]
    table_s[4:8, :] = jnp.zeros((4, SLOTS), jnp.int32)
    give = pltpu.make_async_copy(table_s, table, table_sem)
    give.start()
    copies[0].wait()
    for r in range(REQ_DEV):
        x_s[r * NEW : (r + 1) * NEW, :] = tok[r].astype(F32)
    x = x_s[...]
    mean_square = jnp.mean(x * x, axis=-1, keepdims=True)
    copies[1].wait()
    normed = (x * lax.rsqrt(mean_square + EPSILON) * gain[...].astype(F32).reshape(1, D)).astype(BF16)
    for r in range(REQ_DEV):
        pos_s[r * NEW : (r + 1) * NEW, :] = lengths[home + r] + iota((NEW, HD), 0)
    copies[3].wait()
    angle = pos_s[...].astype(F32) * inv[...]
    cosine = jnp.cos(angle)
    sine = jnp.sin(angle)
    sine = jnp.where(iota((ROWS, HD), 1) < HD // 2, -sine, sine)

    def rope(v):
        return v * cosine + pltpu.roll(v, HD // 2, 1) * sine

    q = jnp.zeros((ROWS, QCOLS), F32)
    for i in range(3):
        copies[4 + i].wait()
        q = q + nn_dot(normed[:, i * third : (i + 1) * third], wq[i * third : (i + 1) * third, :])
    for g in range(G):
        roped = rope(q[:, g * HD : (g + 1) * HD])
        for pair in range(REQ_DEV // 2):
            q_pack[pair * 32 + g * 8 : pair * 32 + g * 8 + 8, :] = roped[pair * 8 : pair * 8 + 8, :]
        t_s[g * NEW : (g + 1) * NEW, :] = roped[0:NEW, :]
    t_s[G * NEW : 16, :] = jnp.zeros((16 - G * NEW, HD), F32)
    for pair in range(REQ_DEV // 2):
        q_pack[pair * 32 + 24 : pair * 32 + 32, :] = jnp.zeros((8, HD), F32)
    packed = t_s[...].astype(BF16)
    for i in range(SEQ):
        q_long[i] = packed
    copies[7].wait()
    k_new[...] = rope(nn_dot(normed, wk[...])).astype(BF16)
    copies[8].wait()
    v_new[...] = nn_dot(normed, wv[...]).astype(BF16)
    give.wait()


def to_row(column, eye):
    return jnp.sum(jnp.where(eye, column, 0.0), axis=0, keepdims=True)


def attend_kernel(
    table, q_pack, k_new, v_new, q_all, k_c, v_h,
    att, part0, part,
    v_c, fresh_s, short_s, top_s, acc_s, sum_s, att_s, o_0, m_0, l_0, long_s, m_s, l_s, o_s, sem,
):
    copy = pltpu.make_async_copy(v_h, v_c, sem)
    copy.start(priority=1)
    row = iota((32, ROWS), 0)
    col = iota((32, ROWS), 1)
    lane = iota((32, PAGE), 1)
    half = iota((32, PAGE), 0) % 8 // NEW

    def pair_score(pair, carry):
        q = q_pack[pl.ds(pl.multiple_of(pair * 32, 32), 32), :].astype(BF16)
        fresh = nt_dot(q, k_new[...]) * SCALE
        fresh_ok = (pair * 2 + row % 8 // NEW == col // NEW) & (col % NEW <= row % NEW)
        fresh = jnp.where(fresh_ok, fresh, NEGATIVE)
        fresh_s[pair] = fresh
        pages = [k_c[table[0, pair * CHUNK + i]] for i in range(CHUNK)]
        s = nt_dot(q, jnp.concatenate(pages, axis=0)) * SCALE
        own = jnp.where(half == 0, table[3, 16 + pair * 2], table[3, 17 + pair * 2])
        tops = []
        for i in range(CHUNK):
            inside = (half == i // SHORT_BLK) & (lane < own - i % SHORT_BLK * PAGE)
            part_s = jnp.where(inside, s[:, i * PAGE : (i + 1) * PAGE], NEGATIVE)
            short_s[pair, :, i * PAGE : (i + 1) * PAGE] = part_s
            tops.append(part_s)
        while len(tops) > 1:
            tops = [jnp.maximum(x, y) for x, y in zip(tops[::2], tops[1::2])]
        m = jnp.maximum(jnp.max(tops[0], axis=1, keepdims=True), jnp.max(fresh, axis=1, keepdims=True))
        top_s[pair] = jnp.broadcast_to(m, (32, HD))
        return carry

    lax.fori_loop(0, REQ_DEV // 2, pair_score, 0, unroll=2)

    trips = (table[3, 0] + 1) // 2
    m_s[...] = jnp.full((LONGS, 16, HD), NEGATIVE, F32)
    l_s[...] = jnp.zeros((LONGS, 16, HD), F32)
    o_s[...] = jnp.zeros((LONGS, 16, HD), F32)
    key_lane = iota((16, PAGE), 1)

    def entries(chunk):
        words = [table[1 + chunk // (SLOTS // CHUNK), chunk % (SLOTS // CHUNK) * CHUNK + i] for i in range(CHUNK)]
        return words, (words[0] >> 7) & 7

    def long_score(j, carry):
        got = []
        for chunk in (2 * j, 2 * j + 1):
            words, key = entries(chunk)
            pages = [k_c[word & 127] for word in words]
            s = nt_dot(q_all[2 * key], jnp.concatenate(pages, axis=0)) * SCALE
            tops = []
            for i, word in enumerate(words):
                part_s = jnp.where(key_lane < (word >> 10), s[:, i * PAGE : (i + 1) * PAGE], NEGATIVE)
                long_s[chunk, :, i * PAGE : (i + 1) * PAGE] = part_s
                tops.append(part_s)
            while len(tops) > 1:
                tops = [jnp.maximum(x, y) for x, y in zip(tops[::2], tops[1::2])]
            got.append((key, tops[0]))
        for key, top in got:
            m_s[key] = jnp.maximum(m_s[key], top)
        return carry

    lax.fori_loop(0, trips, long_score, 0)
    for k in range(LONGS):
        m_s[k] = jnp.broadcast_to(jnp.maximum(jnp.max(m_s[k], axis=1, keepdims=True), 0.1 * NEGATIVE), (16, HD))
    copy.wait()

    def pair_sum(pair, carry):
        m = top_s[pair]
        w = jnp.exp(fresh_s[pair] - m[:, 0:ROWS]).astype(BF16)
        total = jnp.sum(w.astype(F32), axis=1, keepdims=True)
        acc = nn_dot(w, v_new[...])
        ws = [jnp.exp(short_s[pair, :, i * PAGE : (i + 1) * PAGE] - m).astype(BF16) for i in range(CHUNK)]
        pages = [v_c[table[0, pair * CHUNK + i]] for i in range(CHUNK)]
        acc = acc + nn_dot(jnp.concatenate(ws, axis=1), jnp.concatenate(pages, axis=0))
        total = total + jnp.sum(sum(w.astype(F32) for w in ws), axis=1, keepdims=True)
        acc_s[pair] = acc
        sum_s[pair] = jnp.broadcast_to(total, (32, HD))
        out = acc / total
        at = pl.multiple_of(pair * 8, 8)
        for g in range(G):
            att_s[pl.ds(at, 8), g * HD : (g + 1) * HD] = out[g * 8 : (g + 1) * 8, :]
        return carry

    lax.fori_loop(0, REQ_DEV // 2, pair_sum, 0, unroll=2)
    att[...] = att_s[...]
    for g in range(G):
        o_0[g * NEW : (g + 1) * NEW, :] = acc_s[0, g * 8 : g * 8 + NEW, :]
        m_0[g * NEW : (g + 1) * NEW, :] = top_s[0, g * 8 : g * 8 + NEW, :]
        l_0[g * NEW : (g + 1) * NEW, :] = sum_s[0, g * 8 : g * 8 + NEW, :]
    eye = (iota((16, HD), 0) == iota((16, HD), 1)) & (iota((16, HD), 0) < G * NEW)
    part0[...] = o_0[...]
    part0[12:13, :] = to_row(m_0[...], eye)
    part0[13:14, :] = to_row(l_0[...], eye)
    part0[14:16, :] = jnp.zeros((2, HD), F32)

    def long_sum(j, carry):
        got = []
        for chunk in (2 * j, 2 * j + 1):
            words, key = entries(chunk)
            m = m_s[key]
            ws = [jnp.exp(long_s[chunk, :, i * PAGE : (i + 1) * PAGE] - m).astype(BF16) for i in range(CHUNK)]
            pages = [v_c[word & 127] for word in words]
            o = nn_dot(jnp.concatenate(ws, axis=1), jnp.concatenate(pages, axis=0))
            got.append((key, sum(w.astype(F32) for w in ws), o))
        for key, w, o in got:
            l_s[key] = l_s[key] + w
            o_s[key] = o_s[key] + o
        return carry

    lax.fori_loop(0, trips, long_sum, 0)
    for k in range(LONGS):
        total = jnp.broadcast_to(jnp.sum(l_s[k], axis=1, keepdims=True), (16, HD))
        part[2 * k, 0:12, :] = o_s[k, 0:12, :].astype(BF16)
        part[2 * k, 12:14, :] = jnp.concatenate([spread(m_s[k]), spread(total)], axis=0).astype(BF16)
        part[2 * k, 14:16, :] = jnp.zeros((2, HD), BF16)
        part[2 * k + 1] = jnp.zeros((16, HD), BF16)


def spread(column):
    row = iota((16, HD), 0)
    lane = iota((16, HD), 1)
    out = jnp.zeros((16, HD), F32)
    rest = column
    for i in range(3):
        piece = lax.reduce_precision(rest, 8, 7)
        rest = rest - piece
        out = jnp.where((lane == row + 16 * i) & (row < G * NEW), piece, out)
    return jnp.sum(out, axis=0, keepdims=True)


def gathered(row):
    return row + pltpu.roll(row, HD - 16, 1) + pltpu.roll(row, HD - 32, 1)


def place():
    tensor = lax.axis_index("tensor")
    return tensor // 2, tensor % 2


def half_product(a, w, core, out):
    for x in range(TEN // 2):
        at = pl.multiple_of((2 * x + core) * COLS, COLS)
        out[x] = nn_dot(a, w[:, pl.ds(at, COLS)]).astype(BF16)


def keep_kernel(a, w, keep):
    half_product(a[...], w, place()[1], keep)


def out_kernel(att, part0, parts, w_out, full, send, att_s, m_s, l_s):
    att_s[...] = att[...]

    @pl.when(lax.axis_index("seq") % 2 == 0)
    def _():
        for s in range(SEQ):
            stats = parts[s].astype(F32)
            m_s[s : s + 1, :] = stats[12:13, :]
            l_s[s : s + 1, :] = stats[13:14, :]
        m0 = part0[12:13, :]
        m = gathered(m_s[...])
        top = jnp.maximum(jnp.max(m, axis=0, keepdims=True), m0)
        grow = jnp.exp(m - top)
        grow0 = jnp.exp(m0 - top)
        total = jnp.sum(grow * gathered(l_s[...]), axis=0, keepdims=True) + grow0 * part0[13:14, :]
        live = iota((1, HD), 1) < G * NEW
        inverse = jnp.where(live, 1.0 / jnp.where(live, total, 1.0), 0.0)
        eye = iota((16, HD), 0) == iota((16, HD), 1)

        def scaled(o, coef):
            column = jnp.sum(jnp.where(eye, coef, 0.0), axis=1, keepdims=True)
            return o * column

        out = scaled(part0[...], grow0 * inverse)
        coefs = grow * inverse
        for s in range(SEQ):
            out = out + scaled(parts[s].astype(F32), coefs[s : s + 1, :])
        for g in range(G):
            att_s[0:NEW, g * HD : (g + 1) * HD] = out[g * NEW : (g + 1) * NEW, :]

    full[...] = att_s[...].astype(BF16)
    half_product(full[...], w_out, 1 - place()[1], send)


def pair_kernel(keep, got, own, s1, s2, s3):
    x = place()[0]
    own[...] = keep[x].astype(F32) + got[x].astype(F32)
    for d, out in ((1, s1), (2, s2), (3, s3)):
        to = (x + d) % 4
        out[...] = (keep[to].astype(F32) + got[to].astype(F32)).astype(BF16)


def core_sum_kernel(keep, got, out):
    out[...] = (keep[...].astype(F32) + got[...].astype(F32)).astype(BF16)


def residual_kernel(tok, own, r1, r2, r3, res, x_s):
    core = place()[1]
    for x in range(TEN // 2):
        at = pl.multiple_of((2 * x + core) * COLS, COLS)
        for r in range(REQ_DEV):
            x_s[r * NEW : (r + 1) * NEW, :] = tok[r, :, pl.ds(at, COLS)].astype(F32)
        total = own[x].astype(F32) + r1[x].astype(F32) + r2[x].astype(F32) + r3[x].astype(F32)
        res[x] = (x_s[...] + total).astype(BF16)


def half_gate(blocks, core, gain_s, w_gate, w_up, gate, up, square):
    for x in range(TEN // 2):
        at = pl.multiple_of((2 * x + core) * COLS, COLS)
        v = blocks[x].astype(F32)
        square = square + jnp.sum(v * v, axis=1, keepdims=True)
        scaled = (v * gain_s[:, pl.ds(at, COLS)]).astype(BF16)
        gate = gate + nn_dot(scaled, w_gate[pl.ds(at, COLS), :])
        up = up + nn_dot(scaled, w_up[pl.ds(at, COLS), :])
    return gate, up, square


def near_kernel(mine, gain, w_gate, w_up, gate, up, square, gain_s):
    gain_s[...] = gain[...].astype(F32).reshape(1, D)
    zero = jnp.zeros((ROWS, FF_DEV), F32)
    g, u, q = half_gate(mine, place()[1], gain_s, w_gate, w_up, zero, zero, jnp.zeros((ROWS, 1), F32))
    gate[...] = g
    up[...] = u
    square[...] = jnp.broadcast_to(q, (ROWS, HD))


def far_kernel(other, gain, gate, up, square, w_gate, w_up, w_down, act, send, gain_s):
    core = place()[1]
    gain_s[...] = gain[...].astype(F32).reshape(1, D)
    g, u, q = half_gate(other, 1 - core, gain_s, w_gate, w_up, gate[...], up[...], square[:, 0:1])
    inverse = lax.rsqrt(q * (1.0 / D) + EPSILON)
    g = g * inverse
    act[...] = (g / (1.0 + jnp.exp(-g)) * (u * inverse)).astype(BF16)
    half_product(act[...], w_down, 1 - core, send)


def fetch_kernel(after, wg_h, wu_h, wd_h, wg, wu, wd, sems):
    for copy in start_all([(wg_h, wg), (wu_h, wu), (wd_h, wd)], sems):
        copy.wait()


def final_kernel(res, own, r1, r2, r3, out):
    total = own[...] + r1[...].astype(F32) + r2[...].astype(F32) + r3[...].astype(F32)
    total = (res[place()[0]].astype(F32) + total).astype(BF16)
    for r in range(REQ_DEV):
        out[r] = total[r * NEW : (r + 1) * NEW, :]


def swap_core(v):
    return lax.ppermute(v, "tensor", [(i, i ^ 1) for i in range(TEN)])


def along_x(v, d):
    return lax.ppermute(v, "tensor", [(i, (i + 2 * d) % TEN) for i in range(TEN)])


def scatter_sum(keep, send):
    got = swap_core(send)
    block = sds((ROWS, COLS), BF16)
    own, s1, s2, s3 = call(pair_kernel, (sds((ROWS, COLS), F32), block, block, block), [VMEM, VMEM], [], 1)(keep, got)
    return own, along_x(s1, 1), along_x(s2, 2), along_x(s3, 3)


def per_device(
    tokens,
    lengths,
    page_request,
    page_block,
    k_cache,
    v_cache,
    attn_gain,
    w_query,
    w_key,
    w_value,
    w_out,
    mlp_gain,
    w_gate,
    w_up,
    w_down,
):
    half = np.arange(HD) % (HD // 2)
    inv = jnp.asarray((1.0 / ROPE_BASE ** (half * 2.0 / HD)).astype(np.float32).reshape(1, HD))
    k_cache = k_cache.reshape(SLOTS, PAGE, HD)
    v_cache = v_cache.reshape(SLOTS, PAGE, HD)
    dma = pltpu.SemaphoreType.DMA

    def in_hbm(*arrays):
        return tuple(pltpu.with_memory_space_constraint(a, pltpu.HBM) for a in arrays)

    q_pack, k_new, v_new, q_long, table = call(
        qkv_kernel,
        (
            sds((REQ_DEV // 2 * 32, HD), F32),
            sds((ROWS, HD), BF16),
            sds((ROWS, HD), BF16),
            sds((SEQ, 16, HD), BF16),
            pltpu.SMEM((8, SLOTS), jnp.int32),
        ),
        [HBM] * 9,
        [
            pltpu.SMEM(lengths.shape, jnp.int32),
            pltpu.VMEM((1, SLOTS), jnp.int32),
            pltpu.VMEM((1, SLOTS), jnp.int32),
            pltpu.VMEM(tokens.shape, BF16),
            pltpu.VMEM((D,), BF16),
            pltpu.VMEM((1, HD), F32),
            pltpu.VMEM(w_query.shape, BF16),
            pltpu.VMEM(w_key.shape, BF16),
            pltpu.VMEM(w_value.shape, BF16),
            pltpu.VMEM((ROWS, D), F32),
            pltpu.VMEM((ROWS, HD), jnp.int32),
            pltpu.VMEM((16, HD), F32),
            pltpu.VMEM((8, SLOTS), jnp.int32),
            dma((11,)),
            dma(()),
        ],
        8,
        [VMEM] * 4 + [SMEM],
    )(*in_hbm(lengths, page_request, page_block, tokens, attn_gain, inv, w_query, w_key, w_value))

    q_all = lax.all_to_all(q_long, "seq", 0, 0, tiled=True)

    column = pltpu.VMEM((16, HD), F32)
    longs = pltpu.VMEM((LONGS, 16, HD), F32)
    pairs = REQ_DEV // 2
    att, part0, part = call(
        attend_kernel,
        (sds((ROWS, QCOLS), F32), sds((16, HD), F32), sds((SEQ, 16, HD), BF16)),
        [SMEM] + [VMEM] * 5 + [HBM],
        [
            pltpu.VMEM(v_cache.shape, BF16),
            pltpu.VMEM((pairs, 32, ROWS), F32),
            pltpu.VMEM((pairs, 32, CHUNK * PAGE), F32),
            pltpu.VMEM((pairs, 32, HD), F32),
            pltpu.VMEM((pairs, 32, HD), F32),
            pltpu.VMEM((pairs, 32, HD), F32),
            pltpu.VMEM((ROWS, QCOLS), F32),
            column,
            column,
            column,
            pltpu.VMEM((2 * SLOTS // CHUNK, 16, CHUNK * PAGE), F32),
            longs,
            longs,
            longs,
            dma(()),
        ],
        10,
    )(table, q_pack, k_new, v_new, q_all, k_cache, *in_hbm(v_cache))

    parts = lax.all_to_all(part, "seq", 0, 0, tiled=True)

    half = sds((TEN // 2, ROWS, COLS), BF16)
    full, send = call(
        out_kernel,
        (sds((ROWS, QCOLS), BF16), half),
        [VMEM] * 4,
        [pltpu.VMEM((ROWS, QCOLS), F32), pltpu.VMEM((SEQ, HD), F32), pltpu.VMEM((SEQ, HD), F32)],
        2,
    )(att, part0, parts, w_out)
    got = swap_core(send)
    keep = call(keep_kernel, half, [VMEM] * 2, [], 1)(full, w_out)
    own = call(core_sum_kernel, half, [VMEM] * 2, [], 1)(keep, got)
    weights = (w_gate, w_up, w_down)
    weights = call(
        fetch_kernel, tuple(pltpu.VMEM(w.shape, BF16) for w in weights), [VMEM] + [HBM] * 3, [dma((3,))], 1
    )(own, *in_hbm(*weights))
    w_gate, w_up, w_down = (pltpu.with_memory_space_constraint(w, pltpu.VMEM) for w in weights)
    mine = call(
        residual_kernel, half, [VMEM] * 5, [pltpu.VMEM((ROWS, COLS), F32)], 1
    )(tokens, own, along_x(own, 1), along_x(own, 2), along_x(own, 3))
    other = swap_core(mine)

    wide = sds((ROWS, FF_DEV), F32)
    gain_s = pltpu.VMEM((1, D), F32)
    gate, up, square = call(
        near_kernel, (wide, wide, sds((ROWS, HD), F32)), [VMEM] * 4, [gain_s], 2
    )(mine, mlp_gain, w_gate, w_up)
    act, send = call(
        far_kernel, (sds((ROWS, FF_DEV), BF16), half), [VMEM] * 8, [gain_s], 3
    )(other, mlp_gain, gate, up, square, w_gate, w_up, w_down)
    keep = call(keep_kernel, half, [VMEM] * 2, [], 1)(act, w_down)
    own, r1, r2, r3 = scatter_sum(keep, send)

    return call(final_kernel, sds((REQ_DEV, NEW, COLS), BF16), [VMEM] * 5, [], 1)(mine, own, r1, r2, r3)


def solution(mesh):
    placed = (
        P("seq", None, None),
        P(),
        P("seq"),
        P("seq"),
        P("seq", "tensor", None, None),
        P("seq", "tensor", None, None),
        P(),
        P(None, "tensor"),
        P(None, "tensor"),
        P(None, "tensor"),
        P("tensor", None),
        P(),
        P(None, "tensor"),
        P(None, "tensor"),
        P("tensor", None),
    )

    return jax.shard_map(per_device, mesh=mesh, in_specs=placed, out_specs=P("seq", None, "tensor"), check_vma=False)
```

```python
import math

import jax
import jax.numpy as jnp
import numpy as np
from jax import lax
from jax.experimental import pallas as pl
from jax.experimental.pallas import tpu as pltpu
from jax.sharding import PartitionSpec as P


EPSILON = 1e-05
NEGATIVE = -1e30
ROPE_BASE = 500000.0
F32 = jnp.float32
BF16 = jnp.bfloat16

SEQ = 16
TEN = 8
D = 3072
HD = 128
PAGE = 128
REQ_DEV = 16
NEW = 4
G = 3
ROWS = REQ_DEV * NEW
QCOLS = G * HD
COLS = D // TEN
FF_DEV = 512
SLOTS = 128
LANES = 16
LONG_STEP = 32
LONGS = 8
SHORT_BLK = 4
SCALE = 1.0 / math.sqrt(HD)
CHUNK = 8


VMEM = pl.BlockSpec(memory_space=pltpu.VMEM)
SMEM = pl.BlockSpec(memory_space=pltpu.SMEM)
HBM = pl.BlockSpec(memory_space=pltpu.HBM)
MIB = 1 << 20


def call(kernel, out_shape, in_specs, scratch, limit, out_specs=None):
    return pl.pallas_call(
        kernel,
        out_shape=out_shape,
        in_specs=in_specs,
        out_specs=out_specs or jax.tree.map(lambda _: VMEM, out_shape),
        scratch_shapes=scratch,
        compiler_params=pltpu.CompilerParams(vmem_limit_bytes=limit * MIB),
    )


def sds(shape, dtype):
    return jax.ShapeDtypeStruct(shape, dtype)


def nt_dot(a, b):
    return lax.dot_general(a, b, (((1,), (1,)), ((), ())), preferred_element_type=F32)


def nn_dot(a, b):
    return jnp.dot(a, b, preferred_element_type=F32)


def iota(shape, dim):
    return lax.broadcasted_iota(jnp.int32, shape, dim)


def start_all(pairs, sems):
    copies = [pltpu.make_async_copy(src, dst, sems.at[i]) for i, (src, dst) in enumerate(pairs)]
    for copy in copies:
        copy.start(priority=1)
    return copies


def qkv_kernel(
    lengths_h, request_h, block_h, tok_h, gain_h, inv_h, wq_h, wk_h, wv_h,
    q_pack, k_new, v_new, q_long, table,
    lengths, request, block, tok, gain, inv, wq, wk, wv, x_s, pos_s, table_s, sems, table_sem,
):
    third = D // 3
    copies = start_all(
        [(tok_h, tok), (gain_h, gain), (lengths_h, lengths), (inv_h, inv)]
        + [(wq_h.at[pl.ds(i * third, third)], wq.at[pl.ds(i * third, third)]) for i in range(3)]
        + [(wk_h, wk), (wv_h, wv), (request_h, request.at[0]), (block_h, block.at[0])],
        sems,
    )
    home = lax.axis_index("seq") * REQ_DEV
    copies[9].wait()
    copies[10].wait()
    copies[2].wait()
    req = jnp.broadcast_to(request[...], (8, SLOTS))
    blk = jnp.broadcast_to(block[...], (8, SLOTS))
    lane = iota((8, SLOTS), 1)
    long_len = jnp.zeros((8, SLOTS), jnp.int32)
    for k in range(LONGS):
        long_len = jnp.where(req == k * LONG_STEP, lengths[k * LONG_STEP], long_len)
    limit = long_len - blk * PAGE
    key = jnp.where(limit > 0, req // LONG_STEP, LONGS)
    start = jnp.zeros((8, SLOTS), F32)
    first = jnp.zeros((8, SLOTS), F32)
    for k in range(LONGS):
        held = jnp.sum(jnp.where(key == k, 1.0, 0.0), axis=1, keepdims=True)
        first = jnp.where(key == k, start, first)
        start = start + jnp.floor((held + (CHUNK - 1)) * (1.0 / CHUNK)) * CHUNK
    packed = lane + key * 128 + jnp.minimum(limit, PAGE) * 1024
    mine = (req >= home) & (req < home + REQ_DEV) & (blk < SHORT_BLK)
    index = jnp.where(mine, (req - home) * SHORT_BLK + blk, -1)
    slot = iota((SLOTS, SLOTS), 0)
    spot = iota((SLOTS, SLOTS), 1)

    def column(row):
        wide = jnp.broadcast_to(row[0:1, :].astype(F32), (SLOTS, SLOTS))
        return jnp.sum(jnp.where(slot == spot, wide, 0.0), axis=1, keepdims=True)

    def scatter(at, value):
        return jnp.sum(jnp.where(at == spot.astype(F32), value, 0.0), axis=0, keepdims=True).astype(jnp.int32)

    table_s[0:1, :] = scatter(column(index), slot.astype(F32))
    keys = key[0:1, :].astype(F32)
    ahead = jnp.sum(jnp.where((column(key) == keys) & (slot < spot), 1.0, 0.0), axis=0, keepdims=True)
    at = column(jnp.where(keys < LONGS, first[0:1, :] + ahead, -1.0))
    words = column(packed)
    table_s[1:2, :] = scatter(at, words)
    table_s[2:3, :] = scatter(at - SLOTS, words)
    facts = jnp.where(lane == 0, (start * (1.0 / CHUNK)).astype(jnp.int32), 0)
    for r in range(REQ_DEV):
        known = jnp.where((home + r) % LONG_STEP == 0, 0, lengths[home + r])
        facts = jnp.where(lane == 16 + r, known, facts)
    table_s[3:4, :] = facts[0:1, :]
    table_s[4:8, :] = jnp.zeros((4, SLOTS), jnp.int32)
    give = pltpu.make_async_copy(table_s, table, table_sem)
    give.start()
    copies[0].wait()
    for r in range(REQ_DEV):
        x_s[r * NEW : (r + 1) * NEW, :] = tok[r].astype(F32)
    x = x_s[...]
    mean_square = jnp.mean(x * x, axis=-1, keepdims=True)
    copies[1].wait()
    normed = (x * lax.rsqrt(mean_square + EPSILON) * gain[...].astype(F32).reshape(1, D)).astype(BF16)
    for r in range(REQ_DEV):
        pos_s[r * NEW : (r + 1) * NEW, :] = lengths[home + r] + iota((NEW, HD), 0)
    copies[3].wait()
    angle = pos_s[...].astype(F32) * inv[...]
    cosine = jnp.cos(angle)
    sine = jnp.sin(angle)
    sine = jnp.where(iota((ROWS, HD), 1) < HD // 2, -sine, sine)

    def rope(v):
        return v * cosine + pltpu.roll(v, HD // 2, 1) * sine

    q = jnp.zeros((ROWS, QCOLS), F32)
    for i in range(3):
        copies[4 + i].wait()
        q = q + nn_dot(normed[:, i * third : (i + 1) * third], wq[i * third : (i + 1) * third, :])
    for g in range(G):
        roped = rope(q[:, g * HD : (g + 1) * HD])
        for r in range(REQ_DEV):
            at = r * LANES + g * NEW
            q_pack[at : at + NEW, :] = roped[r * NEW : (r + 1) * NEW, :]
    for r in range(REQ_DEV):
        q_pack[r * LANES + G * NEW : (r + 1) * LANES, :] = jnp.zeros((LANES - G * NEW, HD), F32)
    packed = q_pack[0:LANES, :].astype(BF16)
    for i in range(SEQ):
        q_long[i] = packed
    copies[7].wait()
    k_new[...] = rope(nn_dot(normed, wk[...])).astype(BF16)
    copies[8].wait()
    v_new[...] = nn_dot(normed, wv[...]).astype(BF16)
    give.wait()


def to_row(column, eye):
    return jnp.sum(jnp.where(eye, column, 0.0), axis=0, keepdims=True)


def attend_kernel(
    table, q_pack, k_new, v_new, q_all, k_c, v_h, wo_h,
    att, part0, part, wo,
    v_c, fresh_s, short_s, top_s, acc_s, sum_s, att_s, long_s, m_s, l_s, o_s, sems,
):
    copies = start_all([(v_h, v_c), (wo_h, wo)], sems)
    row = iota((LANES, ROWS), 0)
    col = iota((LANES, ROWS), 1)
    key_lane = iota((LANES, PAGE), 1)

    def request_score(r):
        q = q_pack[pl.ds(pl.multiple_of(r * LANES, LANES), LANES), :].astype(BF16)
        fresh = nt_dot(q, k_new[...]) * SCALE
        fresh = jnp.where((col // NEW == r) & (col % NEW <= row % NEW), fresh, NEGATIVE)
        fresh_s[r] = fresh
        pages = [k_c[table[0, r * SHORT_BLK + i]] for i in range(SHORT_BLK)]
        s = nt_dot(q, jnp.concatenate(pages, axis=0)) * SCALE
        used = table[3, 16 + r]
        tops = []
        for i in range(SHORT_BLK):
            part_s = jnp.where(key_lane < used - i * PAGE, s[:, i * PAGE : (i + 1) * PAGE], NEGATIVE)
            short_s[r, :, i * PAGE : (i + 1) * PAGE] = part_s
            tops.append(part_s)
        top = jnp.maximum(jnp.maximum(tops[0], tops[1]), jnp.maximum(tops[2], tops[3]))
        m = jnp.maximum(jnp.max(top, axis=1, keepdims=True), jnp.max(fresh, axis=1, keepdims=True))
        top_s[r] = jnp.broadcast_to(m, (LANES, HD))

    def pair_score(pair, carry):
        request_score(2 * pair)
        request_score(2 * pair + 1)
        return carry

    lax.fori_loop(0, REQ_DEV // 2, pair_score, 0, unroll=4)

    trips = (table[3, 0] + 3) // 4
    m_s[...] = jnp.full((LONGS, 16, HD), NEGATIVE, F32)
    l_s[...] = jnp.zeros((LONGS, 16, HD), F32)
    o_s[...] = jnp.zeros((LONGS, 16, HD), F32)

    def entries(chunk):
        words = [table[1 + chunk // (SLOTS // CHUNK), chunk % (SLOTS // CHUNK) * CHUNK + i] for i in range(CHUNK)]
        return words, (words[0] >> 7) & 7

    def long_score(j, carry):
        got = []
        for chunk in (4 * j, 4 * j + 1, 4 * j + 2, 4 * j + 3):
            words, key = entries(chunk)
            pages = [k_c[word & 127] for word in words]
            s = nt_dot(q_all[2 * key], jnp.concatenate(pages, axis=0)) * SCALE
            tops = []
            for i, word in enumerate(words):
                part_s = jnp.where(key_lane < (word >> 10), s[:, i * PAGE : (i + 1) * PAGE], NEGATIVE)
                long_s[chunk, :, i * PAGE : (i + 1) * PAGE] = part_s
                tops.append(part_s)
            while len(tops) > 1:
                tops = [jnp.maximum(x, y) for x, y in zip(tops[::2], tops[1::2])]
            got.append((key, tops[0]))
        for key, top in got:
            m_s[key] = jnp.maximum(m_s[key], top)
        return carry

    lax.fori_loop(0, trips, long_score, 0)
    for k in range(LONGS):
        m_s[k] = jnp.broadcast_to(jnp.maximum(jnp.max(m_s[k], axis=1, keepdims=True), 0.1 * NEGATIVE), (16, HD))
    copies[0].wait()

    def request_sum(r):
        m = top_s[r]
        w = jnp.exp(fresh_s[r] - m[:, 0:ROWS]).astype(BF16)
        total = jnp.sum(w.astype(F32), axis=1, keepdims=True)
        acc = nn_dot(w, v_new[...])
        ws = [jnp.exp(short_s[r, :, i * PAGE : (i + 1) * PAGE] - m).astype(BF16) for i in range(SHORT_BLK)]
        pages = [v_c[table[0, r * SHORT_BLK + i]] for i in range(SHORT_BLK)]
        acc = acc + nn_dot(jnp.concatenate(ws, axis=1), jnp.concatenate(pages, axis=0))
        total = total + jnp.sum(sum(w.astype(F32) for w in ws), axis=1, keepdims=True)
        acc_s[r] = acc
        sum_s[r] = jnp.broadcast_to(total, (LANES, HD))
        return acc / total

    def pair_sum(pair, carry):
        outs = request_sum(2 * pair), request_sum(2 * pair + 1)
        at = pl.multiple_of(pair * 8, 8)
        for g in range(G):
            rows = jnp.concatenate([out[g * NEW : (g + 1) * NEW, :] for out in outs], axis=0)
            att_s[pl.ds(at, 8), g * HD : (g + 1) * HD] = rows
        return carry

    lax.fori_loop(0, REQ_DEV // 2, pair_sum, 0, unroll=4)
    att[...] = att_s[...]
    eye = (iota((16, HD), 0) == iota((16, HD), 1)) & (iota((16, HD), 0) < G * NEW)
    part0[...] = acc_s[0]
    part0[12:13, :] = to_row(top_s[0], eye)
    part0[13:14, :] = to_row(sum_s[0], eye)
    part0[14:16, :] = jnp.zeros((2, HD), F32)

    def long_sum(j, carry):
        got = []
        for chunk in (4 * j, 4 * j + 1, 4 * j + 2, 4 * j + 3):
            words, key = entries(chunk)
            m = m_s[key]
            ws = [jnp.exp(long_s[chunk, :, i * PAGE : (i + 1) * PAGE] - m).astype(BF16) for i in range(CHUNK)]
            pages = [v_c[word & 127] for word in words]
            o = nn_dot(jnp.concatenate(ws, axis=1), jnp.concatenate(pages, axis=0))
            got.append((key, sum(w.astype(F32) for w in ws), o))
        for key, w, o in got:
            l_s[key] = l_s[key] + w
            o_s[key] = o_s[key] + o
        return carry

    lax.fori_loop(0, trips, long_sum, 0)
    for k in range(LONGS):
        total = jnp.broadcast_to(jnp.sum(l_s[k], axis=1, keepdims=True), (16, HD))
        part[2 * k, 0:12, :] = o_s[k, 0:12, :].astype(BF16)
        part[2 * k, 12:14, :] = jnp.concatenate([spread(m_s[k]), spread(total)], axis=0).astype(BF16)
        part[2 * k, 14:16, :] = jnp.zeros((2, HD), BF16)
        part[2 * k + 1] = jnp.zeros((16, HD), BF16)
    copies[1].wait()


def spread(column):
    row = iota((16, HD), 0)
    lane = iota((16, HD), 1)
    out = jnp.zeros((16, HD), F32)
    rest = column
    for i in range(3):
        piece = lax.reduce_precision(rest, 8, 7)
        rest = rest - piece
        out = jnp.where((lane == row + 16 * i) & (row < G * NEW), piece, out)
    return jnp.sum(out, axis=0, keepdims=True)


def gathered(row):
    return row + pltpu.roll(row, HD - 16, 1) + pltpu.roll(row, HD - 32, 1)


def place():
    tensor = lax.axis_index("tensor")
    return tensor // 2, tensor % 2


def half_product(a, w, core, out):
    for x in range(TEN // 2):
        at = pl.multiple_of((2 * x + core) * COLS, COLS)
        out[x] = nn_dot(a, w[:, pl.ds(at, COLS)]).astype(BF16)


def keep_kernel(a, w, keep):
    half_product(a[...], w, place()[1], keep)


def out_kernel(att, part0, parts, w_out, full, send, att_s, m_s, l_s):
    att_s[...] = att[...]

    @pl.when(lax.axis_index("seq") % 2 == 0)
    def _():
        for s in range(SEQ):
            stats = parts[s].astype(F32)
            m_s[s : s + 1, :] = stats[12:13, :]
            l_s[s : s + 1, :] = stats[13:14, :]
        m0 = part0[12:13, :]
        m = gathered(m_s[...])
        top = jnp.maximum(jnp.max(m, axis=0, keepdims=True), m0)
        grow = jnp.exp(m - top)
        grow0 = jnp.exp(m0 - top)
        total = jnp.sum(grow * gathered(l_s[...]), axis=0, keepdims=True) + grow0 * part0[13:14, :]
        live = iota((1, HD), 1) < G * NEW
        inverse = jnp.where(live, 1.0 / jnp.where(live, total, 1.0), 0.0)
        eye = iota((16, HD), 0) == iota((16, HD), 1)

        def scaled(o, coef):
            column = jnp.sum(jnp.where(eye, coef, 0.0), axis=1, keepdims=True)
            return o * column

        out = scaled(part0[...], grow0 * inverse)
        coefs = grow * inverse
        for s in range(SEQ):
            out = out + scaled(parts[s].astype(F32), coefs[s : s + 1, :])
        for g in range(G):
            att_s[0:NEW, g * HD : (g + 1) * HD] = out[g * NEW : (g + 1) * NEW, :]

    full[...] = att_s[...].astype(BF16)
    half_product(full[...], w_out, 1 - place()[1], send)


def pair_kernel(keep, got, own, s1, s2, s3):
    x = place()[0]
    own[...] = keep[x].astype(F32) + got[x].astype(F32)
    for d, out in ((1, s1), (2, s2), (3, s3)):
        to = (x + d) % 4
        out[...] = (keep[to].astype(F32) + got[to].astype(F32)).astype(BF16)


def core_sum_kernel(keep, got, out):
    out[...] = (keep[...].astype(F32) + got[...].astype(F32)).astype(BF16)


def residual_kernel(tok, own, r1, r2, r3, res, x_s):
    core = place()[1]
    for x in range(TEN // 2):
        at = pl.multiple_of((2 * x + core) * COLS, COLS)
        for r in range(REQ_DEV):
            x_s[r * NEW : (r + 1) * NEW, :] = tok[r, :, pl.ds(at, COLS)].astype(F32)
        total = own[x].astype(F32) + r1[x].astype(F32) + r2[x].astype(F32) + r3[x].astype(F32)
        res[x] = (x_s[...] + total).astype(BF16)


def half_gate(blocks, core, gain_s, w_gate, w_up, gate, up, square):
    for x in range(TEN // 2):
        at = pl.multiple_of((2 * x + core) * COLS, COLS)
        v = blocks[x].astype(F32)
        square = square + jnp.sum(v * v, axis=1, keepdims=True)
        scaled = (v * gain_s[:, pl.ds(at, COLS)]).astype(BF16)
        gate = gate + nn_dot(scaled, w_gate[pl.ds(at, COLS), :])
        up = up + nn_dot(scaled, w_up[pl.ds(at, COLS), :])
    return gate, up, square


def near_kernel(mine, gain, w_gate, w_up, gate, up, square, gain_s):
    gain_s[...] = gain[...].astype(F32).reshape(1, D)
    zero = jnp.zeros((ROWS, FF_DEV), F32)
    g, u, q = half_gate(mine, place()[1], gain_s, w_gate, w_up, zero, zero, jnp.zeros((ROWS, 1), F32))
    gate[...] = g
    up[...] = u
    square[...] = jnp.broadcast_to(q, (ROWS, HD))


def far_kernel(other, gain, gate, up, square, w_gate, w_up, w_down, act, send, gain_s):
    core = place()[1]
    gain_s[...] = gain[...].astype(F32).reshape(1, D)
    g, u, q = half_gate(other, 1 - core, gain_s, w_gate, w_up, gate[...], up[...], square[:, 0:1])
    inverse = lax.rsqrt(q * (1.0 / D) + EPSILON)
    g = g * inverse
    act[...] = (g / (1.0 + jnp.exp(-g)) * (u * inverse)).astype(BF16)
    half_product(act[...], w_down, 1 - core, send)


def fetch_kernel(after, wg_h, wu_h, wd_h, wg, wu, wd, sems):
    for copy in start_all([(wg_h, wg), (wu_h, wu), (wd_h, wd)], sems):
        copy.wait()


def final_kernel(res, own, r1, r2, r3, out):
    total = own[...] + r1[...].astype(F32) + r2[...].astype(F32) + r3[...].astype(F32)
    total = (res[place()[0]].astype(F32) + total).astype(BF16)
    for r in range(REQ_DEV):
        out[r] = total[r * NEW : (r + 1) * NEW, :]


def swap_core(v):
    return lax.ppermute(v, "tensor", [(i, i ^ 1) for i in range(TEN)])


def along_x(v, d):
    return lax.ppermute(v, "tensor", [(i, (i + 2 * d) % TEN) for i in range(TEN)])


def scatter_sum(keep, send):
    got = swap_core(send)
    block = sds((ROWS, COLS), BF16)
    own, s1, s2, s3 = call(pair_kernel, (sds((ROWS, COLS), F32), block, block, block), [VMEM, VMEM], [], 1)(keep, got)
    return own, along_x(s1, 1), along_x(s2, 2), along_x(s3, 3)


def per_device(
    tokens,
    lengths,
    page_request,
    page_block,
    k_cache,
    v_cache,
    attn_gain,
    w_query,
    w_key,
    w_value,
    w_out,
    mlp_gain,
    w_gate,
    w_up,
    w_down,
):
    half = np.arange(HD) % (HD // 2)
    inv = jnp.asarray((1.0 / ROPE_BASE ** (half * 2.0 / HD)).astype(np.float32).reshape(1, HD))
    k_cache = k_cache.reshape(SLOTS, PAGE, HD)
    v_cache = v_cache.reshape(SLOTS, PAGE, HD)
    dma = pltpu.SemaphoreType.DMA

    def in_hbm(*arrays):
        return tuple(pltpu.with_memory_space_constraint(a, pltpu.HBM) for a in arrays)

    q_pack, k_new, v_new, q_long, table = call(
        qkv_kernel,
        (
            sds((REQ_DEV * LANES, HD), F32),
            sds((ROWS, HD), BF16),
            sds((ROWS, HD), BF16),
            sds((SEQ, 16, HD), BF16),
            pltpu.SMEM((8, SLOTS), jnp.int32),
        ),
        [HBM] * 9,
        [
            pltpu.SMEM(lengths.shape, jnp.int32),
            pltpu.VMEM((1, SLOTS), jnp.int32),
            pltpu.VMEM((1, SLOTS), jnp.int32),
            pltpu.VMEM(tokens.shape, BF16),
            pltpu.VMEM((D,), BF16),
            pltpu.VMEM((1, HD), F32),
            pltpu.VMEM(w_query.shape, BF16),
            pltpu.VMEM(w_key.shape, BF16),
            pltpu.VMEM(w_value.shape, BF16),
            pltpu.VMEM((ROWS, D), F32),
            pltpu.VMEM((ROWS, HD), jnp.int32),
            pltpu.VMEM((8, SLOTS), jnp.int32),
            dma((11,)),
            dma(()),
        ],
        8,
        [VMEM] * 4 + [SMEM],
    )(*in_hbm(lengths, page_request, page_block, tokens, attn_gain, inv, w_query, w_key, w_value))

    q_all = lax.all_to_all(q_long, "seq", 0, 0, tiled=True)

    longs = pltpu.VMEM((LONGS, LANES, HD), F32)
    each = pltpu.VMEM((REQ_DEV, LANES, HD), F32)
    att, part0, part, w_out = call(
        attend_kernel,
        (
            sds((ROWS, QCOLS), F32),
            sds((LANES, HD), F32),
            sds((SEQ, LANES, HD), BF16),
            pltpu.VMEM(w_out.shape, BF16),
        ),
        [SMEM] + [VMEM] * 5 + [HBM] * 2,
        [
            pltpu.VMEM(v_cache.shape, BF16),
            pltpu.VMEM((REQ_DEV, LANES, ROWS), F32),
            pltpu.VMEM((REQ_DEV, LANES, SHORT_BLK * PAGE), F32),
            each,
            each,
            each,
            pltpu.VMEM((ROWS, QCOLS), F32),
            pltpu.VMEM((2 * SLOTS // CHUNK, LANES, CHUNK * PAGE), F32),
            longs,
            longs,
            longs,
            dma((2,)),
        ],
        10,
    )(table, q_pack, k_new, v_new, q_all, k_cache, *in_hbm(v_cache, w_out))
    w_out = pltpu.with_memory_space_constraint(w_out, pltpu.VMEM)

    parts = lax.all_to_all(part, "seq", 0, 0, tiled=True)

    half = sds((TEN // 2, ROWS, COLS), BF16)
    full, send = call(
        out_kernel,
        (sds((ROWS, QCOLS), BF16), half),
        [VMEM] * 4,
        [pltpu.VMEM((ROWS, QCOLS), F32), pltpu.VMEM((SEQ, HD), F32), pltpu.VMEM((SEQ, HD), F32)],
        2,
    )(att, part0, parts, w_out)
    got = swap_core(send)
    keep = call(keep_kernel, half, [VMEM] * 2, [], 1)(full, w_out)
    own = call(core_sum_kernel, half, [VMEM] * 2, [], 1)(keep, got)
    weights = (w_gate, w_up, w_down)
    weights = call(
        fetch_kernel, tuple(pltpu.VMEM(w.shape, BF16) for w in weights), [VMEM] + [HBM] * 3, [dma((3,))], 1
    )(own, *in_hbm(*weights))
    w_gate, w_up, w_down = (pltpu.with_memory_space_constraint(w, pltpu.VMEM) for w in weights)
    mine = call(
        residual_kernel, half, [VMEM] * 5, [pltpu.VMEM((ROWS, COLS), F32)], 1
    )(tokens, own, along_x(own, 1), along_x(own, 2), along_x(own, 3))
    other = swap_core(mine)

    wide = sds((ROWS, FF_DEV), F32)
    gain_s = pltpu.VMEM((1, D), F32)
    gate, up, square = call(
        near_kernel, (wide, wide, sds((ROWS, HD), F32)), [VMEM] * 4, [gain_s], 2
    )(mine, mlp_gain, w_gate, w_up)
    act, send = call(
        far_kernel, (sds((ROWS, FF_DEV), BF16), half), [VMEM] * 8, [gain_s], 3
    )(other, mlp_gain, gate, up, square, w_gate, w_up, w_down)
    keep = call(keep_kernel, half, [VMEM] * 2, [], 1)(act, w_down)
    own, r1, r2, r3 = scatter_sum(keep, send)

    return call(final_kernel, sds((REQ_DEV, NEW, COLS), BF16), [VMEM] * 5, [], 1)(mine, own, r1, r2, r3)


def solution(mesh):
    placed = (
        P("seq", None, None),
        P(),
        P("seq"),
        P("seq"),
        P("seq", "tensor", None, None),
        P("seq", "tensor", None, None),
        P(),
        P(None, "tensor"),
        P(None, "tensor"),
        P(None, "tensor"),
        P("tensor", None),
        P(),
        P(None, "tensor"),
        P(None, "tensor"),
        P("tensor", None),
    )

    return jax.shard_map(per_device, mesh=mesh, in_specs=placed, out_specs=P("seq", None, "tensor"), check_vma=False)
```
